32 devices in a mesh: seq: 8 (over z, x), batch: 4 (over y, core).
Axes of the slice: x: 2, y: 2, z: 4, core: 2. Of those that a mesh axis runs over, the one named last changes fastest.
Arguments:
- tokens: bfloat16 [4, 2048, 2048], P('batch', 'seq'), may hold values from -6 to 6
- lengths: int32 [4, 1], replicated, may hold values from 512 to 2048, as said below
- cotangent: bfloat16 [4, 2048, 2048], P('batch', 'seq'), may hold values from -6 to 6
- ln1_gain: bfloat16 [2048], P(('seq', 'batch')), may hold values from 0.5 to 1.5
- ln1_bias: bfloat16 [2048], P(('seq', 'batch')), may hold values from -1.5 to 1.5
- w_qkv: bfloat16 [2048, 3, 2048], P('seq', None, 'batch'), may hold values from -0.1875 to 0.1875
- qv_bias: bfloat16 [2, 2048], P(None, 'batch'), may hold values from -1.5 to 1.5
- w_out: bfloat16 [2048, 2048], P('batch', 'seq'), may hold values from -0.375 to 0.375
- out_bias: bfloat16 [2048], P(('seq', 'batch')), may hold values from -1.5 to 1.5
- ln2_gain: bfloat16 [2048], P(('seq', 'batch')), may hold values from 0.5 to 1.5
- ln2_bias: bfloat16 [2048], P(('seq', 'batch')), may hold values from -1.5 to 1.5
- w_fc: bfloat16 [2048, 8192], P('seq', 'batch'), may hold values from -0.125 to 0.125
- fc_bias: bfloat16 [8192], P('batch'), may hold values from -1.5 to 1.5
- w_proj: bfloat16 [8192, 2048], P('batch', 'seq'), may hold values from -0.0625 to 0.0625
- proj_bias: bfloat16 [2048], P(('seq', 'batch')), may hold values from -1.5 to 1.5
Outputs:
- block_out: bfloat16 [4, 2048, 2048], P('batch', 'seq')
- grad_tokens: bfloat16 [4, 2048, 2048], P('batch', 'seq')
- grad_ln1_gain: float32 [2048], P(('seq', 'batch'))
- grad_ln1_bias: float32 [2048], P(('seq', 'batch'))
- grad_w_qkv: float32 [2048, 3, 2048], P('seq', None, 'batch')
- grad_qv_bias: float32 [2, 2048], P(None, 'batch')
- grad_w_out: float32 [2048, 2048], P('batch', 'seq')
- grad_out_bias: float32 [2048], P(('seq', 'batch'))
- grad_ln2_gain: float32 [2048], P(('seq', 'batch'))
- grad_ln2_bias: float32 [2048], P(('seq', 'batch'))
- grad_w_fc: float32 [2048, 8192], P('seq', 'batch')
- grad_fc_bias: float32 [8192], P('batch')
- grad_w_proj: float32 [8192, 2048], P('batch', 'seq')
- grad_proj_bias: float32 [2048], P(('seq', 'batch'))
The draws below stay inside these ranges and needn't reach their ends.
Inputs may be any that keep to these rules, and one draw needn't show every extreme that they name: `lengths`: some sequence has all 2048 slots true and some other has exactly 512.
All inputs are finite; a program needn't handle non-finite values.
Results may differ from the reference program's by a relative error of at most 0.018.
Values may be sent and summed in bfloat16 or wider, within the bound.
No kernel may reach another device: no remote copies, remote signals or barrier semaphores. Data moves between devices by JAX's collectives and lax.ppermute only.
A program may use at most 448 MiB of HBM per device.

```python
import math
import jax
import jax.numpy as jnp
from jax import lax

D = 2048
HEADS = 16
HEAD_DIM = 128
FF = 8192
WINDOW = 256
LENGTH = 2048
CHAINS = 4
CHAIN_TOKENS = 2048
SEQS = 1


def draw_lengths(key, part):
    total = CHAINS * SEQS
    base = jax.random.randint(jax.random.fold_in(key, 11), (total,), LENGTH // 4, LENGTH + 1, dtype=jnp.int32)
    order = jax.random.permutation(jax.random.fold_in(key, 12), jnp.arange(total, dtype=jnp.int32))
    places = jnp.arange(total, dtype=jnp.int32)
    base = jnp.where(places == order[0], LENGTH, jnp.where(places == order[1], LENGTH // 4, base))
    return base.reshape(CHAINS, SEQS).astype(jnp.int32)


def block_levels(rng, extent, split, least, high):
    factor_of = 1.0
    for dim, parts in split:
        draws = jax.random.uniform(jax.random.fold_in(jax.random.fold_in(rng, 6), dim), (parts,), jnp.float32, least / len(split), high / len(split))
        factor_of = factor_of * jnp.repeat(jnp.exp(draws), extent[dim] // parts).reshape((-1,) + (1,) * (len(extent) - 1 - dim))
    return factor_of


def gaussian(own_key, shape, scale, most, pieces=(), kind=jnp.bfloat16):
    level = block_levels(own_key, shape, pieces, -0.22, 0.18) if pieces else 1.0
    values = jax.random.normal(own_key, shape, jnp.float32) * scale * level
    return jnp.minimum(jnp.maximum(values, -most), most).astype(kind)


def setup_inputs(seed: int = 0) -> dict:
    splits = jax.random.split(jax.random.key(seed), 16)
    return {
        "tokens": gaussian(splits[0], (CHAINS, CHAIN_TOKENS, D), 1.0, 6.0, ((0, 4), (1, 8))),
        "lengths": draw_lengths(jax.random.fold_in(splits[15], 71), 0),
        "cotangent": gaussian(splits[2], (CHAINS, CHAIN_TOKENS, D), 1.0, 6.0, ((0, 4), (1, 8))),
        "ln1_gain": jnp.clip(1.0 + 0.1 * jax.random.normal(splits[3], (D,), jnp.float32), 0.5, 1.5).astype(jnp.bfloat16),
        "ln1_bias": gaussian(splits[4], (D,), 0.3, 1.5, ((0, 32),)),
        "w_qkv": gaussian(splits[5], (D, 3, D), (D // 2) ** -0.5, 0.1875, ((0, 8), (2, 4))),
        "qv_bias": gaussian(splits[6], (2, D), 0.3, 1.5, ((1, 4),)),
        "w_out": gaussian(splits[7], (D, D), (D // 8) ** -0.5, 0.375, ((0, 4), (1, 8))),
        "out_bias": gaussian(splits[8], (D,), 0.3, 1.5, ((0, 32),)),
        "ln2_gain": jnp.clip(1.0 + 0.1 * jax.random.normal(splits[9], (D,), jnp.float32), 0.5, 1.5).astype(jnp.bfloat16),
        "ln2_bias": gaussian(splits[10], (D,), 0.3, 1.5, ((0, 32),)),
        "w_fc": gaussian(splits[11], (D, FF), D ** -0.5, 0.125, ((0, 8), (1, 4))),
        "fc_bias": gaussian(splits[12], (FF,), 0.3, 1.5, ((0, 4),)),
        "w_proj": gaussian(splits[13], (FF, D), FF ** -0.5, 0.0625, ((0, 4), (1, 8))),
        "proj_bias": gaussian(splits[14], (D,), 0.3, 1.5, ((0, 32),)),
    }


@jax.custom_vjp
def low(v):
    return lax.optimization_barrier(v.astype(jnp.bfloat16)).astype(jnp.float32)

@jax.custom_vjp
def low_back(v):
    return v

def low_keep(v):
    return (low(v), None)

def low_pass(kept, grad):
    return (grad,)

def back_keep(v):
    return (v, None)

def back_low(kept, grad):
    return (low(grad),)
low.defvjp(low_keep, low_pass)
low_back.defvjp(back_keep, back_low)

def layer_norm(values, gain, shift):
    mean = lax.optimization_barrier(jnp.mean(values, axis=-1, keepdims=True))
    centered = values - mean
    factor = lax.rsqrt(lax.optimization_barrier(jnp.mean(centered * centered, axis=-1, keepdims=True)) + 1e-05)
    return centered * factor * gain + shift

def gelu_tanh(values):
    return jax.nn.gelu(values, approximate=True)

def allowed_keys(query_pos, key_pos, limit):
    later = query_pos[:, None]
    earlier = key_pos[None, :]
    gap = later - earlier
    same = later // LENGTH == earlier // LENGTH
    live = (earlier % LENGTH < limit[:, None]) | (gap == 0)
    return (earlier >= 0) & (gap >= 0) & (gap < WINDOW) & same & live

def block_forward(inputs, limit, params):
    g_one, b_one, w_in, qv_shift, w_mix, mix_shift, g_two, b_two, w_up, up_shift, w_down, down_shift = params
    highest = lax.Precision.HIGHEST
    count = inputs.shape[0]
    width = inputs.shape[1]
    scale = HEAD_DIM ** (-0.5)
    normed = low(layer_norm(inputs, g_one, b_one))
    packed = jnp.dot(normed, w_in, precision=highest)
    query = low_back(low(packed[:, :width] + qv_shift[:width]))
    key = low_back(low(packed[:, width:2 * width]))
    value = low_back(low(packed[:, 2 * width:] + qv_shift[width:]))
    key_pad = jnp.concatenate([jnp.zeros((WINDOW, width), jnp.float32), key], axis=0)
    value_pad = jnp.concatenate([jnp.zeros((WINDOW, width), jnp.float32), value], axis=0)
    block = math.gcd(count, 512)

    def attend(index):
        start = index * block
        qblock = lax.dynamic_slice_in_dim(query, start, block, 0).reshape(block, HEADS, HEAD_DIM)
        kblock = lax.dynamic_slice_in_dim(key_pad, start, block + WINDOW, 0).reshape(block + WINDOW, HEADS, HEAD_DIM)
        vblock = lax.dynamic_slice_in_dim(value_pad, start, block + WINDOW, 0).reshape(block + WINDOW, HEADS, HEAD_DIM)
        query_pos = start + jnp.arange(block, dtype=jnp.int32)
        key_pos = start - WINDOW + jnp.arange(block + WINDOW, dtype=jnp.int32)
        bound = lax.dynamic_slice_in_dim(limit, start, block, 0)
        mask = allowed_keys(query_pos, key_pos, bound)
        scores = low_back(jnp.einsum('qhd,khd->hqk', qblock, kblock, precision=highest) * scale)
        scores = jnp.where(mask[None], scores, -1e+30)
        top = lax.optimization_barrier(jnp.max(scores, axis=-1, keepdims=True))
        expo = jnp.exp(scores - top)
        probs = low(expo / lax.optimization_barrier(jnp.sum(expo, axis=-1, keepdims=True)))
        return jnp.einsum('hqk,khd->qhd', probs, vblock, precision=highest).reshape(block, width)
    mixed = lax.map(jax.checkpoint(attend), jnp.arange(count // block, dtype=jnp.int32)).reshape(count, width)
    mixed = low_back(low(mixed))
    branch = low_back(jnp.dot(mixed, w_mix, precision=highest) + mix_shift)
    resid = inputs + branch
    second = low(layer_norm(resid, g_two, b_two))
    pre = low_back(jnp.dot(second, w_up, precision=highest) + up_shift)
    active = low(gelu_tanh(pre))
    ffn = low_back(jnp.dot(active, w_down, precision=highest) + down_shift)
    return resid + ffn

def reference(tokens, lengths, cotangent, ln1_gain, ln1_bias, w_qkv, qv_bias, w_out, out_bias, ln2_gain, ln2_bias, w_fc, fc_bias, w_proj, proj_bias):
    chains, chain_tokens, width = tokens.shape
    flat_qkv = w_qkv.reshape(width, 3 * width)
    flat_qv = qv_bias.reshape(2 * width)
    params = tuple((p.astype(jnp.float32) for p in (ln1_gain, ln1_bias, flat_qkv, flat_qv, w_out, out_bias, ln2_gain, ln2_bias, w_fc, fc_bias, w_proj, proj_bias)))
    flat = tokens.reshape(chains * chain_tokens, width).astype(jnp.float32)
    cot_flat = cotangent.reshape(chains * chain_tokens, width).astype(jnp.float32)
    seq_lengths = lengths.reshape(-1).astype(jnp.int32)
    total_seqs = seq_lengths.shape[0]
    group = math.gcd(total_seqs, max(1, 4096 // LENGTH))
    count = group * LENGTH
    turns = total_seqs // group

    def run(carry, index):
        start = index * count
        inputs = lax.dynamic_slice_in_dim(flat, start, count, 0)
        cot = lax.dynamic_slice_in_dim(cot_flat, start, count, 0)
        lens = lax.dynamic_slice_in_dim(seq_lengths, index * group, group, 0)
        positions = jnp.arange(count, dtype=jnp.int32)
        limit = jnp.take(lens, positions // LENGTH)
        valid = (positions % LENGTH < limit).astype(jnp.float32)

        def forward(values, *weights):
            return block_forward(values, limit, weights)
        result, backward = jax.vjp(forward, inputs, *params)
        grads = backward(cot * valid[:, None])
        summed = tuple((a + b for a, b in zip(carry, grads[1:])))
        return (summed, (result, grads[0]))
    zeros = tuple((jnp.zeros_like(p) for p in params))
    totals, (outputs, grad_in) = lax.scan(run, zeros, jnp.arange(turns, dtype=jnp.int32))
    block_out = outputs.reshape(chains, chain_tokens, width).astype(jnp.bfloat16)
    grad_tokens = grad_in.reshape(chains, chain_tokens, width).astype(jnp.bfloat16)
    grad_qkv = totals[2].reshape(width, 3, width)
    grad_qv = totals[3].reshape(2, width)
    return (block_out, grad_tokens, totals[0], totals[1], grad_qkv, grad_qv, totals[4], totals[5], totals[6], totals[7], totals[8], totals[9], totals[10], totals[11])
```

```python
import jax
import jax.numpy as jnp
from jax import lax
from jax.experimental import pallas as pl
from jax.experimental.pallas import tpu as pltpu
from jax.sharding import PartitionSpec as P

HEAD_DIM = 128
WINDOW = 256
F32 = jnp.float32
BF16 = jnp.bfloat16


def ring_order(count):
    return list(range(0, count, 2)) + list(range(count - 1, 0, -2))


def ring_place(index, count):
    return jnp.where(index % 2 == 0, index // 2, count - 1 - index // 2)


def ring_index(place, count):
    return jnp.where(place < count // 2, 2 * place, 2 * (count - 1 - place) + 1)


def hop(value, forward):
    order = ring_order(lax.axis_size("seq"))
    ahead = order[1:] + order[:1]
    pairs = zip(order, ahead) if forward else zip(ahead, order)
    return lax.ppermute(value, "seq", list(pairs))


def swap(value, axis, bit):
    return lax.ppermute(value, axis, [(i, i ^ bit) for i in range(lax.axis_size(axis))])


def bits_of(count):
    return [1 << k for k in range(count.bit_length() - 1)]


def forward_steps(count, flip):
    return count - 1 - count // 2 if flip else count // 2


def ring_gather(value, flip=False):
    count = lax.axis_size("seq")
    slots = [value] + [None] * (count - 1)
    steps = forward_steps(count, flip)
    ahead = behind = value
    for t in range(1, steps + 1):
        ahead = hop(ahead, True)
        slots[count - t] = ahead
        if t <= count - 1 - steps:
            behind = hop(behind, False)
            slots[t] = behind
    for t in range(steps + 1, count - steps):
        behind = hop(behind, False)
        slots[t] = behind
    return slots


def ring_scatter(make, flip=False, wire=BF16):
    count = lax.axis_size("seq")
    steps = forward_steps(count, flip)
    ahead = behind = None
    for j in range(steps, 0, -1):
        part = make(j) if ahead is None else make(j) + ahead.astype(F32)
        ahead = hop(part.astype(wire), True)
    for j in range(steps + 1, count):
        part = make(j) if behind is None else make(j) + behind.astype(F32)
        behind = hop(part.astype(wire), False)
    return make(0) + ahead.astype(F32) + behind.astype(F32)


def seq_total(value):
    for bit in bits_of(lax.axis_size("seq")):
        value = value + swap(value, "seq", bit)
    return value


def batch_gather(value):
    parts = {0: value}
    for bit in reversed(bits_of(lax.axis_size("batch"))):
        parts.update({r | bit: swap(v, "batch", bit) for r, v in list(parts.items())})
    return [parts[r] for r in range(len(parts))]


def batch_scatter(parts, wire=BF16):
    parts = dict(enumerate(parts))
    for bit in bits_of(len(parts)):
        for r in [r for r in parts if r & bit]:
            got = swap(parts[r].astype(wire), "batch", bit)
            parts[r ^ bit] = parts[r ^ bit].astype(F32) + got.astype(F32)
            del parts[r]
    return parts[0]


def to_slots(value, axis=-1):
    count = lax.axis_size("seq")
    width = value.shape[axis] // count
    place = ring_place(lax.axis_index("seq"), count)
    return jnp.concatenate(
        [
            lax.dynamic_slice_in_dim(
                value, ring_index((place + j) % count, count) * width, width, axis
            )
            for j in range(count)
        ],
        axis=axis,
    )


def from_slots(value, axis=-1):
    count = lax.axis_size("seq")
    width = value.shape[axis] // count
    place = ring_place(lax.axis_index("seq"), count)
    return jnp.concatenate(
        [
            lax.dynamic_slice_in_dim(
                value, (ring_place(jnp.int32(i), count) - place) % count * width, width, axis
            )
            for i in range(count)
        ],
        axis=axis,
    )


def norm_stats(values):
    mean = jnp.mean(values, axis=-1, keepdims=True)
    centered = values - mean
    factor = lax.rsqrt(jnp.mean(centered * centered, axis=-1, keepdims=True) + 1e-05)
    return centered * factor, factor


def norm_back(grad, unit, factor, gain):
    scaled = grad * gain
    inner = jnp.mean(scaled * unit, axis=-1, keepdims=True)
    return factor * (scaled - jnp.mean(scaled, axis=-1, keepdims=True) - unit * inner)


def gelu_tanh(values):
    return jax.nn.gelu(values, approximate=True)


def dot_t(left, right, left_dim, right_dim):
    return lax.dot_general(
        left, right, (((left_dim,), (right_dim,)), ((), ())), preferred_element_type=F32
    )


def masks(start, limit):
    row = lax.broadcasted_iota(jnp.int32, (WINDOW, WINDOW), 0)
    col = lax.broadcasted_iota(jnp.int32, (WINDOW, WINDOW), 1)
    own = col <= row
    spot = jnp.where(own, start + col, start - WINDOW + col)
    return own, (spot >= 0) & ((spot < limit) | (row == col))


def weights_of(query, key, early_key, own, live):
    scores = jnp.where(own, dot_t(query, key, 1, 1), dot_t(query, early_key, 1, 1))
    scores = jnp.where(live, scores * (HEAD_DIM**-0.5), -1e30)
    expo = jnp.exp(scores - jnp.max(scores, axis=-1, keepdims=True))
    return expo / jnp.sum(expo, axis=-1, keepdims=True)


def attend_kernel(limits, start, packed, early, mixed):
    width = mixed.shape[1]
    own, live = masks(start[0], limits[pl.program_id(0)])
    for at in range(0, width, HEAD_DIM):
        cols = lambda k: slice(k * width + at, k * width + at + HEAD_DIM)
        probs = weights_of(packed[:, cols(0)], packed[:, cols(1)], early[:, cols(0)], own, live)
        near = jnp.where(own, probs, 0.0).astype(BF16)
        far = jnp.where(own, 0.0, probs).astype(BF16)
        mixed[:, cols(0)] = (
            dot_t(near, packed[:, cols(2)], 1, 0) + dot_t(far, early[:, cols(1)], 1, 0)
        ).astype(BF16)


def attend_back_kernel(limits, start, packed, early, grad, g_packed, g_early):
    width = grad.shape[1]
    scale = HEAD_DIM**-0.5
    own, live = masks(start[0], limits[pl.program_id(0)])
    for at in range(0, width, HEAD_DIM):
        cols = lambda k: slice(k * width + at, k * width + at + HEAD_DIM)
        query, key, value = (packed[:, cols(k)] for k in range(3))
        early_key, early_value = (early[:, cols(k)] for k in range(2))
        out = grad[:, cols(0)]
        probs = weights_of(query, key, early_key, own, live)
        g_probs = jnp.where(own, dot_t(out, value, 1, 1), dot_t(out, early_value, 1, 1))
        delta = jnp.sum(probs * g_probs, axis=-1, keepdims=True)
        g_scores = probs * (g_probs - delta)
        near = jnp.where(own, probs, 0.0).astype(BF16)
        far = jnp.where(own, 0.0, probs).astype(BF16)
        g_near = jnp.where(own, g_scores, 0.0).astype(BF16)
        g_far = jnp.where(own, 0.0, g_scores).astype(BF16)
        g_packed[:, cols(0)] = (
            (dot_t(g_near, key, 1, 0) + dot_t(g_far, early_key, 1, 0)) * scale
        ).astype(BF16)
        g_packed[:, cols(1)] = (dot_t(g_near, query, 0, 0) * scale).astype(BF16)
        g_packed[:, cols(2)] = dot_t(near, out, 0, 0).astype(BF16)
        g_early[:, cols(0)] = (dot_t(g_far, query, 0, 0) * scale).astype(BF16)
        g_early[:, cols(1)] = dot_t(far, out, 0, 0).astype(BF16)


def per_chain(kernel, limits, start, arrays, widths, flops):
    rows = arrays[0].shape[0]
    block = lambda w: pl.BlockSpec((WINDOW, w), lambda i, *_: (i, 0))
    moved = 2 * rows * (sum(a.shape[1] for a in arrays) + sum(widths))
    return pl.pallas_call(
        kernel,
        grid_spec=pltpu.PrefetchScalarGridSpec(
            num_scalar_prefetch=2,
            grid=(rows // WINDOW,),
            in_specs=[block(a.shape[1]) for a in arrays],
            out_specs=[block(w) for w in widths],
        ),
        out_shape=[jax.ShapeDtypeStruct((rows, w), BF16) for w in widths],
        cost_estimate=pl.CostEstimate(
            flops=flops, bytes_accessed=moved, transcendentals=rows * WINDOW
        ),
    )(limits, start, *arrays)


def shards(
    tokens,
    lengths,
    cotangent,
    ln1_gain,
    ln1_bias,
    w_qkv,
    qv_bias,
    w_out,
    out_bias,
    ln2_gain,
    ln2_bias,
    w_fc,
    fc_bias,
    w_proj,
    proj_bias,
):
    groups = lax.axis_size("batch")
    chain = lax.axis_index("batch")
    place = lax.axis_index("seq")
    rows, width = tokens.shape[1:]
    slice_width = width // lax.axis_size("seq")
    heads_width = w_out.shape[0]
    assert rows == WINDOW and lengths.shape[1] == 1 and tokens.shape[0] == 1
    start = (place * rows).astype(jnp.int32)
    limits = jnp.stack([lengths[chain ^ r, 0] for r in range(groups)])
    valid = (start + jnp.arange(rows, dtype=jnp.int32) < limits[0]).astype(F32)

    tokens, cotangent = tokens[0], cotangent[0]
    count = lax.axis_size("seq")
    early_tokens = lax.ppermute(tokens, "seq", [(i, i + 1) for i in range(count - 1)])
    own_tokens = to_slots(tokens)
    all_tokens = jnp.concatenate(batch_gather(own_tokens), axis=0)
    all_early = jnp.concatenate(batch_gather(to_slots(early_tokens)), axis=0)
    grad_out = to_slots(cotangent).astype(F32) * valid[:, None]
    grad_y_own = grad_out.astype(BF16)
    grad_y = jnp.concatenate(batch_gather(grad_y_own), axis=0)

    vectors = jnp.stack([ln1_gain, ln1_bias, out_bias, ln2_gain, ln2_bias, proj_bias])
    parts = jnp.stack(batch_gather(vectors))
    parts = jnp.concatenate([parts[chain ^ r] for r in range(groups)], axis=1)
    vectors = jnp.concatenate(ring_gather(parts), axis=1).astype(F32)
    gain_one, shift_one, mix_shift, gain_two, shift_two, down_shift = (
        vectors[i] for i in range(6)
    )

    proj_in = jnp.concatenate(ring_gather(w_qkv.reshape(slice_width, 3 * heads_width)), axis=0)
    proj_mix = jnp.concatenate(ring_gather(w_out, True), axis=1)
    proj_up = jnp.concatenate(ring_gather(w_fc), axis=0)
    proj_down = jnp.concatenate(ring_gather(w_proj, True), axis=1)

    normed = (norm_stats(all_tokens.astype(F32))[0] * gain_one + shift_one).astype(BF16)
    normed_early = (norm_stats(all_early.astype(F32))[0] * gain_one + shift_one).astype(BF16)
    qv_float = qv_bias.astype(F32)
    no_shift = jnp.zeros_like(qv_float[0])
    packed_shift = jnp.concatenate([qv_float[0], no_shift, qv_float[1]])
    packed = (dot_t(normed, proj_in, 1, 0) + packed_shift).astype(BF16)
    early = (
        dot_t(normed_early, proj_in[:, heads_width:], 1, 0) + packed_shift[heads_width:]
    ).astype(BF16)
    square = 2 * packed.shape[0] * WINDOW * heads_width
    starts = start.reshape(1)
    (mixed,) = per_chain(
        attend_kernel, limits, starts, (packed, early), (heads_width,), 4 * square
    )

    def spread(left, right, right_dim):
        half = left.shape[0] // 2
        far = dot_t(left[half:], right, 1, right_dim).astype(BF16)
        near = dot_t(left[:half], right, 1, right_dim).astype(BF16)
        each = [near[i : i + rows] for i in range(0, half, rows)]
        return batch_scatter(each + [far[i : i + rows] for i in range(0, half, rows)])

    inputs = own_tokens.astype(F32)
    resid = inputs + spread(mixed, proj_mix, 0) + mix_shift

    unit_two, factor_two = norm_stats(resid)
    second = jnp.concatenate(
        batch_gather((unit_two * gain_two + shift_two).astype(BF16)), axis=0
    )
    pre = dot_t(second, proj_up, 1, 0) + fc_bias.astype(F32)
    active_f, gelu_back = jax.vjp(gelu_tanh, pre)
    active = active_f.astype(BF16)
    result = resid + spread(active, proj_down, 0) + down_shift
    block_out = from_slots(result.astype(BF16))

    def cut(value, j):
        return value[:, j * slice_width : (j + 1) * slice_width]

    grad_w_proj = ring_scatter(lambda j: dot_t(active, cut(grad_y, j), 0, 0))
    grad_pre = gelu_back(dot_t(grad_y, proj_down, 1, 1))[0].astype(BF16)
    grad_w_fc = ring_scatter(lambda j: dot_t(cut(second, j), grad_pre, 0, 0), True)
    grad_fc_bias = jnp.sum(grad_pre.astype(F32), axis=0)
    grad_second = spread(grad_pre, proj_up, 1)
    grad_resid = grad_out + norm_back(grad_second, unit_two, factor_two, gain_two)
    grad_branch_own = grad_resid.astype(BF16)

    grad_branch = jnp.concatenate(batch_gather(grad_branch_own), axis=0)
    grad_w_out = ring_scatter(lambda j: dot_t(mixed, cut(grad_branch, j), 0, 0), True)
    grad_mixed = dot_t(grad_branch, proj_mix, 1, 1).astype(BF16)
    g_packed, g_early = per_chain(
        attend_back_kernel,
        limits,
        starts,
        (packed, early, grad_mixed),
        (3 * heads_width, 2 * heads_width),
        10 * square,
    )

    def qkv_part(j):
        late = dot_t(cut(normed_early, j), g_early, 0, 0)
        return dot_t(cut(normed, j), g_packed, 0, 0) + jnp.pad(late, ((0, 0), (heads_width, 0)))

    grad_w_qkv = ring_scatter(qkv_part).reshape(slice_width, 3, heads_width)
    back = spread(g_early, proj_in[:, heads_width:], 1)
    back = lax.ppermute(
        from_slots(back.astype(BF16)), "seq", [(i + 1, i) for i in range(count - 1)]
    )
    grad_normed = spread(g_packed, proj_in, 1) + to_slots(back).astype(F32)
    unit_one, factor_one = norm_stats(inputs)
    grad_tokens = grad_resid + norm_back(grad_normed, unit_one, factor_one, gain_one)

    column = lambda value: jnp.sum(value.astype(F32), axis=0)
    flat = jnp.concatenate(
        [
            grad_fc_bias,
            column(g_packed[:, :heads_width]),
            column(g_packed[:, 2 * heads_width :]) + column(g_early[:, heads_width:]),
        ]
    )
    flat = seq_total(flat)
    ff = grad_fc_bias.shape[0]
    sums = jnp.stack(
        [
            jnp.sum(grad_normed * unit_one, axis=0),
            jnp.sum(grad_normed, axis=0),
            column(grad_branch_own),
            jnp.sum(grad_second * unit_two, axis=0),
            jnp.sum(grad_second, axis=0),
            column(grad_y_own),
        ]
    )
    sums = ring_scatter(lambda j: cut(sums, j), wire=F32)
    piece = slice_width // groups
    sums = batch_scatter(
        [lax.dynamic_slice_in_dim(sums, (chain ^ r) * piece, piece, 1) for r in range(groups)],
        wire=F32,
    )
    return (
        block_out[None],
        from_slots(grad_tokens.astype(BF16))[None],
        sums[0],
        sums[1],
        grad_w_qkv,
        flat[ff:].reshape(2, heads_width),
        grad_w_out,
        sums[2],
        sums[3],
        sums[4],
        grad_w_fc,
        flat[:ff],
        grad_w_proj,
        sums[5],
    )


def solution(mesh):
    everywhere = P(("seq", "batch"))
    rows = P("batch", "seq", None)
    return jax.shard_map(
        shards,
        mesh=mesh,
        in_specs=(
            rows,
            P(),
            rows,
            everywhere,
            everywhere,
            P("seq", None, "batch"),
            P(None, "batch"),
            P("batch", "seq"),
            everywhere,
            everywhere,
            everywhere,
            P("seq", "batch"),
            P("batch"),
            P("batch", "seq"),
            everywhere,
        ),
        out_specs=(
            rows,
            rows,
            everywhere,
            everywhere,
            P("seq", None, "batch"),
            P(None, "batch"),
            P("batch", "seq"),
            everywhere,
            everywhere,
            everywhere,
            P("seq", "batch"),
            P("batch"),
            P("batch", "seq"),
            everywhere,
        ),
        check_vma=False,
    )
```

```python
import jax
import jax.numpy as jnp
from jax import lax
from jax.experimental import pallas as pl
from jax.experimental.pallas import tpu as pltpu
from jax.sharding import PartitionSpec as P

HEAD_DIM = 128
WINDOW = 256
F32 = jnp.float32
BF16 = jnp.bfloat16


def ring_order(count):
    return list(range(0, count, 2)) + list(range(count - 1, 0, -2))


def ring_place(index, count):
    return jnp.where(index % 2 == 0, index // 2, count - 1 - index // 2)


def ring_index(place, count):
    return jnp.where(place < count // 2, 2 * place, 2 * (count - 1 - place) + 1)


def slot_owners():
    count = lax.axis_size("seq")
    place = ring_place(lax.axis_index("seq"), count)
    return ring_index((place + jnp.arange(count, dtype=jnp.int32)) % count, count)


def owner_slots():
    count = lax.axis_size("seq")
    place = ring_place(lax.axis_index("seq"), count)
    return (ring_place(jnp.arange(count, dtype=jnp.int32), count) - place) % count


def tie(value, *after):
    after = [v for v in after if v is not None]
    return lax.optimization_barrier((value, *after))[0] if after else value


class Ring:
    def __init__(self):
        self.count = lax.axis_size("seq")
        self.queue = {True: [], False: []}
        self.last = {True: None, False: None}
        self.before = []
        self.flip = False

    def hop(self, value, forward):
        order = ring_order(self.count)
        ahead = order[1:] + order[:1]
        pairs = zip(order, ahead) if forward else zip(ahead, order)
        got = lax.ppermute(tie(value, self.last[forward]), "seq", list(pairs))
        self.last[forward] = got
        return got

    def advance(self):
        self.before = [v for v in self.last.values() if v is not None]
        for forward, queue in self.queue.items():
            if queue:
                queue.pop(0)()
        for queue in self.queue.values():
            if queue and hasattr(queue[0], "ready"):
                queue[0].ready()

    def now(self, value):
        return tie(value, *self.before)

    def legs(self):
        steps = self.count - 1 - self.count // 2 if self.flip else self.count // 2
        self.flip = not self.flip
        return ((True, steps), (False, self.count - 1 - steps))

    def gather(self, value):
        slots = [value] + [None] * (self.count - 1)
        for forward, steps in self.legs():
            for t in range(1, steps + 1):
                at = self.count - t if forward else t

                def step(source=(at + (1 if forward else -1)) % self.count, at=at, way=forward):
                    slots[at] = self.hop(slots[source], way)

                self.queue[forward].append(step)
        return slots

    def scatter(self, make):
        return Scatter(self, make)


class Scatter:
    def __init__(self, ring, make):
        self.ring, self.make = ring, make
        self.got = {True: None, False: None}
        for forward, steps in ring.legs():
            for t in range(steps):
                j = steps - t if forward else ring.count - steps + t
                ring.queue[forward].append(Leg(self, forward, j))

    def total(self):
        return self.make(0) + self.got[True].astype(F32) + self.got[False].astype(F32)


class Leg:
    def __init__(self, scatter, forward, j):
        self.scatter, self.forward, self.j = scatter, forward, j
        self.part = None

    def ready(self):
        if self.part is None:
            self.part = self.scatter.make(self.j)

    def __call__(self):
        self.ready()
        part, got = self.part, self.scatter.got[self.forward]
        if got is not None:
            part = part + got.astype(F32)
        self.scatter.got[self.forward] = self.scatter.ring.hop(part.astype(BF16), self.forward)


def swap(value, axis, bit):
    return lax.ppermute(value, axis, [(i, i ^ bit) for i in range(lax.axis_size(axis))])


def bits_of(count):
    return [1 << k for k in range(count.bit_length() - 1)]


def small_gather(value):
    count, groups = lax.axis_size("seq"), lax.axis_size("batch")
    parts = value[None]
    for axis in ("seq", "batch"):
        for bit in bits_of(lax.axis_size(axis)):
            parts = jnp.concatenate([parts, swap(parts, axis, bit)], axis=0)
    own_s, own_b = lax.axis_index("seq"), lax.axis_index("batch")
    order = (slot_owners() ^ own_s)[:, None] + count * (
        jnp.arange(groups, dtype=jnp.int32) ^ own_b
    )
    parts = jnp.take(parts, order.reshape(-1), axis=0)
    return jnp.moveaxis(parts, 0, -2).reshape(*value.shape[:-1], -1)


def small_totals(value, flat):
    count, groups = lax.axis_size("seq"), lax.axis_size("batch")
    own_s, own_b = lax.axis_index("seq"), lax.axis_index("batch")
    parts = jnp.moveaxis(value.reshape(*value.shape[:-1], count * groups, -1), -2, 0)
    order = owner_slots()[jnp.arange(count, dtype=jnp.int32) ^ own_s] * groups + (
        jnp.arange(groups, dtype=jnp.int32) ^ own_b
    )[:, None]
    parts = jnp.take(parts, order.reshape(-1), axis=0)
    for bit in reversed(bits_of(groups)):
        half = parts.shape[0] // 2
        parts = parts[:half] + swap(parts[half:], "batch", bit)
    piece = parts.shape[1:]
    parts = parts.reshape(count, -1)
    for bit in reversed(bits_of(count)):
        half = parts.shape[0] // 2
        sent = jnp.concatenate([parts[half:].reshape(-1), flat])
        got = swap(sent, "seq", bit)
        at = half * parts.shape[1]
        parts = parts[:half] + got[:at].reshape(half, -1)
        flat = flat + got[at:]
    return parts.reshape(piece), flat


def batch_gather(value):
    parts = {0: value}
    for bit in reversed(bits_of(lax.axis_size("batch"))):
        parts.update({r | bit: swap(v, "batch", bit) for r, v in list(parts.items())})
    return [parts[r] for r in range(len(parts))]


def batch_scatter(parts, wire=BF16):
    parts = dict(enumerate(parts))
    for bit in bits_of(len(parts)):
        for r in [r for r in parts if r & bit]:
            got = swap(parts[r].astype(wire), "batch", bit)
            parts[r ^ bit] = parts[r ^ bit].astype(F32) + got.astype(F32)
            del parts[r]
    return parts[0]


def move_kernel(order, value, moved):
    width = value.shape[1] // order.shape[0]
    for i in range(order.shape[0]):
        source = pl.multiple_of(order[i] * width, width)
        moved[:, i * width : (i + 1) * width] = value[:, pl.ds(source, width)]


def reorder(value, order):
    rows, columns = value.shape
    width = columns // order.shape[0]
    if width % 128:
        return jnp.take(value.reshape(rows, -1, width), order, axis=1).reshape(value.shape)
    block = pl.BlockSpec((rows // 4, columns), lambda i, *_: (i, 0))
    return pl.pallas_call(
        move_kernel,
        grid_spec=pltpu.PrefetchScalarGridSpec(
            num_scalar_prefetch=1, grid=(4,), in_specs=[block], out_specs=block
        ),
        out_shape=jax.ShapeDtypeStruct(value.shape, value.dtype),
        cost_estimate=pl.CostEstimate(
            flops=0, bytes_accessed=2 * value.size * value.dtype.itemsize, transcendentals=0
        ),
    )(order, value)


def norm_stats(values):
    mean = jnp.mean(values, axis=-1, keepdims=True)
    centered = values - mean
    factor = lax.rsqrt(jnp.mean(centered * centered, axis=-1, keepdims=True) + 1e-05)
    return centered * factor, factor


def norm_back(grad, unit, factor, gain):
    scaled = grad * gain
    inner = jnp.mean(scaled * unit, axis=-1, keepdims=True)
    return factor * (scaled - jnp.mean(scaled, axis=-1, keepdims=True) - unit * inner)


def gelu_and_slope(values):
    root, cubic = (2 / jnp.pi) ** 0.5, 0.044715
    square = values * values
    bend = jnp.tanh(values * (root + root * cubic * square))
    half = 0.5 + 0.5 * bend
    slope = half + values * (0.5 - 0.5 * bend * bend) * (root + 3 * root * cubic * square)
    return values * half, slope


def dot_t(left, right, left_dim, right_dim):
    return lax.dot_general(
        left, right, (((left_dim,), (right_dim,)), ((), ())), preferred_element_type=F32
    )


def masks(start, limit):
    row = lax.broadcasted_iota(jnp.int32, (WINDOW, WINDOW), 0)
    col = lax.broadcasted_iota(jnp.int32, (WINDOW, WINDOW), 1)
    own = col <= row
    spot = jnp.where(own, start + col, start - WINDOW + col)
    return own, (spot >= 0) & ((spot < limit) | (row == col))


def weights_of(query, key, early_key, own, live):
    scores = jnp.where(own, dot_t(query, key, 1, 1), dot_t(query, early_key, 1, 1))
    scores = jnp.where(live, scores * (HEAD_DIM**-0.5), -1e30)
    expo = jnp.exp(scores - jnp.max(scores, axis=-1, keepdims=True))
    return expo / jnp.sum(expo, axis=-1, keepdims=True)


def attend_kernel(limits, start, packed, early, mixed):
    width = mixed.shape[1]
    own, live = masks(start[0], limits[pl.program_id(0)])
    for at in range(0, width, HEAD_DIM):
        cols = lambda k: slice(k * width + at, k * width + at + HEAD_DIM)
        probs = weights_of(packed[:, cols(0)], packed[:, cols(1)], early[:, cols(0)], own, live)
        near = jnp.where(own, probs, 0.0).astype(BF16)
        far = jnp.where(own, 0.0, probs).astype(BF16)
        mixed[:, cols(0)] = (
            dot_t(near, packed[:, cols(2)], 1, 0) + dot_t(far, early[:, cols(1)], 1, 0)
        ).astype(BF16)


def attend_back_kernel(limits, start, packed, early, grad, g_packed, g_early):
    width = grad.shape[1]
    scale = HEAD_DIM**-0.5
    own, live = masks(start[0], limits[pl.program_id(0)])
    for at in range(0, width, HEAD_DIM):
        cols = lambda k: slice(k * width + at, k * width + at + HEAD_DIM)
        query, key, value = (packed[:, cols(k)] for k in range(3))
        early_key, early_value = (early[:, cols(k)] for k in range(2))
        out = grad[:, cols(0)]
        probs = weights_of(query, key, early_key, own, live)
        g_probs = jnp.where(own, dot_t(out, value, 1, 1), dot_t(out, early_value, 1, 1))
        delta = jnp.sum(probs * g_probs, axis=-1, keepdims=True)
        g_scores = probs * (g_probs - delta)
        near = jnp.where(own, probs, 0.0).astype(BF16)
        far = jnp.where(own, 0.0, probs).astype(BF16)
        g_near = jnp.where(own, g_scores, 0.0).astype(BF16)
        g_far = jnp.where(own, 0.0, g_scores).astype(BF16)
        g_packed[:, cols(0)] = (
            (dot_t(g_near, key, 1, 0) + dot_t(g_far, early_key, 1, 0)) * scale
        ).astype(BF16)
        g_packed[:, cols(1)] = (dot_t(g_near, query, 0, 0) * scale).astype(BF16)
        g_packed[:, cols(2)] = dot_t(near, out, 0, 0).astype(BF16)
        g_early[:, cols(0)] = (dot_t(g_far, query, 0, 0) * scale).astype(BF16)
        g_early[:, cols(1)] = dot_t(far, out, 0, 0).astype(BF16)


def per_chain(kernel, limits, start, arrays, widths, flops):
    rows = arrays[0].shape[0]
    block = lambda w: pl.BlockSpec((WINDOW, w), lambda i, *_: (i, 0))
    moved = 2 * rows * (sum(a.shape[1] for a in arrays) + sum(widths))
    return pl.pallas_call(
        kernel,
        grid_spec=pltpu.PrefetchScalarGridSpec(
            num_scalar_prefetch=2,
            grid=(rows // WINDOW,),
            in_specs=[block(a.shape[1]) for a in arrays],
            out_specs=[block(w) for w in widths],
        ),
        out_shape=[jax.ShapeDtypeStruct((rows, w), BF16) for w in widths],
        cost_estimate=pl.CostEstimate(
            flops=flops, bytes_accessed=moved, transcendentals=rows * WINDOW
        ),
    )(limits, start, *arrays)


def shards(
    tokens,
    lengths,
    cotangent,
    ln1_gain,
    ln1_bias,
    w_qkv,
    qv_bias,
    w_out,
    out_bias,
    ln2_gain,
    ln2_bias,
    w_fc,
    fc_bias,
    w_proj,
    proj_bias,
):
    groups = lax.axis_size("batch")
    chain = lax.axis_index("batch")
    place = lax.axis_index("seq")
    rows, width = tokens.shape[1:]
    count = lax.axis_size("seq")
    slice_width = width // count
    heads_width = w_out.shape[0]
    assert rows == WINDOW and lengths.shape[1] == 1 and tokens.shape[0] == 1
    start = (place * rows).astype(jnp.int32)
    limits = lengths[:, 0][chain ^ jnp.arange(groups, dtype=jnp.int32)]
    valid = (start + jnp.arange(rows, dtype=jnp.int32) < limits[0]).astype(F32)
    to_slots, from_slots = slot_owners(), owner_slots()

    tokens, cotangent = tokens[0], cotangent[0]
    vectors = small_gather(
        jnp.stack([ln1_gain, ln1_bias, out_bias, ln2_gain, ln2_bias, proj_bias])
    ).astype(F32)
    gain_one, shift_one, mix_shift, gain_two, shift_two, down_shift = (
        vectors[i] for i in range(6)
    )
    def cut(value, j):
        return value[:, j * slice_width : (j + 1) * slice_width]

    def rows_of(parts):
        return jnp.concatenate(parts, axis=0)

    def spread(left, right, right_dim):
        half = left.shape[0] // 2
        far = dot_t(left[half:], right, 1, right_dim).astype(BF16)
        near = dot_t(left[:half], right, 1, right_dim).astype(BF16)
        each = [near[i : i + rows] for i in range(0, half, rows)]
        return batch_scatter(each + [far[i : i + rows] for i in range(0, half, rows)])

    ring = Ring()
    qkv_width = 3 * heads_width
    mix_slots = ring.gather(
        jnp.concatenate([w_qkv.reshape(slice_width, qkv_width), w_out.T], axis=1)
    )
    up_slots = ring.gather(w_fc)
    down_slots = ring.gather(w_proj)
    late = {}
    g_down = ring.scatter(lambda j: dot_t(late["active"], cut(late["dy"], j), 0, 0))
    g_up = ring.scatter(lambda j: dot_t(cut(late["second"], j), late["df"], 0, 0))

    def mix_part(j):
        early = dot_t(cut(late["normed_early"], j), late["g_early"], 0, 0)
        part = dot_t(cut(late["normed"], j), late["g_packed"], 0, 0)
        part = part + jnp.pad(early, ((0, 0), (heads_width, 0)))
        return jnp.concatenate([part, dot_t(cut(late["da"], j), late["mixed"], 0, 0)], axis=1)

    g_mix = ring.scatter(mix_part)
    turns = count // 2
    more = max(0, turns - 4)

    def advance(times=1):
        for _ in range(times):
            ring.advance()

    early_tokens = lax.ppermute(tokens, "seq", [(i, i + 1) for i in range(count - 1)])
    advance()
    own_tokens = reorder(tokens, to_slots)
    grad_out = reorder(cotangent, to_slots).astype(F32) * valid[:, None]
    grad_y_own = grad_out.astype(BF16)
    pairs = batch_gather(tie(rows_of([own_tokens, grad_y_own]), vectors))
    all_tokens = rows_of([p[:rows] for p in pairs])
    grad_y = rows_of([p[rows:] for p in pairs])
    own_early = reorder(early_tokens, to_slots)
    all_early = rows_of(batch_gather(own_early))
    advance(2 + more)
    normed = (norm_stats(all_tokens.astype(F32))[0] * gain_one + shift_one).astype(BF16)
    normed_early = (norm_stats(all_early.astype(F32))[0] * gain_one + shift_one).astype(BF16)
    advance()

    advance()
    mix_in = rows_of(mix_slots)
    proj_in, proj_mix = mix_in[:, :qkv_width], mix_in[:, qkv_width:]
    qv_float = qv_bias.astype(F32)
    packed_shift = jnp.concatenate([qv_float[0], jnp.zeros_like(qv_float[0]), qv_float[1]])
    packed = (dot_t(ring.now(normed), proj_in, 1, 0) + packed_shift).astype(BF16)
    early = (
        dot_t(ring.now(normed_early), proj_in[:, heads_width:], 1, 0) + packed_shift[heads_width:]
    ).astype(BF16)
    square = 2 * packed.shape[0] * WINDOW * heads_width
    starts = start.reshape(1)
    advance()
    (mixed,) = per_chain(
        attend_kernel, limits, starts, (ring.now(packed), early), (heads_width,), 4 * square
    )
    branch = spread(mixed, proj_mix, 1)
    advance()
    inputs = own_tokens.astype(F32)
    resid = inputs + ring.now(branch) + mix_shift
    unit_two, factor_two = norm_stats(resid)
    second_own = (unit_two * gain_two + shift_two).astype(BF16)
    second = rows_of(batch_gather(second_own))
    advance()

    advance(1 + more)
    proj_up = rows_of(up_slots)
    pre = dot_t(ring.now(second), proj_up, 1, 0) + fc_bias.astype(F32)
    active, slope = (v.astype(BF16) for v in gelu_and_slope(pre))
    late.update(active=active, dy=grad_y)
    advance(2 + more)
    proj_down = jnp.concatenate(down_slots, axis=1)
    advance()
    grad_active = dot_t(ring.now(grad_y), proj_down, 1, 1)
    grad_pre = (grad_active * slope.astype(F32)).astype(BF16)
    grad_fc_bias = jnp.sum(grad_pre.astype(F32), axis=0)
    late.update(second=second, df=grad_pre)
    advance()
    grad_second = spread(ring.now(grad_pre), proj_up, 1)
    advance()
    result = resid + spread(ring.now(active), proj_down, 0) + down_shift
    block_out = reorder(result.astype(BF16), from_slots)
    advance(1 + more)
    grad_resid = grad_out + norm_back(grad_second, unit_two, factor_two, gain_two)
    grad_branch_own = grad_resid.astype(BF16)
    grad_branch = rows_of(batch_gather(grad_branch_own))
    advance()

    grad_mixed = dot_t(ring.now(grad_branch), proj_mix, 1, 0).astype(BF16)
    g_packed, g_early = per_chain(
        attend_back_kernel,
        limits,
        starts,
        (packed, early, grad_mixed),
        (qkv_width, 2 * heads_width),
        10 * square,
    )
    late.update(
        normed=normed, normed_early=normed_early, g_packed=g_packed, g_early=g_early,
        da=grad_branch, mixed=mixed,
    )
    advance()
    back = spread(ring.now(g_early), proj_in[:, heads_width:], 1)
    moved = lax.ppermute(
        reorder(back.astype(BF16), from_slots), "seq", [(i + 1, i) for i in range(count - 1)]
    )
    advance()
    grad_own = spread(ring.now(g_packed), proj_in, 1)
    while ring.queue[True] or ring.queue[False]:
        advance()
    unit_one, factor_one = norm_stats(inputs)
    unit_early, _ = norm_stats(own_early.astype(F32))
    grad_normed = grad_own + reorder(moved, to_slots).astype(F32)
    grad_tokens = grad_resid + norm_back(grad_normed, unit_one, factor_one, gain_one)

    column = lambda value: jnp.sum(value.astype(F32), axis=0)
    flat = jnp.concatenate(
        [
            grad_fc_bias,
            column(g_packed[:, :heads_width]),
            column(g_packed[:, 2 * heads_width :]) + column(g_early[:, heads_width:]),
        ]
    )
    ff = grad_fc_bias.shape[0]
    sums = jnp.stack(
        [
            jnp.sum(grad_own * unit_one + back * unit_early, axis=0),
            jnp.sum(grad_own + back, axis=0),
            column(grad_branch_own),
            jnp.sum(grad_second * unit_two, axis=0),
            jnp.sum(grad_second, axis=0),
            column(grad_y_own),
        ]
    )
    sums, flat = small_totals(sums, flat)
    grad_mix_in = g_mix.total()
    return (
        block_out[None],
        reorder(grad_tokens.astype(BF16), from_slots)[None],
        sums[0],
        sums[1],
        grad_mix_in[:, :qkv_width].reshape(slice_width, 3, heads_width),
        flat[ff:].reshape(2, heads_width),
        grad_mix_in[:, qkv_width:].T,
        sums[2],
        sums[3],
        sums[4],
        g_up.total(),
        flat[:ff],
        g_down.total(),
        sums[5],
    )


def solution(mesh):
    everywhere = P(("seq", "batch"))
    rows = P("batch", "seq", None)
    return jax.shard_map(
        shards,
        mesh=mesh,
        in_specs=(
            rows,
            P(),
            rows,
            everywhere,
            everywhere,
            P("seq", None, "batch"),
            P(None, "batch"),
            P("batch", "seq"),
            everywhere,
            everywhere,
            everywhere,
            P("seq", "batch"),
            P("batch"),
            P("batch", "seq"),
            everywhere,
        ),
        out_specs=(
            rows,
            rows,
            everywhere,
            everywhere,
            P("seq", None, "batch"),
            P(None, "batch"),
            P("batch", "seq"),
            everywhere,
            everywhere,
            everywhere,
            P("seq", "batch"),
            P("batch"),
            P("batch", "seq"),
            everywhere,
        ),
        check_vma=False,
    )
```

```python
import jax
import jax.numpy as jnp
from jax import lax
from jax.experimental import pallas as pl
from jax.experimental.pallas import tpu as pltpu
from jax.sharding import PartitionSpec as P

HEAD_DIM = 128
TILE = 512
WINDOW = 256
F32 = jnp.float32
BF16 = jnp.bfloat16


def ring_order(count):
    return list(range(0, count, 2)) + list(range(count - 1, 0, -2))


def ring_place(index, count):
    return jnp.where(index % 2 == 0, index // 2, count - 1 - index // 2)


def ring_index(place, count):
    return jnp.where(place < count // 2, 2 * place, 2 * (count - 1 - place) + 1)


def slot_owners(ahead=0):
    count = lax.axis_size("seq")
    place = ring_place((lax.axis_index("seq") + ahead) % count, count)
    return ring_index((place + jnp.arange(count, dtype=jnp.int32)) % count, count)


def owner_slots():
    count = lax.axis_size("seq")
    place = ring_place(lax.axis_index("seq"), count)
    return (ring_place(jnp.arange(count, dtype=jnp.int32), count) - place) % count


def tie(value, *after):
    after = [v for v in after if v is not None]
    return lax.optimization_barrier((value, *after))[0] if after else value


class Ring:
    def __init__(self, after):
        self.count = lax.axis_size("seq")
        self.queue = {True: [], False: []}
        self.last = {True: after, False: after}
        self.before, self.wanted = [], []

    def hop(self, value, forward):
        order = ring_order(self.count)
        ahead = order[1:] + order[:1]
        pairs = zip(order, ahead) if forward else zip(ahead, order)
        value = tie(value, *self.wanted)
        self.before.append(value)
        self.last[forward] = lax.ppermute(value, "seq", list(pairs))
        return self.last[forward]

    def advance(self, times=1):
        for _ in range(times):
            self.before = []
            self.wanted += self.last.values()
            steps = [(way, *queue.pop(0)) for way, queue in self.queue.items() if queue]
            while steps:
                same = [s for s in steps if s[1] is steps[0][1]]
                moved = same[0][1]
                ways = [(w, j) for w, _, j in same]
                for (way, _, j), value in zip(same, moved.blocks(ways, self.wanted)):
                    moved.landed[way, j] = self.hop(value, way)
                steps = [s for s in steps if s not in same]
            self.wanted = []

    def now(self, *values):
        values = tie(values if len(values) > 1 else values[0], *self.before)
        return values

    def due(self, *values):
        self.wanted += values

    def add(self, moved, more_ahead):
        ahead = self.count // 2 if more_ahead else self.count - 1 - self.count // 2
        for forward, steps in ((True, ahead), (False, self.count - 1 - ahead)):
            self.queue[forward] += [(moved, j) for j in moved.slots(forward, steps)]
        return moved


class Gather:
    def __init__(self, value, axis):
        self.value, self.axis = value, axis
        self.landed, self.count = {}, lax.axis_size("seq")
        self.base = None

    def slots(self, forward, steps):
        return [self.count - 1 - t if forward else 1 + t for t in range(steps)]

    def blocks(self, steps, after):
        return [self.landed.get((w, j + (1 if w else -1)), self.value) for w, j in steps]

    def pieces(self):
        landed = self.landed
        return [self.value] + [
            landed.get((False, j), landed.get((True, j))) for j in range(1, self.count)
        ]

    def early(self, ring):
        pieces = self.pieces()
        pieces[self.count // 2] = self.value
        self.base = jnp.concatenate(pieces, axis=self.axis)
        ring.due(self.base)

    def all(self):
        if self.base is None:
            return jnp.concatenate(self.pieces(), axis=self.axis)
        j = self.count // 2
        last = self.landed[True, j]
        return lax.dynamic_update_slice_in_dim(
            self.base, last, j * last.shape[self.axis], self.axis
        )


class Scatter:
    def __init__(self, find):
        self.find, self.landed, self.count = find, {}, lax.axis_size("seq")

    def slots(self, forward, steps):
        return [steps - t if forward else self.count - steps + t for t in range(steps)]

    def blocks(self, steps, after):
        received = [self.landed.get((w, j + (1 if w else -1))) for w, j in steps]
        received = [v if v is None else tie(v, *after) for v in received]
        return join([self.find(j) for _, j in steps], received)

    def total(self, ring):
        value, at, rows = self.find(0)
        own = ring.now(value)[at * rows : (at + 1) * rows].astype(F32)
        return own + self.landed[True, 1].astype(F32) + (
            self.landed[False, self.count - 1].astype(F32)
        )


QUICK = pl.CostEstimate(flops=10**8, bytes_accessed=0, transcendentals=0)


def join(found, received):
    ways, width = len(found), found[0][0].shape[1]
    rows = found[0][2]
    steps = 2 if rows % 32 == 0 else 1
    step, got = rows // steps, [v for v in received if v is not None]

    def kernel(*refs):
        got_refs = list(refs[ways : ways + len(got)])
        for way in range(ways):
            value = refs[way][...]
            if received[way] is not None:
                value = (value.astype(F32) + got_refs.pop(0)[...].astype(F32)).astype(BF16)
            refs[len(refs) - ways + way][...] = value

    block = pl.BlockSpec((step, width), lambda i: (i, 0))
    return pl.pallas_call(
        kernel,
        grid=(steps,),
        in_specs=[
            pl.BlockSpec((step, width), lambda i, j=j: (j * steps + i, 0)) for _, j, _ in found
        ]
        + [block] * len(got),
        out_specs=[block] * ways,
        out_shape=[jax.ShapeDtypeStruct((rows, width), BF16)] * ways,
        cost_estimate=QUICK,
    )(*(v for v, _, _ in found), *got)


def matmul(lefts, right, finish, outs, nt=False, first=0, tiles=None, extra=(), keep=False):
    depth = lefts[0].shape[1]
    columns = right.shape[0 if nt else 1]
    tiles = tiles or columns // TILE
    blocks = sum(v.shape[0] for v in lefts) // WINDOW
    rows = blocks * WINDOW
    specs, shapes = [], []
    for kind in outs:
        high = {"rows": rows, "parts": WINDOW, "sums": 1}[kind]
        for _ in range(blocks if kind == "parts" else 1):
            specs.append(pl.BlockSpec((high, TILE), lambda t: (0, t)))
            kept = F32 if kind == "sums" else BF16
            shapes.append(jax.ShapeDtypeStruct((high, tiles * TILE), kept))
    if keep:
        specs.append(pl.BlockSpec((rows, depth), lambda t: (0, 0)))
        shapes.append(jax.ShapeDtypeStruct((rows, depth), BF16))

    def kernel(*refs):
        left_refs, right_ref = refs[: len(lefts)], refs[len(lefts)]
        extra_refs = refs[len(lefts) + 1 : -len(specs)]
        out_refs = refs[-len(specs) :]
        weights = right_ref[:, first : first + depth] if nt else right_ref[...]
        at = 0
        for ref in left_refs:
            for row in range(0, ref.shape[0], WINDOW):
                value = dot_t(ref[row : row + WINDOW, :], weights, 1, 1 if nt else 0)
                finish(value, at, extra_refs, out_refs)
                at += WINDOW
        if keep:

            @pl.when(pl.program_id(0) == 0)
            def _():
                at = 0
                for ref in left_refs:
                    out_refs[-1][at : at + ref.shape[0], :] = ref[...]
                    at += ref.shape[0]

    if nt:
        right_spec = pl.BlockSpec((TILE, right.shape[1]), lambda t: (t, 0))
    else:
        right_spec = pl.BlockSpec((depth, TILE), lambda t: (0, t + first))
    return pl.pallas_call(
        kernel,
        grid=(tiles,),
        in_specs=[pl.BlockSpec(v.shape, lambda t: (0, 0)) for v in lefts]
        + [right_spec]
        + [pl.BlockSpec((v.shape[0], TILE), lambda t: (0, t)) for v in extra],
        out_specs=specs,
        out_shape=shapes,
        cost_estimate=QUICK,
    )(*lefts, right, *extra)


def finish_parts(value, at, extra, outs):
    outs[at // WINDOW][...] = value.astype(BF16)


def finish_rows(value, at, extra, outs):
    outs[0][at : at + WINDOW, :] = value.astype(BF16)


def finish_bias(value, at, extra, outs):
    outs[0][at : at + WINDOW, :] = (value + extra[0][...]).astype(BF16)


def finish_gelu(value, at, extra, outs):
    active, slope = gelu_and_slope(value + extra[0][...])
    outs[0][at : at + WINDOW, :] = active.astype(BF16)
    outs[1][at : at + WINDOW, :] = slope.astype(BF16)


def finish_slope(value, at, extra, outs):
    value = (value * extra[0][at : at + WINDOW, :].astype(F32)).astype(BF16)
    outs[0][at : at + WINDOW, :] = value
    total = jnp.sum(value.astype(F32), axis=0, keepdims=True)
    outs[1][...] = total if at == 0 else outs[1][...] + total


def token_products(pairs, plan, first=0, width=None):
    width = width or pairs[0][0].shape[1]

    def kernel(*refs):
        for t, parts in enumerate(plan):

            def run(parts=parts):
                value = None
                for k in parts:
                    term = dot_t(refs[2 * k][...], refs[2 * k + 1][...], 0, 0)
                    value = term if value is None else value + term
                refs[-1][...] = value.astype(BF16)

            if all(p == plan[0] for p in plan):
                if t == 0:
                    run()
            else:
                pl.when(pl.program_id(0) == t)(run)

    specs, arrays = [], []
    for left, right, tile, start, tiles in pairs:
        specs.append(pl.BlockSpec((left.shape[0], width), lambda t: (0, first)))
        specs.append(
            pl.BlockSpec(
                (right.shape[0], TILE),
                lambda t, tile=tile, start=start, tiles=tiles: (
                    0,
                    tile + jnp.clip(t - start, 0, tiles - 1),
                ),
            )
        )
        arrays += [left, right]
    return pl.pallas_call(
        kernel,
        grid=(len(plan),),
        in_specs=specs,
        out_specs=pl.BlockSpec((width, TILE), lambda t: (0, t)),
        out_shape=jax.ShapeDtypeStruct((width, len(plan) * TILE), BF16),
        cost_estimate=QUICK,
    )(*arrays)


def norm_parts(parts, gain, shift):
    rows, width = parts[0].shape
    step = 64

    def kernel(*refs):
        for i in range(len(parts)):
            unit, _ = norm_stats(refs[i][...].astype(F32))
            refs[-1][i] = (unit * refs[-3][...] + refs[-2][...]).astype(BF16)

    vector = pl.BlockSpec((1, width), lambda i: (0, 0))
    return pl.pallas_call(
        kernel,
        grid=(rows // step,),
        in_specs=[pl.BlockSpec((step, width), lambda i: (i, 0))] * len(parts) + [vector] * 2,
        out_specs=pl.BlockSpec((len(parts), step, width), lambda i: (0, i, 0)),
        out_shape=jax.ShapeDtypeStruct((len(parts), rows, width), BF16),
        cost_estimate=QUICK,
    )(*parts, gain[None], shift[None]).reshape(len(parts) * rows, width)


def swap(value, axis, bit):
    return lax.ppermute(value, axis, [(i, i ^ bit) for i in range(lax.axis_size(axis))])


def bits_of(count):
    return [1 << k for k in range(count.bit_length() - 1)]


def doubled(parts, axis):
    for bit in bits_of(lax.axis_size(axis)):
        parts = jnp.concatenate([parts, swap(parts, axis, bit)], axis=0)
    return parts


def in_slot_order(parts):
    count, groups = lax.axis_size("seq"), lax.axis_size("batch")
    own_s, own_b = lax.axis_index("seq"), lax.axis_index("batch")
    order = (slot_owners() ^ own_s)[:, None] + count * (
        jnp.arange(groups, dtype=jnp.int32) ^ own_b
    )
    parts = jnp.take(parts, order.reshape(-1), axis=0)
    return jnp.moveaxis(parts, 0, -2).reshape(*parts.shape[1:-1], -1)


def small_totals(value, flat, after):
    count, groups = lax.axis_size("seq"), lax.axis_size("batch")
    own_s, own_b = lax.axis_index("seq"), lax.axis_index("batch")
    parts = jnp.moveaxis(value.reshape(*value.shape[:-1], count * groups, -1), -2, 0)
    order = owner_slots()[jnp.arange(count, dtype=jnp.int32) ^ own_s] * groups + (
        jnp.arange(groups, dtype=jnp.int32) ^ own_b
    )[:, None]
    parts = jnp.take(parts, order.reshape(-1), axis=0)
    for bit in reversed(bits_of(groups)):
        half = parts.shape[0] // 2
        parts = parts[:half] + swap(parts[half:], "batch", bit)
    piece = parts.shape[1:]
    parts = tie(parts.reshape(count, -1), *after)
    for bit in reversed(bits_of(count)):
        half = parts.shape[0] // 2
        sent = jnp.concatenate([parts[half:].reshape(-1), flat])
        got = swap(sent, "seq", bit)
        at = half * parts.shape[1]
        parts = parts[:half] + got[:at].reshape(half, -1)
        flat = flat + got[at:]
    return parts.reshape(piece), flat


def batch_gather(value, later=None):
    parts = {0: value}
    for bit in reversed(bits_of(lax.axis_size("batch"))):
        passed = {r: later(v) if later and r else v for r, v in parts.items()}
        parts.update({r | bit: swap(v, "batch", bit) for r, v in passed.items()})
    return [parts[r] for r in range(len(parts))]


def batch_scatter(parts, seen=None):
    parts = {r: [v] for r, v in enumerate(parts)}
    added = lambda values: sum(v.astype(F32) for v in values)
    bits = bits_of(len(parts))
    for bit in bits:
        for r in sorted((r for r in parts if r & bit), reverse=True):
            values = parts.pop(r)
            sent = values[0] if len(values) == 1 else total_of(values)
            if seen and bit == bits[-1]:
                seen(sent)
            parts[r ^ bit].append(swap(sent, "batch", bit))
    return added(parts[0])


def total_of(values):
    rows, width = values[0].shape

    def kernel(*refs):
        total = refs[0][...].astype(F32)
        for ref in refs[1:-1]:
            total = total + ref[...].astype(F32)
        refs[-1][...] = total.astype(BF16)

    block = pl.BlockSpec((rows // 2, width), lambda i: (i, 0))
    return pl.pallas_call(
        kernel,
        grid=(2,),
        in_specs=[block] * len(values),
        out_specs=block,
        out_shape=jax.ShapeDtypeStruct((rows, width), BF16),
        cost_estimate=QUICK,
    )(*values)


def move_kernel(order, value, moved):
    width = value.shape[1] // order.shape[0]
    for i in range(order.shape[0]):
        source = pl.multiple_of(order[i] * width, width)
        moved[:, i * width : (i + 1) * width] = value[:, pl.ds(source, width)]


def reorder(value, order):
    rows, columns = value.shape
    width = columns // order.shape[0]
    if width % 128:
        return jnp.take(value.reshape(rows, -1, width), order, axis=1).reshape(value.shape)
    block = pl.BlockSpec((rows // 2, columns), lambda i, *_: (i, 0))
    return pl.pallas_call(
        move_kernel,
        grid_spec=pltpu.PrefetchScalarGridSpec(
            num_scalar_prefetch=1, grid=(2,), in_specs=[block], out_specs=block
        ),
        out_shape=jax.ShapeDtypeStruct(value.shape, value.dtype),
        cost_estimate=QUICK,
    )(order, value)


def norm_stats(values):
    mean = jnp.mean(values, axis=-1, keepdims=True)
    centered = values - mean
    factor = lax.rsqrt(jnp.mean(centered * centered, axis=-1, keepdims=True) + 1e-05)
    return centered * factor, factor


def norm_back(grad, unit, factor, gain):
    scaled = grad * gain
    inner = jnp.mean(scaled * unit, axis=-1, keepdims=True)
    return factor * (scaled - jnp.mean(scaled, axis=-1, keepdims=True) - unit * inner)


def gelu_and_slope(values):
    root, cubic = (2 / jnp.pi) ** 0.5, 0.044715
    square = values * values
    bend = jnp.tanh(values * (root + root * cubic * square))
    half = 0.5 + 0.5 * bend
    slope = half + values * (0.5 - 0.5 * bend * bend) * (root + 3 * root * cubic * square)
    return values * half, slope


def dot_t(left, right, left_dim, right_dim):
    return lax.dot_general(
        left, right, (((left_dim,), (right_dim,)), ((), ())), preferred_element_type=F32
    )


def masks(start, limit):
    row = lax.broadcasted_iota(jnp.int32, (WINDOW, WINDOW), 0)
    col = lax.broadcasted_iota(jnp.int32, (WINDOW, WINDOW), 1)
    own = col <= row
    spot = jnp.where(own, start + col, start - WINDOW + col)
    return own, (spot >= 0) & ((spot < limit) | (row == col))


def weights_of(query, key, early_key, own, live):
    scores = jnp.where(own, dot_t(query, key, 1, 1), dot_t(query, early_key, 1, 1))
    scores = jnp.where(live, scores * (HEAD_DIM**-0.5), -1e30)
    expo = jnp.exp(scores - jnp.max(scores, axis=-1, keepdims=True))
    return expo / jnp.sum(expo, axis=-1, keepdims=True)


def attend_kernel(limits, start, packed, early, mix, mixed, weights, *branch):
    width = mixed.shape[1]
    own, live = masks(start[0], limits[pl.program_id(0)])
    for head, at in enumerate(range(0, width, HEAD_DIM)):
        cols = lambda k: slice(k * width + at, k * width + at + HEAD_DIM)
        probs = weights_of(packed[:, cols(0)], packed[:, cols(1)], early[:, cols(0)], own, live)
        weights[:, head * WINDOW : (head + 1) * WINDOW] = probs.astype(BF16)
        near = jnp.where(own, probs, 0.0).astype(BF16)
        far = jnp.where(own, 0.0, probs).astype(BF16)
        mixed[:, cols(0)] = (
            dot_t(near, packed[:, cols(2)], 1, 0) + dot_t(far, early[:, cols(1)], 1, 0)
        ).astype(BF16)
    out = dot_t(mixed[...], mix[...], 1, 1).astype(BF16)
    for i, part in enumerate(branch):
        @pl.when(pl.program_id(0) == i)
        def _(part=part):
            part[...] = out


def attend_back_kernel(limits, start, packed, early, weights, grad, g_packed, g_early):
    width = grad.shape[1]
    scale = HEAD_DIM**-0.5
    row = lax.broadcasted_iota(jnp.int32, (WINDOW, WINDOW), 0)
    own = lax.broadcasted_iota(jnp.int32, (WINDOW, WINDOW), 1) <= row
    for head, at in enumerate(range(0, width, HEAD_DIM)):
        cols = lambda k: slice(k * width + at, k * width + at + HEAD_DIM)
        query, key, value = (packed[:, cols(k)] for k in range(3))
        early_key, early_value = (early[:, cols(k)] for k in range(2))
        out = grad[:, cols(0)]
        probs = weights[:, head * WINDOW : (head + 1) * WINDOW].astype(F32)
        g_probs = jnp.where(own, dot_t(out, value, 1, 1), dot_t(out, early_value, 1, 1))
        delta = jnp.sum(probs * g_probs, axis=-1, keepdims=True)
        g_scores = probs * (g_probs - delta)
        near = jnp.where(own, probs, 0.0).astype(BF16)
        far = jnp.where(own, 0.0, probs).astype(BF16)
        g_near = jnp.where(own, g_scores, 0.0).astype(BF16)
        g_far = jnp.where(own, 0.0, g_scores).astype(BF16)
        g_packed[:, cols(0)] = (
            (dot_t(g_near, key, 1, 0) + dot_t(g_far, early_key, 1, 0)) * scale
        ).astype(BF16)
        g_packed[:, cols(1)] = (dot_t(g_near, query, 0, 0) * scale).astype(BF16)
        g_packed[:, cols(2)] = dot_t(near, out, 0, 0).astype(BF16)
        g_early[:, cols(0)] = (dot_t(g_far, query, 0, 0) * scale).astype(BF16)
        g_early[:, cols(1)] = dot_t(far, out, 0, 0).astype(BF16)


def per_chain(kernel, limits, start, arrays, widths, shared=(), parts=0):
    rows = arrays[0].shape[0]
    whole = lambda shape: pl.BlockSpec(shape, lambda i, *_: (0, 0))
    block = lambda w: pl.BlockSpec((WINDOW, w), lambda i, *_: (i, 0))
    part = (WINDOW, shared[0].shape[0] if shared else 0)
    return pl.pallas_call(
        kernel,
        grid_spec=pltpu.PrefetchScalarGridSpec(
            num_scalar_prefetch=2,
            grid=(rows // WINDOW,),
            in_specs=[block(a.shape[1]) for a in arrays]
            + [pl.BlockSpec((v.shape[0], TILE), lambda i, *_: (0, 3)) for v in shared],
            out_specs=[block(w) for w in widths] + [whole(part)] * parts,
        ),
        out_shape=[jax.ShapeDtypeStruct((rows, w), BF16) for w in widths]
        + [jax.ShapeDtypeStruct(part, BF16)] * parts,
        cost_estimate=QUICK,
    )(limits, start, *arrays, *shared)


def shards(
    tokens,
    lengths,
    cotangent,
    ln1_gain,
    ln1_bias,
    w_qkv,
    qv_bias,
    w_out,
    out_bias,
    ln2_gain,
    ln2_bias,
    w_fc,
    fc_bias,
    w_proj,
    proj_bias,
):
    groups = lax.axis_size("batch")
    chain = lax.axis_index("batch")
    place = lax.axis_index("seq")
    rows, width = tokens.shape[1:]
    count = lax.axis_size("seq")
    slice_width = width // count
    heads_width = w_out.shape[0]
    assert rows == WINDOW and lengths.shape[1] == 1 and tokens.shape[0] == 1
    start = (place * rows).astype(jnp.int32)
    limits = lengths[:, 0][chain ^ jnp.arange(groups, dtype=jnp.int32)]
    valid = (start + jnp.arange(rows, dtype=jnp.int32) < limits[0]).astype(F32)
    to_slots, from_slots = slot_owners(), owner_slots()
    back_order = from_slots[slot_owners(-1)]

    tokens, cotangent = tokens[0], cotangent[0]
    vectors = jnp.stack([ln1_gain, ln1_bias, out_bias, ln2_gain, ln2_bias, proj_bias])
    vectors = doubled(vectors[None], "seq")
    ring = Ring(vectors)
    vectors = in_slot_order(doubled(vectors, "batch"))
    gain_one, shift_one, mix_shift, gain_two, shift_two, down_shift = (
        vectors[i].astype(F32) for i in range(6)
    )

    qkv_width = 3 * heads_width
    assert heads_width == TILE
    mix_in = jnp.concatenate([w_qkv.reshape(slice_width, qkv_width), w_out.T], axis=1)
    mix_in, up_in, down_in = Gather(mix_in, 0), Gather(w_fc, 0), Gather(w_proj, 1)
    late = {}
    g_down, g_up = (Scatter(lambda j, n=n: (late[n], j, slice_width)) for n in ("down", "up"))

    def find_mix(j):
        for value, lo, wide in late["mix"]:
            if lo <= j * slice_width < lo + wide:
                return value, j - lo // slice_width, slice_width

    g_mix = Scatter(find_mix)
    for moved, more_ahead in (
        (mix_in, True), (up_in, False), (down_in, True), (g_down, False), (g_up, True), (g_mix, False)
    ):
        ring.add(moved, more_ahead)
    more = max(0, count // 2 - 4)

    ring.advance()
    own_tokens = reorder(ring.now(tokens), to_slots)
    next_tokens = reorder(ring.now(tokens), slot_owners(1))
    early_tokens = lax.ppermute(next_tokens, "seq", [(i, i + 1) for i in range(count - 1)])
    parts = batch_gather(tie(own_tokens, vectors))
    ring.advance()
    early_parts = batch_gather(early_tokens)
    grad_out = reorder(ring.now(cotangent), to_slots).astype(F32) * valid[:, None]
    grad_y_own = grad_out.astype(BF16)
    ring.due(grad_y_own)
    ring.advance(1 + more)
    normed = norm_parts(ring.now(*parts), gain_one, shift_one)
    ring.due(normed)
    grad_y = batch_gather(tie(grad_y_own, early_parts[0]))
    ring.advance()
    normed_early = norm_parts(ring.now(*early_parts), gain_one, shift_one)
    ring.due(normed_early)
    mix_in.early(ring)
    ring.advance()
    ring.due(*grad_y)

    mix_in = mix_in.all()
    zeros = jnp.zeros((heads_width,), F32)
    shift = jnp.concatenate([qv_bias[0].astype(F32), zeros, qv_bias[1].astype(F32)])[None]
    (packed,) = matmul(
        [ring.now(normed)], mix_in, finish_bias, ["rows"], tiles=3, extra=[shift]
    )
    (early,) = matmul(
        [ring.now(normed_early)],
        mix_in,
        finish_bias,
        ["rows"],
        first=1,
        tiles=2,
        extra=[shift[:, heads_width:]],
    )
    starts = start.reshape(1)
    ring.due(packed, early)
    ring.advance()
    mixed, weights, *branch = per_chain(
        attend_kernel,
        limits,
        starts,
        (ring.now(packed), early),
        (heads_width, heads_width // HEAD_DIM * WINDOW),
        (mix_in,),
        groups,
    )
    ring.due(*branch)
    ring.advance()
    branch = batch_scatter(ring.now(*branch), ring.due)
    ring.advance(1 + more)
    inputs = own_tokens.astype(F32)
    resid = inputs + branch + mix_shift
    unit_two, factor_two = norm_stats(resid)
    second_own = (unit_two * gain_two + shift_two).astype(BF16)
    up_in = up_in.all()
    ring.due(second_own, up_in)
    ring.advance()
    second = batch_gather(second_own, ring.now)

    active, slope, second = matmul(
        ring.now(*second),
        up_in,
        finish_gelu,
        ["rows", "rows"],
        extra=[fc_bias.astype(F32)[None]],
        keep=True,
    )
    ring.due(active)
    ring.advance(1 + more)
    straight = lambda left, right: token_products(
        [(left, right, 0, 0, right.shape[1] // TILE)], [[0]] * (right.shape[1] // TILE)
    )
    grad_y = jnp.concatenate(grad_y, axis=0)
    late["down"] = straight(grad_y, ring.now(active))
    ring.due(late["down"])
    ring.advance()
    down_in.early(ring)
    ring.advance()
    down_in = down_in.all()
    grad_pre, grad_fc_bias = matmul(
        [ring.now(grad_y)], down_in, finish_slope, ["rows", "sums"], nt=True, extra=[slope]
    )
    ring.due(grad_pre)
    ring.advance()
    parts = matmul([ring.now(grad_pre)], up_in, finish_parts, ["parts"], nt=True)
    ring.due(*parts)
    ring.advance()
    sent = []
    grad_second = batch_scatter(ring.now(*parts), sent.append)
    late["up"] = straight(tie(second, *sent), grad_pre)
    ring.due(late["up"])
    ring.advance()
    grad_second = ring.now(grad_second)
    grad_resid = grad_out + norm_back(grad_second, unit_two, factor_two, gain_two)
    grad_branch_own = grad_resid.astype(BF16)
    result = matmul([tie(active, grad_branch_own)], down_in, finish_parts, ["parts"])
    ring.due(*result)
    ring.advance(1 + more)
    grad_branch = batch_gather(grad_branch_own, ring.now)
    grad_w_proj = g_down.total(ring).T
    ring.due(grad_w_proj)

    grad_mixed, grad_branch = matmul(
        tie(grad_branch, grad_w_proj), mix_in, finish_rows, ["rows"], first=3, tiles=1, keep=True
    )
    ring.due(grad_mixed)
    ring.advance()
    g_packed, g_early = per_chain(
        attend_back_kernel,
        limits,
        starts,
        (packed, early, weights, ring.now(grad_mixed)),
        (qkv_width, 2 * heads_width),
    )
    pairs = [
        (normed, g_packed, 0, 0, 3), (normed_early, g_early, 0, 1, 2), (grad_branch, mixed, 0, 3, 1)
    ]

    def mix_piece(first, wide):
        return token_products(pairs, [[0], [0, 1], [0, 1], [2]], first, wide), first * wide, wide

    late["mix"] = [mix_piece(2, TILE)]
    ring.due(late["mix"][0][0])
    result = batch_scatter(ring.now(*result), ring.due)
    ring.advance()
    back = matmul(
        [ring.now(g_early)], mix_in, finish_parts, ["parts"], nt=True, first=heads_width
    )
    sent = []
    back = batch_scatter(back, sent.append)
    pairs[0] = (tie(normed, *sent), *pairs[0][1:])
    late["mix"].append(mix_piece(1, TILE))
    ring.due(late["mix"][1][0])
    ring.advance()
    grad_own = matmul([ring.now(g_packed)], mix_in, finish_parts, ["parts"], nt=True)
    pairs[0] = (ring.now(normed), *pairs[0][1:])
    late["mix"].append(mix_piece(3, TILE))
    ring.due(late["mix"][2][0], *grad_own)
    ring.advance()
    back = ring.now(back)
    moved = reorder(back.astype(BF16), back_order)
    grad_own = batch_scatter(tie(grad_own, moved), ring.due)
    moved = lax.ppermute(moved, "seq", [(i + 1, i) for i in range(count - 1)])
    pairs[0] = (ring.now(normed), *pairs[0][1:])
    late["mix"].append(mix_piece(0, TILE))
    ring.due(late["mix"][3][0])
    ring.advance()
    result = resid + result + down_shift
    block_out = reorder(ring.now(result).astype(BF16), from_slots)
    while any(ring.queue.values()):
        ring.advance()
    unit_one, factor_one = norm_stats(inputs)
    unit_early, _ = norm_stats(early_tokens.astype(F32))
    grad_normed = grad_own + moved.astype(F32)
    grad_tokens = grad_resid + norm_back(grad_normed, unit_one, factor_one, gain_one)

    column = lambda value: jnp.sum(value.astype(F32), axis=0)
    flat = jnp.concatenate(
        [
            grad_fc_bias[0],
            column(g_packed[:, :heads_width]),
            column(g_packed[:, 2 * heads_width :]) + column(g_early[:, heads_width:]),
        ]
    )
    ff = grad_fc_bias.shape[1]
    sums = jnp.stack(
        [
            jnp.sum(grad_own * unit_one + back * unit_early, axis=0),
            jnp.sum(grad_own + back, axis=0),
            column(grad_branch_own),
            jnp.sum(grad_second * unit_two, axis=0),
            jnp.sum(grad_second, axis=0),
            column(grad_y_own),
        ]
    )
    sums, flat = small_totals(sums, flat, ring.last.values())
    grad_mix_in = g_mix.total(ring)
    return (
        block_out[None],
        reorder(grad_tokens.astype(BF16), from_slots)[None],
        sums[0],
        sums[1],
        grad_mix_in[:, :qkv_width].reshape(slice_width, 3, heads_width),
        flat[ff:].reshape(2, heads_width),
        grad_mix_in[:, qkv_width:].T,
        sums[2],
        sums[3],
        sums[4],
        g_up.total(ring),
        flat[:ff],
        grad_w_proj,
        sums[5],
    )


def solution(mesh):
    everywhere = P(("seq", "batch"))
    rows = P("batch", "seq", None)
    return jax.shard_map(
        shards,
        mesh=mesh,
        in_specs=(
            rows,
            P(),
            rows,
            everywhere,
            everywhere,
            P("seq", None, "batch"),
            P(None, "batch"),
            P("batch", "seq"),
            everywhere,
            everywhere,
            everywhere,
            P("seq", "batch"),
            P("batch"),
            P("batch", "seq"),
            everywhere,
        ),
        out_specs=(
            rows,
            rows,
            everywhere,
            everywhere,
            P("seq", None, "batch"),
            P(None, "batch"),
            P("batch", "seq"),
            everywhere,
            everywhere,
            everywhere,
            P("seq", "batch"),
            P("batch"),
            P("batch", "seq"),
            everywhere,
        ),
        check_vma=False,
    )
```

```python
import jax
import jax.numpy as jnp
from jax import lax
from jax.experimental import pallas as pl
from jax.experimental.pallas import tpu as pltpu
from jax.sharding import PartitionSpec as P

HEAD_DIM = 128
TILE = 512
WINDOW = 256
F32 = jnp.float32
BF16 = jnp.bfloat16


def ring_order(count):
    return list(range(0, count, 2)) + list(range(count - 1, 0, -2))


def ring_place(index, count):
    return jnp.where(index % 2 == 0, index // 2, count - 1 - index // 2)


def ring_index(place, count):
    return jnp.where(place < count // 2, 2 * place, 2 * (count - 1 - place) + 1)


def slot_owners(ahead=0):
    count = lax.axis_size("seq")
    place = ring_place((lax.axis_index("seq") + ahead) % count, count)
    return ring_index((place + jnp.arange(count, dtype=jnp.int32)) % count, count)


def owner_slots():
    count = lax.axis_size("seq")
    place = ring_place(lax.axis_index("seq"), count)
    return (ring_place(jnp.arange(count, dtype=jnp.int32), count) - place) % count


def tie(value, *after):
    after = [v for v in after if v is not None]
    return lax.optimization_barrier((value, *after))[0] if after else value


class Ring:
    def __init__(self, after):
        self.count = lax.axis_size("seq")
        self.queue = {True: [], False: []}
        self.last = {True: after, False: after}
        self.before, self.wanted = [], []

    def hop(self, value, forward):
        order = ring_order(self.count)
        ahead = order[1:] + order[:1]
        pairs = zip(order, ahead) if forward else zip(ahead, order)
        value = tie(value, *self.wanted)
        self.before.append(value)
        self.last[forward] = lax.ppermute(value, "seq", list(pairs))
        return self.last[forward]

    def advance(self, times=1):
        for _ in range(times):
            self.before = []
            self.wanted += self.last.values()
            steps = [(way, *queue.pop(0)) for way, queue in self.queue.items() if queue]
            while steps:
                same = [s for s in steps if s[1] is steps[0][1]]
                moved = same[0][1]
                ways = [(w, j) for w, _, j in same]
                for (way, _, j), value in zip(same, moved.blocks(ways, self.wanted)):
                    moved.landed[way, j] = self.hop(value, way)
                steps = [s for s in steps if s not in same]
            self.wanted = []

    def now(self, *values):
        values = tie(values if len(values) > 1 else values[0], *self.before)
        return values

    def due(self, *values):
        self.wanted += values

    def add(self, moved, more_ahead):
        ahead = self.count // 2 if more_ahead else self.count - 1 - self.count // 2
        for forward, steps in ((True, ahead), (False, self.count - 1 - ahead)):
            self.queue[forward] += [(moved, j) for j in moved.slots(forward, steps)]
        return moved


class Gather:
    def __init__(self, value, axis):
        self.value, self.axis = value, axis
        self.landed, self.count = {}, lax.axis_size("seq")
        self.base = None

    def slots(self, forward, steps):
        return [self.count - 1 - t if forward else 1 + t for t in range(steps)]

    def blocks(self, steps, after):
        return [self.landed.get((w, j + (1 if w else -1)), self.value) for w, j in steps]

    def pieces(self):
        landed = self.landed
        return [self.value] + [
            landed.get((False, j), landed.get((True, j))) for j in range(1, self.count)
        ]

    def early(self, ring):
        pieces = self.pieces()
        pieces[self.count // 2] = self.value
        self.base = jnp.concatenate(pieces, axis=self.axis)
        ring.due(self.base)

    def all(self):
        if self.base is None:
            return jnp.concatenate(self.pieces(), axis=self.axis)
        j = self.count // 2
        last = self.landed[True, j]
        return lax.dynamic_update_slice_in_dim(
            self.base, last, j * last.shape[self.axis], self.axis
        )


class Scatter:
    def __init__(self, find):
        self.find, self.landed, self.count = find, {}, lax.axis_size("seq")

    def slots(self, forward, steps):
        return [steps - t if forward else self.count - steps + t for t in range(steps)]

    def blocks(self, steps, after):
        received = [self.landed.get((w, j + (1 if w else -1))) for w, j in steps]
        received = [v if v is None else tie(v, *after) for v in received]
        return join([self.find(j) for _, j in steps], received)

    def total(self, ring):
        value, at, rows = self.find(0)
        own = ring.now(value)[at * rows : (at + 1) * rows].astype(F32)
        return own + self.landed[True, 1].astype(F32) + (
            self.landed[False, self.count - 1].astype(F32)
        )


QUICK = pl.CostEstimate(flops=10**8, bytes_accessed=0, transcendentals=0)


def join(found, received):
    ways, width = len(found), found[0][0].shape[1]
    rows = found[0][2]
    steps = 2 if rows % 32 == 0 else 1
    step, got = rows // steps, [v for v in received if v is not None]

    def kernel(*refs):
        got_refs = list(refs[ways : ways + len(got)])
        for way in range(ways):
            value = refs[way][...]
            if received[way] is not None:
                value = (value.astype(F32) + got_refs.pop(0)[...].astype(F32)).astype(BF16)
            refs[len(refs) - ways + way][...] = value

    block = pl.BlockSpec((step, width), lambda i: (i, 0))
    return pl.pallas_call(
        kernel,
        grid=(steps,),
        in_specs=[
            pl.BlockSpec((step, width), lambda i, j=j: (j * steps + i, 0)) for _, j, _ in found
        ]
        + [block] * len(got),
        out_specs=[block] * ways,
        out_shape=[jax.ShapeDtypeStruct((rows, width), BF16)] * ways,
        cost_estimate=QUICK,
    )(*(v for v, _, _ in found), *got)


def matmul(lefts, right, finish, outs, nt=False, first=0, tiles=None, extra=(), keep=False):
    depth = lefts[0].shape[1]
    columns = right.shape[0 if nt else 1]
    tiles = tiles or columns // TILE
    blocks = sum(v.shape[0] for v in lefts) // WINDOW
    rows = blocks * WINDOW
    specs, shapes = [], []
    for kind in outs:
        high = {"rows": rows, "parts": WINDOW, "sums": 1}[kind]
        for _ in range(blocks if kind == "parts" else 1):
            specs.append(pl.BlockSpec((high, TILE), lambda t: (0, t)))
            kept = F32 if kind == "sums" else BF16
            shapes.append(jax.ShapeDtypeStruct((high, tiles * TILE), kept))
    if keep:
        specs.append(pl.BlockSpec((rows, depth), lambda t: (0, 0)))
        shapes.append(jax.ShapeDtypeStruct((rows, depth), BF16))

    def kernel(*refs):
        left_refs, right_ref = refs[: len(lefts)], refs[len(lefts)]
        extra_refs = refs[len(lefts) + 1 : -len(specs)]
        out_refs = refs[-len(specs) :]
        weights = right_ref[:, first : first + depth] if nt else right_ref[...]
        at = 0
        for ref in left_refs:
            for row in range(0, ref.shape[0], WINDOW):
                value = dot_t(ref[row : row + WINDOW, :], weights, 1, 1 if nt else 0)
                finish(value, at, extra_refs, out_refs)
                at += WINDOW
        if keep:

            @pl.when(pl.program_id(0) == 0)
            def _():
                at = 0
                for ref in left_refs:
                    out_refs[-1][at : at + ref.shape[0], :] = ref[...]
                    at += ref.shape[0]

    if nt:
        right_spec = pl.BlockSpec((TILE, right.shape[1]), lambda t: (t, 0))
    else:
        right_spec = pl.BlockSpec((depth, TILE), lambda t: (0, t + first))
    return pl.pallas_call(
        kernel,
        grid=(tiles,),
        in_specs=[pl.BlockSpec(v.shape, lambda t: (0, 0)) for v in lefts]
        + [right_spec]
        + [pl.BlockSpec((v.shape[0], TILE), lambda t: (0, t)) for v in extra],
        out_specs=specs,
        out_shape=shapes,
        cost_estimate=QUICK,
    )(*lefts, right, *extra)


def finish_parts(value, at, extra, outs):
    outs[at // WINDOW][...] = value.astype(BF16)


def finish_rows(value, at, extra, outs):
    outs[0][at : at + WINDOW, :] = value.astype(BF16)


def finish_bias(value, at, extra, outs):
    outs[0][at : at + WINDOW, :] = (value + extra[0][...]).astype(BF16)


def finish_gelu(value, at, extra, outs):
    active, slope = gelu_and_slope(value + extra[0][...])
    outs[0][at : at + WINDOW, :] = active.astype(BF16)
    outs[1][at : at + WINDOW, :] = slope.astype(BF16)


def finish_slope(value, at, extra, outs):
    value = (value * extra[0][at : at + WINDOW, :].astype(F32)).astype(BF16)
    outs[0][at : at + WINDOW, :] = value
    total = jnp.sum(value.astype(F32), axis=0, keepdims=True)
    outs[1][...] = total if at == 0 else outs[1][...] + total


def token_products(pairs, plan, first=0, width=None):
    width = width or pairs[0][0].shape[1]

    def kernel(*refs):
        for t, parts in enumerate(plan):

            def run(parts=parts):
                value = None
                for k in parts:
                    term = dot_t(refs[2 * k][...], refs[2 * k + 1][...], 0, 0)
                    value = term if value is None else value + term
                refs[-1][...] = value.astype(BF16)

            if all(p == plan[0] for p in plan):
                if t == 0:
                    run()
            else:
                pl.when(pl.program_id(0) == t)(run)

    specs, arrays = [], []
    for left, right, tile, start, tiles in pairs:
        specs.append(pl.BlockSpec((left.shape[0], width), lambda t: (0, first)))
        specs.append(
            pl.BlockSpec(
                (right.shape[0], TILE),
                lambda t, tile=tile, start=start, tiles=tiles: (
                    0,
                    tile + jnp.clip(t - start, 0, tiles - 1),
                ),
            )
        )
        arrays += [left, right]
    return pl.pallas_call(
        kernel,
        grid=(len(plan),),
        in_specs=specs,
        out_specs=pl.BlockSpec((width, TILE), lambda t: (0, t)),
        out_shape=jax.ShapeDtypeStruct((width, len(plan) * TILE), BF16),
        cost_estimate=QUICK,
    )(*arrays)


def norm_parts(parts, gain, shift):
    rows, width = parts[0].shape
    step = 64

    def kernel(*refs):
        for i in range(len(parts)):
            unit, _ = norm_stats(refs[i][...].astype(F32))
            refs[-1][i] = (unit * refs[-3][...] + refs[-2][...]).astype(BF16)

    vector = pl.BlockSpec((1, width), lambda i: (0, 0))
    return pl.pallas_call(
        kernel,
        grid=(rows // step,),
        in_specs=[pl.BlockSpec((step, width), lambda i: (i, 0))] * len(parts) + [vector] * 2,
        out_specs=pl.BlockSpec((len(parts), step, width), lambda i: (0, i, 0)),
        out_shape=jax.ShapeDtypeStruct((len(parts), rows, width), BF16),
        cost_estimate=QUICK,
    )(*parts, gain[None], shift[None]).reshape(len(parts) * rows, width)


def swap(value, axis, bit):
    return lax.ppermute(value, axis, [(i, i ^ bit) for i in range(lax.axis_size(axis))])


def bits_of(count):
    return [1 << k for k in range(count.bit_length() - 1)]


def doubled(parts, axis):
    for bit in bits_of(lax.axis_size(axis)):
        parts = jnp.concatenate([parts, swap(parts, axis, bit)], axis=0)
    return parts


def in_slot_order(parts):
    count, groups = lax.axis_size("seq"), lax.axis_size("batch")
    own_s, own_b = lax.axis_index("seq"), lax.axis_index("batch")
    order = (slot_owners() ^ own_s)[:, None] + count * (
        jnp.arange(groups, dtype=jnp.int32) ^ own_b
    )
    parts = jnp.take(parts, order.reshape(-1), axis=0)
    return jnp.moveaxis(parts, 0, -2).reshape(*parts.shape[1:-1], -1)


def small_totals(value, flat, after):
    count, groups = lax.axis_size("seq"), lax.axis_size("batch")
    own_s, own_b = lax.axis_index("seq"), lax.axis_index("batch")
    parts = jnp.moveaxis(value.reshape(*value.shape[:-1], count * groups, -1), -2, 0)
    order = owner_slots()[jnp.arange(count, dtype=jnp.int32) ^ own_s] * groups + (
        jnp.arange(groups, dtype=jnp.int32) ^ own_b
    )[:, None]
    parts = jnp.take(parts, order.reshape(-1), axis=0)
    for bit in reversed(bits_of(groups)):
        half = parts.shape[0] // 2
        parts = parts[:half] + swap(parts[half:], "batch", bit)
    piece = parts.shape[1:]
    parts = tie(parts.reshape(count, -1), *after)
    for bit in reversed(bits_of(count)):
        half = parts.shape[0] // 2
        sent = jnp.concatenate([parts[half:].reshape(-1), flat])
        got = swap(sent, "seq", bit)
        at = half * parts.shape[1]
        parts = parts[:half] + got[:at].reshape(half, -1)
        flat = flat + got[at:]
    return parts.reshape(piece), flat


def batch_gather(value, later=None):
    parts = {0: value}
    for bit in reversed(bits_of(lax.axis_size("batch"))):
        passed = {r: later(v) if later and r else v for r, v in parts.items()}
        parts.update({r | bit: swap(v, "batch", bit) for r, v in passed.items()})
    return [parts[r] for r in range(len(parts))]


def batch_scatter(parts, seen=None, apart=False):
    parts = {r: [v] for r, v in enumerate(parts)}
    added = lambda values: sum(v.astype(F32) for v in values)
    bits = bits_of(len(parts))
    for bit in bits:
        for r in sorted((r for r in parts if r & bit), reverse=True):
            values = parts.pop(r)
            sent = values[0] if len(values) == 1 else total_of(values)
            if seen and bit == bits[-1]:
                seen(sent)
            parts[r ^ bit].append(swap(sent, "batch", bit))
    return parts[0] if apart else added(parts[0])


def total_of(values):
    rows, width = values[0].shape

    def kernel(*refs):
        total = refs[0][...].astype(F32)
        for ref in refs[1:-1]:
            total = total + ref[...].astype(F32)
        refs[-1][...] = total.astype(BF16)

    block = pl.BlockSpec((rows // 2, width), lambda i: (i, 0))
    return pl.pallas_call(
        kernel,
        grid=(2,),
        in_specs=[block] * len(values),
        out_specs=block,
        out_shape=jax.ShapeDtypeStruct((rows, width), BF16),
        cost_estimate=QUICK,
    )(*values)


def move_kernel(order, *refs):
    *values, moved = refs
    width = moved.shape[1] // order.shape[0]
    for i in range(order.shape[0]):
        source = pl.ds(pl.multiple_of(order[i] * width, width), width)
        block = values[0][:, source]
        if len(values) > 1:
            block = sum(v[:, source].astype(F32) for v in values).astype(moved.dtype)
        moved[:, i * width : (i + 1) * width] = block


def reorder(value, order):
    values = value if isinstance(value, (list, tuple)) else [value]
    value = values[0]
    rows, columns = value.shape
    width = columns // order.shape[0]
    if width % 128:
        value = value if len(values) == 1 else total_of(values)
        return jnp.take(value.reshape(rows, -1, width), order, axis=1).reshape(value.shape)
    block = pl.BlockSpec((rows // 2, columns), lambda i, *_: (i, 0))
    return pl.pallas_call(
        move_kernel,
        grid_spec=pltpu.PrefetchScalarGridSpec(
            num_scalar_prefetch=1, grid=(2,), in_specs=[block] * len(values), out_specs=block
        ),
        out_shape=jax.ShapeDtypeStruct(value.shape, value.dtype),
        cost_estimate=QUICK,
    )(order, *values)


def norm_stats(values):
    mean = jnp.mean(values, axis=-1, keepdims=True)
    centered = values - mean
    factor = lax.rsqrt(jnp.mean(centered * centered, axis=-1, keepdims=True) + 1e-05)
    return centered * factor, factor


def norm_back(grad, unit, factor, gain):
    scaled = grad * gain
    inner = jnp.mean(scaled * unit, axis=-1, keepdims=True)
    return factor * (scaled - jnp.mean(scaled, axis=-1, keepdims=True) - unit * inner)


def gelu_and_slope(values):
    root, cubic = (2 / jnp.pi) ** 0.5, 0.044715
    square = values * values
    bend = jnp.tanh(values * (root + root * cubic * square))
    half = 0.5 + 0.5 * bend
    slope = half + values * (0.5 - 0.5 * bend * bend) * (root + 3 * root * cubic * square)
    return values * half, slope


def dot_t(left, right, left_dim, right_dim):
    return lax.dot_general(
        left, right, (((left_dim,), (right_dim,)), ((), ())), preferred_element_type=F32
    )


def masks(start, limit):
    row = lax.broadcasted_iota(jnp.int32, (WINDOW, WINDOW), 0)
    col = lax.broadcasted_iota(jnp.int32, (WINDOW, WINDOW), 1)
    own = col <= row
    spot = jnp.where(own, start + col, start - WINDOW + col)
    return own, (spot >= 0) & ((spot < limit) | (row == col))


def weights_of(query, key, early_key, own, live):
    scores = jnp.where(own, dot_t(query, key, 1, 1), dot_t(query, early_key, 1, 1))
    scores = jnp.where(live, scores * (HEAD_DIM**-0.5), -1e30)
    expo = jnp.exp(scores - jnp.max(scores, axis=-1, keepdims=True))
    return expo / jnp.sum(expo, axis=-1, keepdims=True)


def attend_kernel(limits, start, packed, early, mix, mixed, weights, *branch):
    width = mixed.shape[1]
    own, live = masks(start[0], limits[pl.program_id(0)])
    for head, at in enumerate(range(0, width, HEAD_DIM)):
        cols = lambda k: slice(k * width + at, k * width + at + HEAD_DIM)
        probs = weights_of(packed[:, cols(0)], packed[:, cols(1)], early[:, cols(0)], own, live)
        weights[:, head * WINDOW : (head + 1) * WINDOW] = probs.astype(BF16)
        near = jnp.where(own, probs, 0.0).astype(BF16)
        far = jnp.where(own, 0.0, probs).astype(BF16)
        mixed[:, cols(0)] = (
            dot_t(near, packed[:, cols(2)], 1, 0) + dot_t(far, early[:, cols(1)], 1, 0)
        ).astype(BF16)
    out = dot_t(mixed[...], mix[...], 1, 1).astype(BF16)
    for i, part in enumerate(branch):
        @pl.when(pl.program_id(0) == i)
        def _(part=part):
            part[...] = out


def attend_back_kernel(limits, start, packed, early, weights, grad, g_packed, g_early):
    width = grad.shape[1]
    scale = HEAD_DIM**-0.5
    row = lax.broadcasted_iota(jnp.int32, (WINDOW, WINDOW), 0)
    own = lax.broadcasted_iota(jnp.int32, (WINDOW, WINDOW), 1) <= row
    for head, at in enumerate(range(0, width, HEAD_DIM)):
        cols = lambda k: slice(k * width + at, k * width + at + HEAD_DIM)
        query, key, value = (packed[:, cols(k)] for k in range(3))
        early_key, early_value = (early[:, cols(k)] for k in range(2))
        out = grad[:, cols(0)]
        probs = weights[:, head * WINDOW : (head + 1) * WINDOW].astype(F32)
        g_probs = jnp.where(own, dot_t(out, value, 1, 1), dot_t(out, early_value, 1, 1))
        delta = jnp.sum(probs * g_probs, axis=-1, keepdims=True)
        g_scores = probs * (g_probs - delta)
        near = jnp.where(own, probs, 0.0).astype(BF16)
        far = jnp.where(own, 0.0, probs).astype(BF16)
        g_near = jnp.where(own, g_scores, 0.0).astype(BF16)
        g_far = jnp.where(own, 0.0, g_scores).astype(BF16)
        g_packed[:, cols(0)] = (
            (dot_t(g_near, key, 1, 0) + dot_t(g_far, early_key, 1, 0)) * scale
        ).astype(BF16)
        g_packed[:, cols(1)] = (dot_t(g_near, query, 0, 0) * scale).astype(BF16)
        g_packed[:, cols(2)] = dot_t(near, out, 0, 0).astype(BF16)
        g_early[:, cols(0)] = (dot_t(g_far, query, 0, 0) * scale).astype(BF16)
        g_early[:, cols(1)] = dot_t(far, out, 0, 0).astype(BF16)


def per_chain(kernel, limits, start, arrays, widths, shared=(), parts=0):
    rows = arrays[0].shape[0]
    whole = lambda shape: pl.BlockSpec(shape, lambda i, *_: (0, 0))
    block = lambda w: pl.BlockSpec((WINDOW, w), lambda i, *_: (i, 0))
    part = (WINDOW, shared[0].shape[0] if shared else 0)
    return pl.pallas_call(
        kernel,
        grid_spec=pltpu.PrefetchScalarGridSpec(
            num_scalar_prefetch=2,
            grid=(rows // WINDOW,),
            in_specs=[block(a.shape[1]) for a in arrays]
            + [pl.BlockSpec((v.shape[0], TILE), lambda i, *_: (0, 3)) for v in shared],
            out_specs=[block(w) for w in widths] + [whole(part)] * parts,
        ),
        out_shape=[jax.ShapeDtypeStruct((rows, w), BF16) for w in widths]
        + [jax.ShapeDtypeStruct(part, BF16)] * parts,
        cost_estimate=QUICK,
    )(limits, start, *arrays, *shared)


def shards(
    tokens,
    lengths,
    cotangent,
    ln1_gain,
    ln1_bias,
    w_qkv,
    qv_bias,
    w_out,
    out_bias,
    ln2_gain,
    ln2_bias,
    w_fc,
    fc_bias,
    w_proj,
    proj_bias,
):
    groups = lax.axis_size("batch")
    chain = lax.axis_index("batch")
    place = lax.axis_index("seq")
    rows, width = tokens.shape[1:]
    count = lax.axis_size("seq")
    slice_width = width // count
    heads_width = w_out.shape[0]
    assert rows == WINDOW and lengths.shape[1] == 1 and tokens.shape[0] == 1
    start = (place * rows).astype(jnp.int32)
    limits = lengths[:, 0][chain ^ jnp.arange(groups, dtype=jnp.int32)]
    valid = (start + jnp.arange(rows, dtype=jnp.int32) < limits[0]).astype(F32)
    to_slots, from_slots = slot_owners(), owner_slots()
    back_order = from_slots[slot_owners(-1)]

    tokens, cotangent = tokens[0], cotangent[0]
    vectors = jnp.stack([ln1_gain, ln1_bias, out_bias, ln2_gain, ln2_bias, proj_bias])
    vectors = doubled(vectors[None], "seq")
    ring = Ring(vectors)
    vectors = in_slot_order(doubled(vectors, "batch"))
    gain_one, shift_one, mix_shift, gain_two, shift_two, down_shift = (
        vectors[i].astype(F32) for i in range(6)
    )

    qkv_width = 3 * heads_width
    assert heads_width == TILE
    mix_in = jnp.concatenate([w_qkv.reshape(slice_width, qkv_width), w_out.T], axis=1)
    mix_in, up_in, down_in = Gather(mix_in, 0), Gather(w_fc, 0), Gather(w_proj, 1)
    late = {}
    g_down, g_up = (Scatter(lambda j, n=n: (late[n], j, slice_width)) for n in ("down", "up"))

    def find_mix(j):
        for value, lo, wide in late["mix"]:
            if lo <= j * slice_width < lo + wide:
                return value, j - lo // slice_width, slice_width

    g_mix = Scatter(find_mix)
    for moved, more_ahead in (
        (mix_in, True), (up_in, False), (down_in, True), (g_down, False), (g_up, True), (g_mix, False)
    ):
        ring.add(moved, more_ahead)
    more = max(0, count // 2 - 4)

    ring.advance()
    own_tokens = reorder(ring.now(tokens), to_slots)
    next_tokens = reorder(ring.now(tokens), slot_owners(1))
    early_tokens = lax.ppermute(next_tokens, "seq", [(i, i + 1) for i in range(count - 1)])
    parts = batch_gather(tie(own_tokens, vectors))
    ring.advance()
    early_parts = batch_gather(early_tokens)
    grad_out = reorder(ring.now(cotangent), to_slots).astype(F32) * valid[:, None]
    grad_y_own = grad_out.astype(BF16)
    ring.due(grad_y_own)
    ring.advance(1 + more)
    normed = norm_parts(ring.now(*parts), gain_one, shift_one)
    ring.due(normed)
    grad_y = batch_gather(tie(grad_y_own, early_parts[0]))
    ring.advance()
    normed_early = norm_parts(ring.now(*early_parts), gain_one, shift_one)
    ring.due(normed_early)
    mix_in.early(ring)
    ring.advance()
    ring.due(*grad_y)

    mix_in = mix_in.all()
    zeros = jnp.zeros((heads_width,), F32)
    shift = jnp.concatenate([qv_bias[0].astype(F32), zeros, qv_bias[1].astype(F32)])[None]
    (packed,) = matmul(
        [ring.now(normed)], mix_in, finish_bias, ["rows"], tiles=3, extra=[shift]
    )
    (early,) = matmul(
        [ring.now(normed_early)],
        mix_in,
        finish_bias,
        ["rows"],
        first=1,
        tiles=2,
        extra=[shift[:, heads_width:]],
    )
    starts = start.reshape(1)
    ring.due(packed, early)
    ring.advance()
    mixed, weights, *branch = per_chain(
        attend_kernel,
        limits,
        starts,
        (ring.now(packed), early),
        (heads_width, heads_width // HEAD_DIM * WINDOW),
        (mix_in,),
        groups,
    )
    ring.due(*branch)
    ring.advance()
    branch = batch_scatter(ring.now(*branch), ring.due)
    grad_y = jnp.concatenate(grad_y, axis=0)
    ring.due(grad_y)
    ring.advance(1 + more)
    inputs = own_tokens.astype(F32)
    resid = inputs + branch + mix_shift
    unit_two, factor_two = norm_stats(resid)
    second_own = (unit_two * gain_two + shift_two).astype(BF16)
    up_in = up_in.all()
    ring.due(second_own, up_in)
    ring.advance()
    second = batch_gather(second_own, ring.now)

    active, slope, second = matmul(
        ring.now(*second),
        up_in,
        finish_gelu,
        ["rows", "rows"],
        extra=[fc_bias.astype(F32)[None]],
        keep=True,
    )
    ring.due(active)
    ring.advance(1 + more)
    straight = lambda left, right: token_products(
        [(left, right, 0, 0, right.shape[1] // TILE)], [[0]] * (right.shape[1] // TILE)
    )
    late["down"] = straight(grad_y, ring.now(active))
    ring.due(late["down"])
    ring.advance()
    down_in.early(ring)
    ring.advance()
    down_in = down_in.all()
    grad_pre, grad_fc_bias = matmul(
        [ring.now(grad_y)], down_in, finish_slope, ["rows", "sums"], nt=True, extra=[slope]
    )
    ring.due(grad_pre)
    ring.advance()
    parts = matmul([ring.now(grad_pre)], up_in, finish_parts, ["parts"], nt=True)
    ring.due(*parts)
    ring.advance()
    sent = []
    grad_second = batch_scatter(ring.now(*parts), sent.append)
    late["up"] = straight(tie(second, *sent), grad_pre)
    ring.due(late["up"])
    ring.advance()
    grad_second = ring.now(grad_second)
    grad_resid = grad_out + norm_back(grad_second, unit_two, factor_two, gain_two)
    grad_branch_own = grad_resid.astype(BF16)
    result = matmul([tie(active, grad_branch_own)], down_in, finish_parts, ["parts"])
    ring.due(*result)
    ring.advance(1 + more)
    grad_branch = batch_gather(grad_branch_own, ring.now)
    grad_w_proj = g_down.total(ring).T
    ring.due(grad_w_proj)

    grad_mixed, grad_branch = matmul(
        tie(grad_branch, grad_w_proj), mix_in, finish_rows, ["rows"], first=3, tiles=1, keep=True
    )
    ring.due(grad_mixed)
    ring.advance()
    g_packed, g_early = per_chain(
        attend_back_kernel,
        limits,
        starts,
        (packed, early, weights, ring.now(grad_mixed)),
        (qkv_width, 2 * heads_width),
    )
    pairs = [
        (normed, g_packed, 0, 0, 3), (normed_early, g_early, 0, 1, 2), (grad_branch, mixed, 0, 3, 1)
    ]

    def mix_piece(first, wide):
        return token_products(pairs, [[0], [0, 1], [0, 1], [2]], first, wide), first * wide, wide

    late["mix"] = [mix_piece(2, TILE)]
    ring.due(late["mix"][0][0])
    result = batch_scatter(ring.now(*result), ring.due)
    ring.advance()
    back = matmul(
        [ring.now(g_early)], mix_in, finish_parts, ["parts"], nt=True, first=heads_width
    )
    pairs[0] = (tie(normed, back[0]), *pairs[0][1:])
    late["mix"].append(mix_piece(1, TILE))
    ring.due(late["mix"][1][0])
    ring.advance()
    sent = []
    back = batch_scatter(ring.now(*back), sent.append, True)
    grad_own = matmul([tie(g_packed, *sent)], mix_in, finish_parts, ["parts"], nt=True)
    pairs[0] = (tie(normed, grad_own[0]), *pairs[0][1:])
    late["mix"].append(mix_piece(3, TILE))
    ring.due(late["mix"][2][0])
    ring.advance()
    moved = reorder(ring.now(*back), back_order)
    grad_own = batch_scatter(tie(grad_own, moved), ring.due)
    moved = lax.ppermute(moved, "seq", [(i + 1, i) for i in range(count - 1)])
    back = sum(v.astype(F32) for v in back)
    pairs[0] = (ring.now(normed), *pairs[0][1:])
    late["mix"].append(mix_piece(0, TILE))
    ring.due(late["mix"][3][0])
    ring.advance()
    result = resid + result + down_shift
    block_out = reorder(ring.now(result).astype(BF16), from_slots)
    while any(ring.queue.values()):
        ring.advance()
    unit_one, factor_one = norm_stats(inputs)
    unit_early, _ = norm_stats(early_tokens.astype(F32))
    grad_normed = grad_own + moved.astype(F32)
    grad_tokens = grad_resid + norm_back(grad_normed, unit_one, factor_one, gain_one)

    column = lambda value: jnp.sum(value.astype(F32), axis=0)
    flat = jnp.concatenate(
        [
            grad_fc_bias[0],
            column(g_packed[:, :heads_width]),
            column(g_packed[:, 2 * heads_width :]) + column(g_early[:, heads_width:]),
        ]
    )
    ff = grad_fc_bias.shape[1]
    sums = jnp.stack(
        [
            jnp.sum(grad_own * unit_one + back * unit_early, axis=0),
            jnp.sum(grad_own + back, axis=0),
            column(grad_branch_own),
            jnp.sum(grad_second * unit_two, axis=0),
            jnp.sum(grad_second, axis=0),
            column(grad_y_own),
        ]
    )
    grad_tokens = reorder(grad_tokens.astype(BF16), from_slots)
    sums, flat = small_totals(sums, flat, [*ring.last.values(), grad_tokens])
    grad_mix_in = g_mix.total(ring)
    return (
        block_out[None],
        grad_tokens[None],
        sums[0],
        sums[1],
        grad_mix_in[:, :qkv_width].reshape(slice_width, 3, heads_width),
        flat[ff:].reshape(2, heads_width),
        grad_mix_in[:, qkv_width:].T,
        sums[2],
        sums[3],
        sums[4],
        g_up.total(ring),
        flat[:ff],
        grad_w_proj,
        sums[5],
    )


def solution(mesh):
    everywhere = P(("seq", "batch"))
    rows = P("batch", "seq", None)
    return jax.shard_map(
        shards,
        mesh=mesh,
        in_specs=(
            rows,
            P(),
            rows,
            everywhere,
            everywhere,
            P("seq", None, "batch"),
            P(None, "batch"),
            P("batch", "seq"),
            everywhere,
            everywhere,
            everywhere,
            P("seq", "batch"),
            P("batch"),
            P("batch", "seq"),
            everywhere,
        ),
        out_specs=(
            rows,
            rows,
            everywhere,
            everywhere,
            P("seq", None, "batch"),
            P(None, "batch"),
            P("batch", "seq"),
            everywhere,
            everywhere,
            everywhere,
            P("seq", "batch"),
            P("batch"),
            P("batch", "seq"),
            everywhere,
        ),
        check_vma=False,
    )
```

```python
import jax
import jax.numpy as jnp
from jax import lax
from jax.experimental import pallas as pl
from jax.experimental.pallas import tpu as pltpu
from jax.sharding import PartitionSpec as P

HEAD_DIM = 128
TILE = 512
WINDOW = 256
F32 = jnp.float32
BF16 = jnp.bfloat16


def ring_order(count):
    return list(range(0, count, 2)) + list(range(count - 1, 0, -2))


def ring_place(index, count):
    return jnp.where(index % 2 == 0, index // 2, count - 1 - index // 2)


def ring_index(place, count):
    return jnp.where(place < count // 2, 2 * place, 2 * (count - 1 - place) + 1)


def slot_owners(ahead=0):
    count = lax.axis_size("seq")
    place = ring_place((lax.axis_index("seq") + ahead) % count, count)
    return ring_index((place + jnp.arange(count, dtype=jnp.int32)) % count, count)


def owner_slots():
    count = lax.axis_size("seq")
    place = ring_place(lax.axis_index("seq"), count)
    return (ring_place(jnp.arange(count, dtype=jnp.int32), count) - place) % count


def tie(value, *after):
    after = [v for v in after if v is not None]
    return lax.optimization_barrier((value, *after))[0] if after else value


class Ring:
    def __init__(self, after):
        self.count = lax.axis_size("seq")
        self.queue = {True: [], False: []}
        self.last = {True: after, False: after}
        self.before, self.wanted = [], []

    def hop(self, value, forward):
        order = ring_order(self.count)
        ahead = order[1:] + order[:1]
        pairs = zip(order, ahead) if forward else zip(ahead, order)
        value = tie(value, *self.wanted)
        self.before.append(value)
        self.last[forward] = lax.ppermute(value, "seq", list(pairs))
        return self.last[forward]

    def advance(self, times=1):
        for _ in range(times):
            self.before = []
            self.wanted += self.last.values()
            steps = [(way, *queue.pop(0)) for way, queue in self.queue.items() if queue]
            while steps:
                same = [s for s in steps if s[1] is steps[0][1]]
                moved = same[0][1]
                ways = [(w, j) for w, _, j in same]
                for (way, _, j), value in zip(same, moved.blocks(ways, self.wanted)):
                    moved.landed[way, j] = self.hop(value, way)
                steps = [s for s in steps if s not in same]
            self.wanted = []

    def now(self, *values):
        values = tie(values if len(values) > 1 else values[0], *self.before)
        return values

    def due(self, *values):
        self.wanted += values

    def add(self, moved, more_ahead):
        ahead = self.count // 2 if more_ahead else self.count - 1 - self.count // 2
        for forward, steps in ((True, ahead), (False, self.count - 1 - ahead)):
            self.queue[forward] += [(moved, j) for j in moved.slots(forward, steps)]
        return moved


class Gather:
    def __init__(self, value, axis):
        self.value, self.axis = value, axis
        self.landed, self.count = {}, lax.axis_size("seq")
        self.base = None

    def slots(self, forward, steps):
        return [self.count - 1 - t if forward else 1 + t for t in range(steps)]

    def blocks(self, steps, after):
        return [self.landed.get((w, j + (1 if w else -1)), self.value) for w, j in steps]

    def pieces(self):
        landed = self.landed
        return [self.value] + [
            landed.get((False, j), landed.get((True, j))) for j in range(1, self.count)
        ]

    def early(self, ring):
        pieces = self.pieces()
        pieces[self.count // 2] = self.value
        self.base = jnp.concatenate(pieces, axis=self.axis)
        ring.due(self.base)

    def all(self):
        if self.base is None:
            return jnp.concatenate(self.pieces(), axis=self.axis)
        j = self.count // 2
        last = self.landed[True, j]
        return lax.dynamic_update_slice_in_dim(
            self.base, last, j * last.shape[self.axis], self.axis
        )


class Scatter:
    def __init__(self, find):
        self.find, self.landed, self.count = find, {}, lax.axis_size("seq")

    def slots(self, forward, steps):
        return [steps - t if forward else self.count - steps + t for t in range(steps)]

    def blocks(self, steps, after):
        received = [self.landed.get((w, j + (1 if w else -1))) for w, j in steps]
        received = [v if v is None else tie(v, *after) for v in received]
        return join([self.find(j) for _, j in steps], received)

    def total(self, ring):
        value, at, rows = self.find(0)
        own = ring.now(value)[at * rows : (at + 1) * rows].astype(F32)
        return own + self.landed[True, 1].astype(F32) + (
            self.landed[False, self.count - 1].astype(F32)
        )


QUICK = pl.CostEstimate(flops=10**8, bytes_accessed=0, transcendentals=0)


def join(found, received):
    ways, width = len(found), found[0][0].shape[1]
    rows = found[0][2]
    steps = 2 if rows % 32 == 0 else 1
    step, got = rows // steps, [v for v in received if v is not None]

    def kernel(*refs):
        got_refs = list(refs[ways : ways + len(got)])
        for way in range(ways):
            value = refs[way][...]
            if received[way] is not None:
                value = (value.astype(F32) + got_refs.pop(0)[...].astype(F32)).astype(BF16)
            refs[len(refs) - ways + way][...] = value

    block = pl.BlockSpec((step, width), lambda i: (i, 0))
    return pl.pallas_call(
        kernel,
        grid=(steps,),
        in_specs=[
            pl.BlockSpec((step, width), lambda i, j=j: (j * steps + i, 0)) for _, j, _ in found
        ]
        + [block] * len(got),
        out_specs=[block] * ways,
        out_shape=[jax.ShapeDtypeStruct((rows, width), BF16)] * ways,
        cost_estimate=QUICK,
    )(*(v for v, _, _ in found), *got)


def matmul(lefts, right, finish, outs, nt=False, first=0, tiles=None, extra=(), keep=False):
    depth = lefts[0].shape[1]
    columns = right.shape[0 if nt else 1]
    tiles = tiles or columns // TILE
    blocks = sum(v.shape[0] for v in lefts) // WINDOW
    rows = blocks * WINDOW
    specs, shapes = [], []
    for kind in outs:
        high = {"rows": rows, "parts": WINDOW, "sums": 1}[kind]
        for _ in range(blocks if kind == "parts" else 1):
            specs.append(pl.BlockSpec((high, TILE), lambda t: (0, t)))
            kept = F32 if kind == "sums" else BF16
            shapes.append(jax.ShapeDtypeStruct((high, tiles * TILE), kept))
    if keep:
        specs.append(pl.BlockSpec((rows, depth), lambda t: (0, 0)))
        shapes.append(jax.ShapeDtypeStruct((rows, depth), BF16))

    def kernel(*refs):
        left_refs, right_ref = refs[: len(lefts)], refs[len(lefts)]
        extra_refs = refs[len(lefts) + 1 : -len(specs)]
        out_refs = refs[-len(specs) :]
        weights = right_ref[:, first : first + depth] if nt else right_ref[...]
        at = 0
        for ref in left_refs:
            for row in range(0, ref.shape[0], WINDOW):
                value = dot_t(ref[row : row + WINDOW, :], weights, 1, 1 if nt else 0)
                finish(value, at, extra_refs, out_refs)
                at += WINDOW
        if keep:

            @pl.when(pl.program_id(0) == 0)
            def _():
                at = 0
                for ref in left_refs:
                    out_refs[-1][at : at + ref.shape[0], :] = ref[...]
                    at += ref.shape[0]

    if nt:
        right_spec = pl.BlockSpec((TILE, right.shape[1]), lambda t: (t, 0))
    else:
        right_spec = pl.BlockSpec((depth, TILE), lambda t: (0, t + first))
    return pl.pallas_call(
        kernel,
        grid=(tiles,),
        in_specs=[pl.BlockSpec(v.shape, lambda t: (0, 0)) for v in lefts]
        + [right_spec]
        + [pl.BlockSpec((v.shape[0], TILE), lambda t: (0, t)) for v in extra],
        out_specs=specs,
        out_shape=shapes,
        cost_estimate=QUICK,
    )(*lefts, right, *extra)


def finish_parts(value, at, extra, outs):
    outs[at // WINDOW][...] = value.astype(BF16)


def finish_rows(value, at, extra, outs):
    outs[0][at : at + WINDOW, :] = value.astype(BF16)


def finish_bias(value, at, extra, outs):
    outs[0][at : at + WINDOW, :] = (value + extra[0][...]).astype(BF16)


def finish_gelu(value, at, extra, outs):
    active, slope = gelu_and_slope(value + extra[0][...])
    outs[0][at : at + WINDOW, :] = active.astype(BF16)
    outs[1][at : at + WINDOW, :] = slope.astype(BF16)


def finish_slope(value, at, extra, outs):
    value = (value * extra[0][at : at + WINDOW, :].astype(F32)).astype(BF16)
    outs[0][at : at + WINDOW, :] = value
    total = jnp.sum(value.astype(F32), axis=0, keepdims=True)
    outs[1][...] = total if at == 0 else outs[1][...] + total


def token_products(pairs, plan, first=0, width=None):
    width = width or pairs[0][0].shape[1]

    def kernel(*refs):
        for t, parts in enumerate(plan):

            def run(parts=parts):
                value = None
                for k in parts:
                    term = dot_t(refs[2 * k][...], refs[2 * k + 1][...], 0, 0)
                    value = term if value is None else value + term
                refs[-1][...] = value.astype(BF16)

            if all(p == plan[0] for p in plan):
                if t == 0:
                    run()
            else:
                pl.when(pl.program_id(0) == t)(run)

    specs, arrays = [], []
    for left, right, tile, start, tiles in pairs:
        specs.append(pl.BlockSpec((left.shape[0], width), lambda t: (0, first)))
        specs.append(
            pl.BlockSpec(
                (right.shape[0], TILE),
                lambda t, tile=tile, start=start, tiles=tiles: (
                    0,
                    tile + jnp.clip(t - start, 0, tiles - 1),
                ),
            )
        )
        arrays += [left, right]
    return pl.pallas_call(
        kernel,
        grid=(len(plan),),
        in_specs=specs,
        out_specs=pl.BlockSpec((width, TILE), lambda t: (0, t)),
        out_shape=jax.ShapeDtypeStruct((width, len(plan) * TILE), BF16),
        cost_estimate=QUICK,
    )(*arrays)


def norm_parts(parts, gain, shift):
    rows, width = parts[0].shape
    step = 64

    def kernel(*refs):
        for i in range(len(parts)):
            unit, _ = norm_stats(refs[i][...].astype(F32))
            refs[-1][i] = (unit * refs[-3][...] + refs[-2][...]).astype(BF16)

    vector = pl.BlockSpec((1, width), lambda i: (0, 0))
    return pl.pallas_call(
        kernel,
        grid=(rows // step,),
        in_specs=[pl.BlockSpec((step, width), lambda i: (i, 0))] * len(parts) + [vector] * 2,
        out_specs=pl.BlockSpec((len(parts), step, width), lambda i: (0, i, 0)),
        out_shape=jax.ShapeDtypeStruct((len(parts), rows, width), BF16),
        cost_estimate=QUICK,
    )(*parts, gain[None], shift[None]).reshape(len(parts) * rows, width)


def swap(value, axis, bit):
    return lax.ppermute(value, axis, [(i, i ^ bit) for i in range(lax.axis_size(axis))])


def bits_of(count):
    return [1 << k for k in range(count.bit_length() - 1)]


def doubled(parts, axis):
    for bit in bits_of(lax.axis_size(axis)):
        parts = jnp.concatenate([parts, swap(parts, axis, bit)], axis=0)
    return parts


def in_slot_order(parts):
    count, groups = lax.axis_size("seq"), lax.axis_size("batch")
    own_s, own_b = lax.axis_index("seq"), lax.axis_index("batch")
    order = (slot_owners() ^ own_s)[:, None] + count * (
        jnp.arange(groups, dtype=jnp.int32) ^ own_b
    )
    parts = jnp.take(parts, order.reshape(-1), axis=0)
    return jnp.moveaxis(parts, 0, -2).reshape(*parts.shape[1:-1], -1)


def small_totals(value, flat, after):
    count, groups = lax.axis_size("seq"), lax.axis_size("batch")
    own_s, own_b = lax.axis_index("seq"), lax.axis_index("batch")
    parts = jnp.moveaxis(value.reshape(*value.shape[:-1], count * groups, -1), -2, 0)
    order = owner_slots()[jnp.arange(count, dtype=jnp.int32) ^ own_s] * groups + (
        jnp.arange(groups, dtype=jnp.int32) ^ own_b
    )[:, None]
    parts = jnp.take(parts, order.reshape(-1), axis=0)
    for bit in reversed(bits_of(groups)):
        half = parts.shape[0] // 2
        parts = parts[:half] + swap(parts[half:], "batch", bit)
    piece = parts.shape[1:]
    parts = tie(parts.reshape(count, -1), *after)
    for bit in reversed(bits_of(count)):
        half = parts.shape[0] // 2
        sent = jnp.concatenate([parts[half:].reshape(-1), flat])
        got = swap(sent, "seq", bit)
        at = half * parts.shape[1]
        parts = parts[:half] + got[:at].reshape(half, -1)
        flat = flat + got[at:]
    return parts.reshape(piece), flat


def batch_gather(value, later=None):
    parts = {0: value}
    for bit in reversed(bits_of(lax.axis_size("batch"))):
        passed = {r: later(v) if later and r else v for r, v in parts.items()}
        parts.update({r | bit: swap(v, "batch", bit) for r, v in passed.items()})
    return [parts[r] for r in range(len(parts))]


def batch_scatter(parts, seen=None, apart=False):
    parts = {r: [v] for r, v in enumerate(parts)}
    added = lambda values: sum(v.astype(F32) for v in values)
    bits = bits_of(len(parts))
    for bit in bits:
        for r in sorted((r for r in parts if r & bit), reverse=True):
            values = parts.pop(r)
            sent = values[0] if len(values) == 1 else total_of(values)
            if seen and bit == bits[-1]:
                seen(sent)
            parts[r ^ bit].append(swap(sent, "batch", bit))
    return parts[0] if apart else added(parts[0])


def total_of(values):
    rows, width = values[0].shape

    def kernel(*refs):
        total = refs[0][...].astype(F32)
        for ref in refs[1:-1]:
            total = total + ref[...].astype(F32)
        refs[-1][...] = total.astype(BF16)

    block = pl.BlockSpec((rows // 2, width), lambda i: (i, 0))
    return pl.pallas_call(
        kernel,
        grid=(2,),
        in_specs=[block] * len(values),
        out_specs=block,
        out_shape=jax.ShapeDtypeStruct((rows, width), BF16),
        cost_estimate=QUICK,
    )(*values)


def move_kernel(order, *refs):
    *values, moved = refs
    width = moved.shape[1] // order.shape[0]
    for i in range(order.shape[0]):
        source = pl.ds(pl.multiple_of(order[i] * width, width), width)
        block = values[0][:, source]
        if len(values) > 1:
            block = sum(v[:, source].astype(F32) for v in values).astype(moved.dtype)
        moved[:, i * width : (i + 1) * width] = block


def reorder(value, order):
    values = value if isinstance(value, (list, tuple)) else [value]
    value = values[0]
    rows, columns = value.shape
    width = columns // order.shape[0]
    if width % 128:
        value = value if len(values) == 1 else total_of(values)
        return jnp.take(value.reshape(rows, -1, width), order, axis=1).reshape(value.shape)
    block = pl.BlockSpec((rows // 2, columns), lambda i, *_: (i, 0))
    return pl.pallas_call(
        move_kernel,
        grid_spec=pltpu.PrefetchScalarGridSpec(
            num_scalar_prefetch=1, grid=(2,), in_specs=[block] * len(values), out_specs=block
        ),
        out_shape=jax.ShapeDtypeStruct(value.shape, value.dtype),
        cost_estimate=QUICK,
    )(order, *values)


def norm_stats(values):
    mean = jnp.mean(values, axis=-1, keepdims=True)
    centered = values - mean
    factor = lax.rsqrt(jnp.mean(centered * centered, axis=-1, keepdims=True) + 1e-05)
    return centered * factor, factor


def norm_back(grad, unit, factor, gain):
    scaled = grad * gain
    inner = jnp.mean(scaled * unit, axis=-1, keepdims=True)
    return factor * (scaled - jnp.mean(scaled, axis=-1, keepdims=True) - unit * inner)


def gelu_and_slope(values):
    root, cubic = (2 / jnp.pi) ** 0.5, 0.044715
    square = values * values
    bend = jnp.tanh(values * (root + root * cubic * square))
    half = 0.5 + 0.5 * bend
    slope = half + values * (0.5 - 0.5 * bend * bend) * (root + 3 * root * cubic * square)
    return values * half, slope


def dot_t(left, right, left_dim, right_dim):
    return lax.dot_general(
        left, right, (((left_dim,), (right_dim,)), ((), ())), preferred_element_type=F32
    )


def masks(start, limit):
    row = lax.broadcasted_iota(jnp.int32, (WINDOW, WINDOW), 0)
    col = lax.broadcasted_iota(jnp.int32, (WINDOW, WINDOW), 1)
    own = col <= row
    spot = jnp.where(own, start + col, start - WINDOW + col)
    return own, (spot >= 0) & ((spot < limit) | (row == col))


def weights_of(query, key, early_key, own, live):
    scores = jnp.where(own, dot_t(query, key, 1, 1), dot_t(query, early_key, 1, 1))
    scores = jnp.where(live, scores * (HEAD_DIM**-0.5), -1e30)
    expo = jnp.exp(scores - jnp.max(scores, axis=-1, keepdims=True))
    return expo / jnp.sum(expo, axis=-1, keepdims=True)


def attend_kernel(limits, start, packed, early, mix, mixed, weights, *branch):
    width = mixed.shape[1]
    own, live = masks(start[0], limits[pl.program_id(0)])
    for head, at in enumerate(range(0, width, HEAD_DIM)):
        cols = lambda k: slice(k * width + at, k * width + at + HEAD_DIM)
        probs = weights_of(packed[:, cols(0)], packed[:, cols(1)], early[:, cols(0)], own, live)
        weights[:, head * WINDOW : (head + 1) * WINDOW] = probs.astype(BF16)
        near = jnp.where(own, probs, 0.0).astype(BF16)
        far = jnp.where(own, 0.0, probs).astype(BF16)
        mixed[:, cols(0)] = (
            dot_t(near, packed[:, cols(2)], 1, 0) + dot_t(far, early[:, cols(1)], 1, 0)
        ).astype(BF16)
    out = dot_t(mixed[...], mix[...], 1, 1).astype(BF16)
    for i, part in enumerate(branch):
        @pl.when(pl.program_id(0) == i)
        def _(part=part):
            part[...] = out


def attend_back_kernel(limits, start, packed, early, weights, grad, g_packed, g_early):
    width = grad.shape[1]
    scale = HEAD_DIM**-0.5
    row = lax.broadcasted_iota(jnp.int32, (WINDOW, WINDOW), 0)
    own = lax.broadcasted_iota(jnp.int32, (WINDOW, WINDOW), 1) <= row
    for head, at in enumerate(range(0, width, HEAD_DIM)):
        cols = lambda k: slice(k * width + at, k * width + at + HEAD_DIM)
        query, key, value = (packed[:, cols(k)] for k in range(3))
        early_key, early_value = (early[:, cols(k)] for k in range(2))
        out = grad[:, cols(0)]
        probs = weights[:, head * WINDOW : (head + 1) * WINDOW].astype(F32)
        g_probs = jnp.where(own, dot_t(out, value, 1, 1), dot_t(out, early_value, 1, 1))
        delta = jnp.sum(probs * g_probs, axis=-1, keepdims=True)
        g_scores = probs * (g_probs - delta)
        near = jnp.where(own, probs, 0.0).astype(BF16)
        far = jnp.where(own, 0.0, probs).astype(BF16)
        g_near = jnp.where(own, g_scores, 0.0).astype(BF16)
        g_far = jnp.where(own, 0.0, g_scores).astype(BF16)
        g_packed[:, cols(0)] = (
            (dot_t(g_near, key, 1, 0) + dot_t(g_far, early_key, 1, 0)) * scale
        ).astype(BF16)
        g_packed[:, cols(1)] = (dot_t(g_near, query, 0, 0) * scale).astype(BF16)
        g_packed[:, cols(2)] = dot_t(near, out, 0, 0).astype(BF16)
        g_early[:, cols(0)] = (dot_t(g_far, query, 0, 0) * scale).astype(BF16)
        g_early[:, cols(1)] = dot_t(far, out, 0, 0).astype(BF16)


def per_chain(kernel, limits, start, arrays, widths, shared=(), parts=0):
    rows = arrays[0].shape[0]
    whole = lambda shape: pl.BlockSpec(shape, lambda i, *_: (0, 0))
    block = lambda w: pl.BlockSpec((WINDOW, w), lambda i, *_: (i, 0))
    part = (WINDOW, shared[0].shape[0] if shared else 0)
    return pl.pallas_call(
        kernel,
        grid_spec=pltpu.PrefetchScalarGridSpec(
            num_scalar_prefetch=2,
            grid=(rows // WINDOW,),
            in_specs=[block(a.shape[1]) for a in arrays]
            + [pl.BlockSpec((v.shape[0], TILE), lambda i, *_: (0, 3)) for v in shared],
            out_specs=[block(w) for w in widths] + [whole(part)] * parts,
        ),
        out_shape=[jax.ShapeDtypeStruct((rows, w), BF16) for w in widths]
        + [jax.ShapeDtypeStruct(part, BF16)] * parts,
        cost_estimate=QUICK,
    )(limits, start, *arrays, *shared)


def shards(
    tokens,
    lengths,
    cotangent,
    ln1_gain,
    ln1_bias,
    w_qkv,
    qv_bias,
    w_out,
    out_bias,
    ln2_gain,
    ln2_bias,
    w_fc,
    fc_bias,
    w_proj,
    proj_bias,
):
    groups = lax.axis_size("batch")
    chain = lax.axis_index("batch")
    place = lax.axis_index("seq")
    rows, width = tokens.shape[1:]
    count = lax.axis_size("seq")
    slice_width = width // count
    heads_width = w_out.shape[0]
    assert rows == WINDOW and lengths.shape[1] == 1 and tokens.shape[0] == 1
    start = (place * rows).astype(jnp.int32)
    limits = lengths[:, 0][chain ^ jnp.arange(groups, dtype=jnp.int32)]
    valid = (start + jnp.arange(rows, dtype=jnp.int32) < limits[0]).astype(F32)
    to_slots, from_slots = slot_owners(), owner_slots()
    back_order = from_slots[slot_owners(-1)]

    tokens, cotangent = tokens[0], cotangent[0]
    vectors = jnp.stack([ln1_gain, ln1_bias, out_bias, ln2_gain, ln2_bias, proj_bias])
    vectors = doubled(vectors[None], "seq")
    ring = Ring(vectors)
    vectors = in_slot_order(doubled(vectors, "batch"))
    gain_one, shift_one, mix_shift, gain_two, shift_two, down_shift = (
        vectors[i].astype(F32) for i in range(6)
    )

    qkv_width = 3 * heads_width
    assert heads_width == TILE
    mix_in = jnp.concatenate([w_qkv.reshape(slice_width, qkv_width), w_out.T], axis=1)
    mix_in, up_in, down_in = Gather(mix_in, 0), Gather(w_fc, 0), Gather(w_proj, 1)
    late = {}
    g_down, g_up = (Scatter(lambda j, n=n: (late[n], j, slice_width)) for n in ("down", "up"))

    def find_mix(j):
        for value, lo, wide in late["mix"]:
            if lo <= j * slice_width < lo + wide:
                return value, j - lo // slice_width, slice_width

    g_mix = Scatter(find_mix)
    for moved, more_ahead in (
        (mix_in, True), (up_in, False), (down_in, True), (g_down, False), (g_up, True), (g_mix, False)
    ):
        ring.add(moved, more_ahead)
    more = max(0, count // 2 - 4)

    ring.advance()
    own_tokens = reorder(ring.now(tokens), to_slots)
    next_tokens = reorder(ring.now(tokens), slot_owners(1))
    early_tokens = lax.ppermute(next_tokens, "seq", [(i, i + 1) for i in range(count - 1)])
    parts = batch_gather(tie(own_tokens, vectors))
    ring.advance()
    early_parts = batch_gather(early_tokens)
    grad_out = reorder(ring.now(cotangent), to_slots).astype(F32) * valid[:, None]
    grad_y_own = grad_out.astype(BF16)
    ring.due(grad_y_own)
    ring.advance(1 + more)
    normed = norm_parts(ring.now(*parts), gain_one, shift_one)
    ring.due(normed)
    grad_y = batch_gather(tie(grad_y_own, early_parts[0]))
    ring.advance()
    normed_early = norm_parts(ring.now(*early_parts), gain_one, shift_one)
    ring.due(normed_early)
    mix_in.early(ring)
    ring.advance()
    ring.due(*grad_y)

    mix_in = mix_in.all()
    zeros = jnp.zeros((heads_width,), F32)
    shift = jnp.concatenate([qv_bias[0].astype(F32), zeros, qv_bias[1].astype(F32)])[None]
    (packed,) = matmul(
        [ring.now(normed)], mix_in, finish_bias, ["rows"], tiles=3, extra=[shift]
    )
    (early,) = matmul(
        [ring.now(normed_early)],
        mix_in,
        finish_bias,
        ["rows"],
        first=1,
        tiles=2,
        extra=[shift[:, heads_width:]],
    )
    starts = start.reshape(1)
    ring.due(packed, early)
    ring.advance()
    mixed, weights, *branch = per_chain(
        attend_kernel,
        limits,
        starts,
        (ring.now(packed), early),
        (heads_width, heads_width // HEAD_DIM * WINDOW),
        (mix_in,),
        groups,
    )
    ring.due(*branch)
    ring.advance()
    branch = batch_scatter(ring.now(*branch), ring.due)
    grad_y = jnp.concatenate(grad_y, axis=0)
    ring.due(grad_y)
    ring.advance(1 + more)
    inputs = own_tokens.astype(F32)
    resid = inputs + branch + mix_shift
    unit_two, factor_two = norm_stats(resid)
    second_own = (unit_two * gain_two + shift_two).astype(BF16)
    up_in = up_in.all()
    ring.due(second_own, up_in)
    ring.advance()
    second = batch_gather(second_own, ring.now)

    active, slope, second = matmul(
        ring.now(*second),
        up_in,
        finish_gelu,
        ["rows", "rows"],
        extra=[fc_bias.astype(F32)[None]],
        keep=True,
    )
    ring.due(active)
    ring.advance(1 + more)
    straight = lambda left, right: token_products(
        [(left, right, 0, 0, right.shape[1] // TILE)], [[0]] * (right.shape[1] // TILE)
    )
    late["down"] = straight(grad_y, ring.now(active))
    ring.due(late["down"])
    ring.advance()
    down_in.early(ring)
    ring.advance()
    down_in = down_in.all()
    grad_pre, grad_fc_bias = matmul(
        [ring.now(grad_y)], down_in, finish_slope, ["rows", "sums"], nt=True, extra=[slope]
    )
    ring.due(grad_pre)
    ring.advance()
    parts = matmul([ring.now(grad_pre)], up_in, finish_parts, ["parts"], nt=True)
    ring.due(*parts)
    ring.advance()
    sent = []
    grad_second = batch_scatter(ring.now(*parts), sent.append)
    late["up"] = straight(tie(second, *sent), grad_pre)
    ring.due(late["up"])
    ring.advance()
    grad_second = ring.now(grad_second)
    grad_resid = grad_out + norm_back(grad_second, unit_two, factor_two, gain_two)
    grad_branch_own = grad_resid.astype(BF16)
    result = matmul([tie(active, grad_branch_own)], down_in, finish_parts, ["parts"])
    ring.due(*result)
    ring.advance(1 + more)
    grad_branch = batch_gather(grad_branch_own, ring.now)
    grad_w_proj = g_down.total(ring).T
    ring.due(grad_w_proj)

    grad_mixed, grad_branch = matmul(
        tie(grad_branch, grad_w_proj), mix_in, finish_rows, ["rows"], first=3, tiles=1, keep=True
    )
    ring.due(grad_mixed)
    ring.advance()
    g_packed, g_early = per_chain(
        attend_back_kernel,
        limits,
        starts,
        (packed, early, weights, ring.now(grad_mixed)),
        (qkv_width, 2 * heads_width),
    )
    pairs = [
        (normed, g_packed, 0, 0, 3), (normed_early, g_early, 0, 1, 2), (grad_branch, mixed, 0, 3, 1)
    ]

    def mix_piece(first, wide):
        return token_products(pairs, [[0], [0, 1], [0, 1], [2]], first, wide), first * wide, wide

    late["mix"] = [mix_piece(2, TILE)]
    ring.due(late["mix"][0][0])
    result = batch_scatter(ring.now(*result), ring.due)
    ring.advance()
    back = matmul(
        [ring.now(g_early)], mix_in, finish_parts, ["parts"], nt=True, first=heads_width
    )
    pairs[0] = (tie(normed, back[0]), *pairs[0][1:])
    late["mix"].append(mix_piece(1, TILE))
    ring.due(late["mix"][1][0])
    ring.advance()
    sent = []
    back = batch_scatter(ring.now(*back), sent.append, True)
    grad_own = matmul([tie(g_packed, *sent)], mix_in, finish_parts, ["parts"], nt=True)
    pairs[0] = (tie(normed, grad_own[0]), *pairs[0][1:])
    late["mix"].append(mix_piece(3, TILE))
    result = resid + result + down_shift
    ring.due(late["mix"][2][0], result)
    ring.advance()
    moved = reorder(ring.now(*back), back_order)
    grad_own = batch_scatter(ring.now(*grad_own), ring.due)
    moved = lax.ppermute(moved, "seq", [(i + 1, i) for i in range(count - 1)])
    back = sum(v.astype(F32) for v in back)
    pairs[0] = (ring.now(normed), *pairs[0][1:])
    late["mix"].append(mix_piece(0, TILE))
    ring.due(late["mix"][3][0])
    ring.advance()
    block_out = reorder(ring.now(result).astype(BF16), from_slots)
    while any(ring.queue.values()):
        ring.advance()
    unit_one, factor_one = norm_stats(inputs)
    unit_early, _ = norm_stats(early_tokens.astype(F32))
    grad_normed = grad_own + moved.astype(F32)
    grad_tokens = grad_resid + norm_back(grad_normed, unit_one, factor_one, gain_one)

    column = lambda value: jnp.sum(value.astype(F32), axis=0)
    flat = jnp.concatenate(
        [
            grad_fc_bias[0],
            column(g_packed[:, :heads_width]),
            column(g_packed[:, 2 * heads_width :]) + column(g_early[:, heads_width:]),
        ]
    )
    ff = grad_fc_bias.shape[1]
    sums = jnp.stack(
        [
            jnp.sum(grad_own * unit_one + back * unit_early, axis=0),
            jnp.sum(grad_own + back, axis=0),
            column(grad_branch_own),
            jnp.sum(grad_second * unit_two, axis=0),
            jnp.sum(grad_second, axis=0),
            column(grad_y_own),
        ]
    )
    grad_tokens = reorder(grad_tokens.astype(BF16), from_slots)
    grad_w_fc = g_up.total(ring)
    after = [*ring.last.values(), grad_tokens, block_out, grad_w_fc]
    sums, flat = small_totals(sums, flat, after)
    grad_mix_in = g_mix.total(ring)
    return (
        block_out[None],
        grad_tokens[None],
        sums[0],
        sums[1],
        grad_mix_in[:, :qkv_width].reshape(slice_width, 3, heads_width),
        flat[ff:].reshape(2, heads_width),
        grad_mix_in[:, qkv_width:].T,
        sums[2],
        sums[3],
        sums[4],
        grad_w_fc,
        flat[:ff],
        grad_w_proj,
        sums[5],
    )


def solution(mesh):
    everywhere = P(("seq", "batch"))
    rows = P("batch", "seq", None)
    return jax.shard_map(
        shards,
        mesh=mesh,
        in_specs=(
            rows,
            P(),
            rows,
            everywhere,
            everywhere,
            P("seq", None, "batch"),
            P(None, "batch"),
            P("batch", "seq"),
            everywhere,
            everywhere,
            everywhere,
            P("seq", "batch"),
            P("batch"),
            P("batch", "seq"),
            everywhere,
        ),
        out_specs=(
            rows,
            rows,
            everywhere,
            everywhere,
            P("seq", None, "batch"),
            P(None, "batch"),
            P("batch", "seq"),
            everywhere,
            everywhere,
            everywhere,
            P("seq", "batch"),
            P("batch"),
            P("batch", "seq"),
            everywhere,
        ),
        check_vma=False,
    )
```

```python
import jax
import jax.numpy as jnp
from jax import lax
from jax.experimental import pallas as pl
from jax.experimental.pallas import tpu as pltpu
from jax.sharding import PartitionSpec as P

HEAD_DIM = 128
TILE = 512
WINDOW = 256
F32 = jnp.float32
BF16 = jnp.bfloat16


def ring_order(count):
    return list(range(0, count, 2)) + list(range(count - 1, 0, -2))


def ring_place(index, count):
    return jnp.where(index % 2 == 0, index // 2, count - 1 - index // 2)


def ring_index(place, count):
    return jnp.where(place < count // 2, 2 * place, 2 * (count - 1 - place) + 1)


def slot_owners(ahead=0):
    count = lax.axis_size("seq")
    place = ring_place((lax.axis_index("seq") + ahead) % count, count)
    return ring_index((place + jnp.arange(count, dtype=jnp.int32)) % count, count)


def owner_slots():
    count = lax.axis_size("seq")
    place = ring_place(lax.axis_index("seq"), count)
    return (ring_place(jnp.arange(count, dtype=jnp.int32), count) - place) % count


def tie(value, *after):
    after = [v for v in after if v is not None]
    return lax.optimization_barrier((value, *after))[0] if after else value


class Ring:
    def __init__(self, after):
        self.count = lax.axis_size("seq")
        self.queue = {True: [], False: []}
        self.last = {True: after, False: after}
        self.before, self.wanted = [], []

    def hop(self, value, forward):
        order = ring_order(self.count)
        ahead = order[1:] + order[:1]
        pairs = zip(order, ahead) if forward else zip(ahead, order)
        value = tie(value, *self.wanted)
        self.before.append(value)
        self.last[forward] = lax.ppermute(value, "seq", list(pairs))
        return self.last[forward]

    def advance(self, times=1):
        for _ in range(times):
            self.before = []
            self.wanted += self.last.values()
            steps = [(way, *queue.pop(0)) for way, queue in self.queue.items() if queue]
            while steps:
                same = [s for s in steps if s[1] is steps[0][1]]
                moved = same[0][1]
                ways = [(w, j) for w, _, j in same]
                for (way, _, j), value in zip(same, moved.blocks(ways, self.wanted)):
                    moved.landed[way, j] = self.hop(value, way)
                steps = [s for s in steps if s not in same]
            self.wanted = []

    def now(self, *values):
        values = tie(values if len(values) > 1 else values[0], *self.before)
        return values

    def due(self, *values):
        self.wanted += values

    def add(self, moved, more_ahead):
        ahead = self.count // 2 if more_ahead else self.count - 1 - self.count // 2
        for forward, steps in ((True, ahead), (False, self.count - 1 - ahead)):
            self.queue[forward] += [(moved, j) for j in moved.slots(forward, steps)]
        return moved


class Gather:
    def __init__(self, value, axis):
        self.value, self.axis = value, axis
        self.landed, self.count = {}, lax.axis_size("seq")
        self.base = None

    def slots(self, forward, steps):
        return [self.count - 1 - t if forward else 1 + t for t in range(steps)]

    def blocks(self, steps, after):
        return [self.landed.get((w, j + (1 if w else -1)), self.value) for w, j in steps]

    def pieces(self):
        landed = self.landed
        return [self.value] + [
            landed.get((False, j), landed.get((True, j))) for j in range(1, self.count)
        ]

    def early(self, ring):
        pieces = self.pieces()
        pieces[self.count // 2] = self.value
        self.base = jnp.concatenate(pieces, axis=self.axis)
        ring.due(self.base)

    def all(self):
        if self.base is None:
            return jnp.concatenate(self.pieces(), axis=self.axis)
        j = self.count // 2
        last = self.landed[True, j]
        return lax.dynamic_update_slice_in_dim(
            self.base, last, j * last.shape[self.axis], self.axis
        )


class Scatter:
    def __init__(self, find):
        self.find, self.landed, self.count = find, {}, lax.axis_size("seq")

    def slots(self, forward, steps):
        return [steps - t if forward else self.count - steps + t for t in range(steps)]

    def blocks(self, steps, after):
        received = [self.landed.get((w, j + (1 if w else -1))) for w, j in steps]
        received = [v if v is None else tie(v, *after) for v in received]
        return join([self.find(j) for _, j in steps], received)

    def ends(self, ring):
        value, at, rows = self.find(0)
        return ring.now(value), at, rows, self.landed[True, 1], self.landed[False, self.count - 1]

    def total(self, ring):
        value, at, rows = self.find(0)
        own = ring.now(value)[at * rows : (at + 1) * rows].astype(F32)
        return own + self.landed[True, 1].astype(F32) + (
            self.landed[False, self.count - 1].astype(F32)
        )


QUICK = pl.CostEstimate(flops=10**8, bytes_accessed=0, transcendentals=0)


def flipped_total(value, at, rows, *received):
    def kernel(own, ahead, behind, out):
        total = own[...].astype(F32) + ahead[...].astype(F32) + behind[...].astype(F32)
        out[...] = total.T

    block = pl.BlockSpec((rows, TILE), lambda t: (0, t))
    return pl.pallas_call(
        kernel,
        grid=(value.shape[1] // TILE,),
        in_specs=[pl.BlockSpec((rows, TILE), lambda t: (at, t)), block, block],
        out_specs=pl.BlockSpec((TILE, rows), lambda t: (t, 0)),
        out_shape=jax.ShapeDtypeStruct((value.shape[1], rows), F32),
        cost_estimate=QUICK,
    )(value, *received)


def mixed_total(value, at, rows, *received):
    def kernel(own, ahead, behind, straight, flipped):
        total = own[...].astype(F32) + ahead[...].astype(F32) + behind[...].astype(F32)

        @pl.when(pl.program_id(0) < 3)
        def _():
            straight[0] = total

        @pl.when(pl.program_id(0) == 3)
        def _():
            flipped[...] = total.T

    block = pl.BlockSpec((rows, TILE), lambda t: (0, t))
    return pl.pallas_call(
        kernel,
        grid=(4,),
        in_specs=[pl.BlockSpec((rows, TILE), lambda t: (at, t)), block, block],
        out_specs=[
            pl.BlockSpec((1, rows, TILE), lambda t: (jnp.minimum(t, 2), 0, 0)),
            pl.BlockSpec((TILE, rows), lambda t: (0, 0)),
        ],
        out_shape=[
            jax.ShapeDtypeStruct((3, rows, TILE), F32),
            jax.ShapeDtypeStruct((TILE, rows), F32),
        ],
        cost_estimate=QUICK,
    )(value, *received)


def join(found, received):
    ways, width = len(found), found[0][0].shape[1]
    rows = found[0][2]
    steps = 2 if rows % 32 == 0 else 1
    step, got = rows // steps, [v for v in received if v is not None]

    def kernel(*refs):
        got_refs = list(refs[ways : ways + len(got)])
        for way in range(ways):
            value = refs[way][...]
            if received[way] is not None:
                value = (value.astype(F32) + got_refs.pop(0)[...].astype(F32)).astype(BF16)
            refs[len(refs) - ways + way][...] = value

    block = pl.BlockSpec((step, width), lambda i: (i, 0))
    return pl.pallas_call(
        kernel,
        grid=(steps,),
        in_specs=[
            pl.BlockSpec((step, width), lambda i, j=j: (j * steps + i, 0)) for _, j, _ in found
        ]
        + [block] * len(got),
        out_specs=[block] * ways,
        out_shape=[jax.ShapeDtypeStruct((rows, width), BF16)] * ways,
        cost_estimate=QUICK,
    )(*(v for v, _, _ in found), *got)


def matmul(lefts, right, finish, outs, nt=False, first=0, tiles=None, extra=(), keep=False):
    depth = lefts[0].shape[1]
    columns = right.shape[0 if nt else 1]
    tiles = tiles or columns // TILE
    blocks = sum(v.shape[0] for v in lefts) // WINDOW
    rows = blocks * WINDOW
    specs, shapes = [], []
    for kind in outs:
        high = {"rows": rows, "parts": WINDOW, "sums": 1}[kind]
        for _ in range(blocks if kind == "parts" else 1):
            specs.append(pl.BlockSpec((high, TILE), lambda t: (0, t)))
            kept = F32 if kind == "sums" else BF16
            shapes.append(jax.ShapeDtypeStruct((high, tiles * TILE), kept))
    if keep:
        specs.append(pl.BlockSpec((rows, depth), lambda t: (0, 0)))
        shapes.append(jax.ShapeDtypeStruct((rows, depth), BF16))

    def kernel(*refs):
        left_refs, right_ref = refs[: len(lefts)], refs[len(lefts)]
        extra_refs = refs[len(lefts) + 1 : -len(specs)]
        out_refs = refs[-len(specs) :]
        weights = right_ref[:, first : first + depth] if nt else right_ref[...]
        at = 0
        for ref in left_refs:
            for row in range(0, ref.shape[0], WINDOW):
                value = dot_t(ref[row : row + WINDOW, :], weights, 1, 1 if nt else 0)
                finish(value, at, extra_refs, out_refs)
                at += WINDOW
        if keep:

            @pl.when(pl.program_id(0) == 0)
            def _():
                at = 0
                for ref in left_refs:
                    out_refs[-1][at : at + ref.shape[0], :] = ref[...]
                    at += ref.shape[0]

    if nt:
        right_spec = pl.BlockSpec((TILE, right.shape[1]), lambda t: (t, 0))
    else:
        right_spec = pl.BlockSpec((depth, TILE), lambda t: (0, t + first))
    return pl.pallas_call(
        kernel,
        grid=(tiles,),
        in_specs=[pl.BlockSpec(v.shape, lambda t: (0, 0)) for v in lefts]
        + [right_spec]
        + [pl.BlockSpec((v.shape[0], TILE), lambda t: (0, t)) for v in extra],
        out_specs=specs,
        out_shape=shapes,
        cost_estimate=QUICK,
    )(*lefts, right, *extra)


def finish_parts(value, at, extra, outs):
    outs[at // WINDOW][...] = value.astype(BF16)


def finish_rows(value, at, extra, outs):
    outs[0][at : at + WINDOW, :] = value.astype(BF16)


def finish_bias(value, at, extra, outs):
    outs[0][at : at + WINDOW, :] = (value + extra[0][...]).astype(BF16)


def finish_gelu(value, at, extra, outs):
    active, slope = gelu_and_slope(value + extra[0][...])
    outs[0][at : at + WINDOW, :] = active.astype(BF16)
    outs[1][at : at + WINDOW, :] = slope.astype(BF16)


def finish_slope(value, at, extra, outs):
    value = (value * extra[0][at : at + WINDOW, :].astype(F32)).astype(BF16)
    outs[0][at : at + WINDOW, :] = value
    total = jnp.sum(value.astype(F32), axis=0, keepdims=True)
    outs[1][...] = total if at == 0 else outs[1][...] + total


def token_products(pairs, plan, first=0, width=None):
    width = width or pairs[0][0].shape[1]

    def kernel(*refs):
        at = 0
        while at < len(plan):
            parts, end = plan[at], at + 1
            while end < len(plan) and plan[end] == parts:
                end += 1

            def run(parts=parts):
                value = None
                for k in parts:
                    term = dot_t(refs[2 * k][...], refs[2 * k + 1][...], 0, 0)
                    value = term if value is None else value + term
                refs[-1][...] = value.astype(BF16)

            if end - at == len(plan):
                run()
            else:
                tile = pl.program_id(0)
                pl.when((tile >= at) & (tile < end))(run)
            at = end

    specs, arrays = [], []
    for left, right, tile, start, tiles in pairs:
        specs.append(pl.BlockSpec((left.shape[0], width), lambda t: (0, first)))
        specs.append(
            pl.BlockSpec(
                (right.shape[0], TILE),
                lambda t, tile=tile, start=start, tiles=tiles: (
                    0,
                    tile + jnp.clip(t - start, 0, tiles - 1),
                ),
            )
        )
        arrays += [left, right]
    return pl.pallas_call(
        kernel,
        grid=(len(plan),),
        in_specs=specs,
        out_specs=pl.BlockSpec((width, TILE), lambda t: (0, t)),
        out_shape=jax.ShapeDtypeStruct((width, len(plan) * TILE), BF16),
        cost_estimate=QUICK,
    )(*arrays)


def norm_parts(parts, gain, shift):
    rows, width = parts[0].shape
    step = 64

    def kernel(*refs):
        for i in range(len(parts)):
            unit, _ = norm_stats(refs[i][...].astype(F32))
            refs[-1][i] = (unit * refs[-3][...] + refs[-2][...]).astype(BF16)

    vector = pl.BlockSpec((1, width), lambda i: (0, 0))
    return pl.pallas_call(
        kernel,
        grid=(rows // step,),
        in_specs=[pl.BlockSpec((step, width), lambda i: (i, 0))] * len(parts) + [vector] * 2,
        out_specs=pl.BlockSpec((len(parts), step, width), lambda i: (0, i, 0)),
        out_shape=jax.ShapeDtypeStruct((len(parts), rows, width), BF16),
        cost_estimate=QUICK,
    )(*parts, gain[None], shift[None]).reshape(len(parts) * rows, width)


def swap(value, axis, bit):
    return lax.ppermute(value, axis, [(i, i ^ bit) for i in range(lax.axis_size(axis))])


def bits_of(count):
    return [1 << k for k in range(count.bit_length() - 1)]


def doubled(parts, axis):
    for bit in bits_of(lax.axis_size(axis)):
        parts = jnp.concatenate([parts, swap(parts, axis, bit)], axis=0)
    return parts


def in_slot_order(parts):
    count, groups = lax.axis_size("seq"), lax.axis_size("batch")
    own_s, own_b = lax.axis_index("seq"), lax.axis_index("batch")
    order = (slot_owners() ^ own_s)[:, None] + count * (
        jnp.arange(groups, dtype=jnp.int32) ^ own_b
    )
    parts = jnp.take(parts, order.reshape(-1), axis=0)
    return jnp.moveaxis(parts, 0, -2).reshape(*parts.shape[1:-1], -1)


def small_totals(value, flat, after, beside):
    count, groups = lax.axis_size("seq"), lax.axis_size("batch")
    own_s, own_b = lax.axis_index("seq"), lax.axis_index("batch")
    parts = jnp.moveaxis(value.reshape(*value.shape[:-1], count * groups, -1), -2, 0)
    order = owner_slots()[jnp.arange(count, dtype=jnp.int32) ^ own_s] * groups + (
        jnp.arange(groups, dtype=jnp.int32) ^ own_b
    )[:, None]
    parts = jnp.take(parts, order.reshape(-1), axis=0)
    for bit in reversed(bits_of(groups)):
        half = parts.shape[0] // 2
        parts = parts[:half] + swap(parts[half:], "batch", bit)
    piece = parts.shape[1:]
    parts = tie(parts.reshape(count, -1), *after)
    for bit in reversed(bits_of(count)):
        half = parts.shape[0] // 2
        sent = jnp.concatenate([parts[half:].reshape(-1), flat])
        if bit == 1:
            sent = tie(sent, *beside)
        got = swap(sent, "seq", bit)
        at = half * parts.shape[1]
        parts = parts[:half] + got[:at].reshape(half, -1)
        flat = flat + got[at:]
    return parts.reshape(piece), flat


def batch_gather(value, later=None):
    parts = {0: value}
    for bit in reversed(bits_of(lax.axis_size("batch"))):
        passed = {r: later(v) if later and r else v for r, v in parts.items()}
        parts.update({r | bit: swap(v, "batch", bit) for r, v in passed.items()})
    return [parts[r] for r in range(len(parts))]


def batch_scatter(parts, seen=None, apart=False):
    parts = {r: [v] for r, v in enumerate(parts)}
    added = lambda values: sum(v.astype(F32) for v in values)
    bits = bits_of(len(parts))
    for bit in bits:
        for r in sorted((r for r in parts if r & bit), reverse=True):
            values = parts.pop(r)
            sent = values[0] if len(values) == 1 else total_of(values)
            if seen and bit == bits[-1]:
                seen(sent)
            parts[r ^ bit].append(swap(sent, "batch", bit))
    return parts[0] if apart else added(parts[0])


def total_of(values):
    rows, width = values[0].shape

    def kernel(*refs):
        total = refs[0][...].astype(F32)
        for ref in refs[1:-1]:
            total = total + ref[...].astype(F32)
        refs[-1][...] = total.astype(BF16)

    block = pl.BlockSpec((rows // 2, width), lambda i: (i, 0))
    return pl.pallas_call(
        kernel,
        grid=(2,),
        in_specs=[block] * len(values),
        out_specs=block,
        out_shape=jax.ShapeDtypeStruct((rows, width), BF16),
        cost_estimate=QUICK,
    )(*values)


def move_kernel(order, *refs):
    *values, moved = refs
    width = moved.shape[1] // order.shape[0]
    for i in range(order.shape[0]):
        source = pl.ds(pl.multiple_of(order[i] * width, width), width)
        block = values[0][:, source]
        if len(values) > 1:
            block = sum(v[:, source].astype(F32) for v in values).astype(moved.dtype)
        moved[:, i * width : (i + 1) * width] = block


def reorder(value, order):
    values = value if isinstance(value, (list, tuple)) else [value]
    value = values[0]
    rows, columns = value.shape
    width = columns // order.shape[0]
    if width % 128:
        value = value if len(values) == 1 else total_of(values)
        return jnp.take(value.reshape(rows, -1, width), order, axis=1).reshape(value.shape)
    block = pl.BlockSpec((rows // 2, columns), lambda i, *_: (i, 0))
    return pl.pallas_call(
        move_kernel,
        grid_spec=pltpu.PrefetchScalarGridSpec(
            num_scalar_prefetch=1, grid=(2,), in_specs=[block] * len(values), out_specs=block
        ),
        out_shape=jax.ShapeDtypeStruct(value.shape, value.dtype),
        cost_estimate=QUICK,
    )(order, *values)


def norm_stats(values):
    mean = jnp.mean(values, axis=-1, keepdims=True)
    centered = values - mean
    factor = lax.rsqrt(jnp.mean(centered * centered, axis=-1, keepdims=True) + 1e-05)
    return centered * factor, factor


def norm_back(grad, unit, factor, gain):
    scaled = grad * gain
    inner = jnp.mean(scaled * unit, axis=-1, keepdims=True)
    return factor * (scaled - jnp.mean(scaled, axis=-1, keepdims=True) - unit * inner)


def gelu_and_slope(values):
    root, cubic = (2 / jnp.pi) ** 0.5, 0.044715
    square = values * values
    bend = jnp.tanh(values * (root + root * cubic * square))
    half = 0.5 + 0.5 * bend
    slope = half + values * (0.5 - 0.5 * bend * bend) * (root + 3 * root * cubic * square)
    return values * half, slope


def dot_t(left, right, left_dim, right_dim):
    return lax.dot_general(
        left, right, (((left_dim,), (right_dim,)), ((), ())), preferred_element_type=F32
    )


def masks(start, limit):
    row = lax.broadcasted_iota(jnp.int32, (WINDOW, WINDOW), 0)
    col = lax.broadcasted_iota(jnp.int32, (WINDOW, WINDOW), 1)
    own = col <= row
    spot = jnp.where(own, start + col, start - WINDOW + col)
    return own, (spot >= 0) & ((spot < limit) | (row == col))


def weights_of(query, key, early_key, own, live):
    scores = jnp.where(own, dot_t(query, key, 1, 1), dot_t(query, early_key, 1, 1))
    scores = jnp.where(live, scores * (HEAD_DIM**-0.5), -1e30)
    expo = jnp.exp(scores - jnp.max(scores, axis=-1, keepdims=True))
    return expo / jnp.sum(expo, axis=-1, keepdims=True)


def attend_kernel(limits, start, packed, early, mix, mixed, weights, *branch):
    width = mixed.shape[1]
    own, live = masks(start[0], limits[pl.program_id(0)])
    for head, at in enumerate(range(0, width, HEAD_DIM)):
        cols = lambda k: slice(k * width + at, k * width + at + HEAD_DIM)
        probs = weights_of(packed[:, cols(0)], packed[:, cols(1)], early[:, cols(0)], own, live)
        weights[:, head * WINDOW : (head + 1) * WINDOW] = probs.astype(BF16)
        near = jnp.where(own, probs, 0.0).astype(BF16)
        far = jnp.where(own, 0.0, probs).astype(BF16)
        mixed[:, cols(0)] = (
            dot_t(near, packed[:, cols(2)], 1, 0) + dot_t(far, early[:, cols(1)], 1, 0)
        ).astype(BF16)
    out = dot_t(mixed[...], mix[...], 1, 1).astype(BF16)
    for i, part in enumerate(branch):
        @pl.when(pl.program_id(0) == i)
        def _(part=part):
            part[...] = out


def attend_back_kernel(limits, start, packed, early, weights, grad, g_packed, g_early):
    width = grad.shape[1]
    scale = HEAD_DIM**-0.5
    row = lax.broadcasted_iota(jnp.int32, (WINDOW, WINDOW), 0)
    own = lax.broadcasted_iota(jnp.int32, (WINDOW, WINDOW), 1) <= row
    for head, at in enumerate(range(0, width, HEAD_DIM)):
        cols = lambda k: slice(k * width + at, k * width + at + HEAD_DIM)
        query, key, value = (packed[:, cols(k)] for k in range(3))
        early_key, early_value = (early[:, cols(k)] for k in range(2))
        out = grad[:, cols(0)]
        probs = weights[:, head * WINDOW : (head + 1) * WINDOW].astype(F32)
        g_probs = jnp.where(own, dot_t(out, value, 1, 1), dot_t(out, early_value, 1, 1))
        delta = jnp.sum(probs * g_probs, axis=-1, keepdims=True)
        g_scores = probs * (g_probs - delta)
        near = jnp.where(own, probs, 0.0).astype(BF16)
        far = jnp.where(own, 0.0, probs).astype(BF16)
        g_near = jnp.where(own, g_scores, 0.0).astype(BF16)
        g_far = jnp.where(own, 0.0, g_scores).astype(BF16)
        g_packed[:, cols(0)] = (
            (dot_t(g_near, key, 1, 0) + dot_t(g_far, early_key, 1, 0)) * scale
        ).astype(BF16)
        g_packed[:, cols(1)] = (dot_t(g_near, query, 0, 0) * scale).astype(BF16)
        g_packed[:, cols(2)] = dot_t(near, out, 0, 0).astype(BF16)
        g_early[:, cols(0)] = (dot_t(g_far, query, 0, 0) * scale).astype(BF16)
        g_early[:, cols(1)] = dot_t(far, out, 0, 0).astype(BF16)


def per_chain(kernel, limits, start, arrays, widths, shared=(), parts=0):
    rows = arrays[0].shape[0]
    whole = lambda shape: pl.BlockSpec(shape, lambda i, *_: (0, 0))
    block = lambda w: pl.BlockSpec((WINDOW, w), lambda i, *_: (i, 0))
    part = (WINDOW, shared[0].shape[0] if shared else 0)
    return pl.pallas_call(
        kernel,
        grid_spec=pltpu.PrefetchScalarGridSpec(
            num_scalar_prefetch=2,
            grid=(rows // WINDOW,),
            in_specs=[block(a.shape[1]) for a in arrays]
            + [pl.BlockSpec((v.shape[0], TILE), lambda i, *_: (0, 3)) for v in shared],
            out_specs=[block(w) for w in widths] + [whole(part)] * parts,
        ),
        out_shape=[jax.ShapeDtypeStruct((rows, w), BF16) for w in widths]
        + [jax.ShapeDtypeStruct(part, BF16)] * parts,
        cost_estimate=QUICK,
    )(limits, start, *arrays, *shared)


def shards(
    tokens,
    lengths,
    cotangent,
    ln1_gain,
    ln1_bias,
    w_qkv,
    qv_bias,
    w_out,
    out_bias,
    ln2_gain,
    ln2_bias,
    w_fc,
    fc_bias,
    w_proj,
    proj_bias,
):
    groups = lax.axis_size("batch")
    chain = lax.axis_index("batch")
    place = lax.axis_index("seq")
    rows, width = tokens.shape[1:]
    count = lax.axis_size("seq")
    slice_width = width // count
    heads_width = w_out.shape[0]
    assert rows == WINDOW and lengths.shape[1] == 1 and tokens.shape[0] == 1
    start = (place * rows).astype(jnp.int32)
    limits = lengths[:, 0][chain ^ jnp.arange(groups, dtype=jnp.int32)]
    valid = (start + jnp.arange(rows, dtype=jnp.int32) < limits[0]).astype(F32)
    to_slots, from_slots = slot_owners(), owner_slots()
    back_order = from_slots[slot_owners(-1)]

    tokens, cotangent = tokens[0], cotangent[0]
    vectors = jnp.stack([ln1_gain, ln1_bias, out_bias, ln2_gain, ln2_bias, proj_bias])
    vectors = doubled(vectors[None], "seq")
    ring = Ring(vectors)
    vectors = in_slot_order(doubled(vectors, "batch"))
    gain_one, shift_one, mix_shift, gain_two, shift_two, down_shift = (
        vectors[i].astype(F32) for i in range(6)
    )

    qkv_width = 3 * heads_width
    assert heads_width == TILE
    mix_in = jnp.concatenate([w_qkv.reshape(slice_width, qkv_width), w_out.T], axis=1)
    mix_in, up_in, down_in = Gather(mix_in, 0), Gather(w_fc, 0), Gather(w_proj, 1)
    late = {}
    g_down, g_up = (Scatter(lambda j, n=n: (late[n], j, slice_width)) for n in ("down", "up"))

    def find_mix(j):
        for value, lo, wide in late["mix"]:
            if lo <= j * slice_width < lo + wide:
                return value, j - lo // slice_width, slice_width

    g_mix = Scatter(find_mix)
    for moved, more_ahead in (
        (mix_in, True), (up_in, False), (down_in, True), (g_down, False), (g_up, True), (g_mix, False)
    ):
        ring.add(moved, more_ahead)
    more = max(0, count // 2 - 4)

    ring.advance()
    own_tokens = reorder(ring.now(tokens), to_slots)
    next_tokens = reorder(ring.now(tokens), slot_owners(1))
    early_tokens = lax.ppermute(next_tokens, "seq", [(i, i + 1) for i in range(count - 1)])
    parts = batch_gather(tie(own_tokens, vectors))
    ring.advance()
    early_parts = batch_gather(early_tokens)
    grad_out = reorder(ring.now(cotangent), to_slots).astype(F32) * valid[:, None]
    grad_y_own = grad_out.astype(BF16)
    ring.due(grad_y_own)
    ring.advance(1 + more)
    normed = norm_parts(ring.now(*parts), gain_one, shift_one)
    ring.due(normed)
    grad_y = batch_gather(tie(grad_y_own, early_parts[0]))
    ring.advance()
    normed_early = norm_parts(ring.now(*early_parts), gain_one, shift_one)
    ring.due(normed_early)
    mix_in.early(ring)
    ring.advance()
    ring.due(*grad_y)

    mix_in = mix_in.all()
    zeros = jnp.zeros((heads_width,), F32)
    shift = jnp.concatenate([qv_bias[0].astype(F32), zeros, qv_bias[1].astype(F32)])[None]
    (packed,) = matmul(
        [ring.now(normed)], mix_in, finish_bias, ["rows"], tiles=3, extra=[shift]
    )
    (early,) = matmul(
        [ring.now(normed_early)],
        mix_in,
        finish_bias,
        ["rows"],
        first=1,
        tiles=2,
        extra=[shift[:, heads_width:]],
    )
    starts = start.reshape(1)
    ring.due(packed, early)
    ring.advance()
    mixed, weights, *branch = per_chain(
        attend_kernel,
        limits,
        starts,
        (ring.now(packed), early),
        (heads_width, heads_width // HEAD_DIM * WINDOW),
        (mix_in,),
        groups,
    )
    ring.due(*branch)
    ring.advance()
    branch = batch_scatter(ring.now(*branch), ring.due)
    grad_y = jnp.concatenate(grad_y, axis=0)
    ring.due(grad_y)
    ring.advance(1 + more)
    inputs = own_tokens.astype(F32)
    resid = inputs + branch + mix_shift
    unit_two, factor_two = norm_stats(resid)
    second_own = (unit_two * gain_two + shift_two).astype(BF16)
    up_in = up_in.all()
    ring.due(second_own, up_in)
    ring.advance()
    second = batch_gather(second_own, ring.now)

    active, slope, second = matmul(
        ring.now(*second),
        up_in,
        finish_gelu,
        ["rows", "rows"],
        extra=[fc_bias.astype(F32)[None]],
        keep=True,
    )
    ring.due(active)
    ring.advance(1 + more)
    straight = lambda left, right: token_products(
        [(left, right, 0, 0, right.shape[1] // TILE)], [[0]] * (right.shape[1] // TILE)
    )
    late["down"] = straight(grad_y, ring.now(active))
    ring.due(late["down"])
    ring.advance()
    down_in.early(ring)
    ring.advance()
    down_in = down_in.all()
    grad_pre, grad_fc_bias = matmul(
        [ring.now(grad_y)], down_in, finish_slope, ["rows", "sums"], nt=True, extra=[slope]
    )
    ring.due(grad_pre)
    ring.advance()
    parts = matmul([ring.now(grad_pre)], up_in, finish_parts, ["parts"], nt=True)
    ring.due(*parts)
    ring.advance()
    sent = []
    grad_second = batch_scatter(ring.now(*parts), sent.append)
    late["up"] = straight(tie(second, *sent), grad_pre)
    ring.due(late["up"])
    ring.advance()
    grad_second = ring.now(grad_second)
    grad_resid = grad_out + norm_back(grad_second, unit_two, factor_two, gain_two)
    grad_branch_own = grad_resid.astype(BF16)
    result = matmul([tie(active, grad_branch_own)], down_in, finish_parts, ["parts"])
    ring.due(*result)
    ring.advance(1 + more)
    grad_branch = batch_gather(grad_branch_own, ring.now)
    grad_w_proj = flipped_total(*g_down.ends(ring))
    ring.due(grad_w_proj)

    grad_mixed, grad_branch = matmul(
        tie(grad_branch, grad_w_proj), mix_in, finish_rows, ["rows"], first=3, tiles=1, keep=True
    )
    ring.due(grad_mixed)
    ring.advance()
    g_packed, g_early = per_chain(
        attend_back_kernel,
        limits,
        starts,
        (packed, early, weights, ring.now(grad_mixed)),
        (qkv_width, 2 * heads_width),
    )
    pairs = [
        (normed, g_packed, 0, 0, 3), (normed_early, g_early, 0, 1, 2), (grad_branch, mixed, 0, 3, 1)
    ]

    def mix_piece(first, wide):
        return token_products(pairs, [[0], [0, 1], [0, 1], [2]], first, wide), first * wide, wide

    late["mix"] = [mix_piece(2, TILE)]
    ring.due(late["mix"][0][0])
    result = batch_scatter(ring.now(*result), ring.due)
    ring.advance()
    back = matmul(
        [ring.now(g_early)], mix_in, finish_parts, ["parts"], nt=True, first=heads_width
    )
    pairs[0] = (tie(normed, back[0]), *pairs[0][1:])
    late["mix"].append(mix_piece(1, TILE))
    result = resid + result + down_shift
    ring.due(late["mix"][1][0], result)
    ring.advance()
    sent = []
    back = batch_scatter(ring.now(*back), sent.append, True)
    grad_own = matmul([tie(g_packed, *sent)], mix_in, finish_parts, ["parts"], nt=True)
    pairs[0] = (tie(normed, grad_own[0]), *pairs[0][1:])
    late["mix"].append(mix_piece(3, TILE))
    ring.due(late["mix"][2][0])
    ring.advance()
    moved = reorder(ring.now(*back), back_order)
    grad_own = batch_scatter(ring.now(*grad_own), ring.due)
    moved = lax.ppermute(moved, "seq", [(i + 1, i) for i in range(count - 1)])
    back = sum(v.astype(F32) for v in back)
    pairs[0] = (ring.now(normed), *pairs[0][1:])
    late["mix"].append(mix_piece(0, TILE))
    ring.due(late["mix"][3][0])
    ring.advance()
    block_out = reorder(ring.now(result).astype(BF16), from_slots)
    while any(ring.queue.values()):
        ring.advance()
    unit_one, factor_one = norm_stats(inputs)
    unit_early, _ = norm_stats(early_tokens.astype(F32))
    grad_normed = grad_own + moved.astype(F32)
    grad_tokens = grad_resid + norm_back(grad_normed, unit_one, factor_one, gain_one)

    column = lambda value: jnp.sum(value.astype(F32), axis=0)
    flat = jnp.concatenate(
        [
            grad_fc_bias[0],
            column(g_packed[:, :heads_width]),
            column(g_packed[:, 2 * heads_width :]) + column(g_early[:, heads_width:]),
        ]
    )
    ff = grad_fc_bias.shape[1]
    sums = jnp.stack(
        [
            jnp.sum(grad_own * unit_one + back * unit_early, axis=0),
            jnp.sum(grad_own + back, axis=0),
            column(grad_branch_own),
            jnp.sum(grad_second * unit_two, axis=0),
            jnp.sum(grad_second, axis=0),
            column(grad_y_own),
        ]
    )
    grad_tokens = reorder(grad_tokens.astype(BF16), from_slots)
    grad_w_fc = g_up.total(ring)
    after = [*ring.last.values(), grad_tokens, block_out, grad_w_fc]
    grad_w_qkv, grad_w_out = mixed_total(*g_mix.ends(ring))
    sums, flat = small_totals(sums, flat, after, [grad_w_qkv, grad_w_out])
    return (
        block_out[None],
        grad_tokens[None],
        sums[0],
        sums[1],
        grad_w_qkv.transpose(1, 0, 2),
        flat[ff:].reshape(2, heads_width),
        grad_w_out,
        sums[2],
        sums[3],
        sums[4],
        grad_w_fc,
        flat[:ff],
        grad_w_proj,
        sums[5],
    )


def solution(mesh):
    everywhere = P(("seq", "batch"))
    rows = P("batch", "seq", None)
    return jax.shard_map(
        shards,
        mesh=mesh,
        in_specs=(
            rows,
            P(),
            rows,
            everywhere,
            everywhere,
            P("seq", None, "batch"),
            P(None, "batch"),
            P("batch", "seq"),
            everywhere,
            everywhere,
            everywhere,
            P("seq", "batch"),
            P("batch"),
            P("batch", "seq"),
            everywhere,
        ),
        out_specs=(
            rows,
            rows,
            everywhere,
            everywhere,
            P("seq", None, "batch"),
            P(None, "batch"),
            P("batch", "seq"),
            everywhere,
            everywhere,
            everywhere,
            P("seq", "batch"),
            P("batch"),
            P("batch", "seq"),
            everywhere,
        ),
        check_vma=False,
    )
```

```python
import jax
import jax.numpy as jnp
from jax import lax
from jax.experimental import pallas as pl
from jax.experimental.pallas import tpu as pltpu
from jax.sharding import PartitionSpec as P

HEAD_DIM = 128
TILE = 512
WINDOW = 256
F32 = jnp.float32
BF16 = jnp.bfloat16


def ring_order(count):
    return list(range(0, count, 2)) + list(range(count - 1, 0, -2))


def ring_place(index, count):
    return jnp.where(index % 2 == 0, index // 2, count - 1 - index // 2)


def ring_index(place, count):
    return jnp.where(place < count // 2, 2 * place, 2 * (count - 1 - place) + 1)


def slot_owners(ahead=0):
    count = lax.axis_size("seq")
    place = ring_place((lax.axis_index("seq") + ahead) % count, count)
    return ring_index((place + jnp.arange(count, dtype=jnp.int32)) % count, count)


def owner_slots():
    count = lax.axis_size("seq")
    place = ring_place(lax.axis_index("seq"), count)
    return (ring_place(jnp.arange(count, dtype=jnp.int32), count) - place) % count


def tie(value, *after):
    after = [v for v in after if v is not None]
    return lax.optimization_barrier((value, *after))[0] if after else value


class Ring:
    def __init__(self, after):
        self.count = lax.axis_size("seq")
        self.queue = {True: [], False: []}
        self.last = {True: after, False: after}
        self.before, self.wanted = [], []

    def hop(self, value, forward):
        order = ring_order(self.count)
        ahead = order[1:] + order[:1]
        pairs = zip(order, ahead) if forward else zip(ahead, order)
        value = tie(value, *self.wanted)
        self.before.append(value)
        self.last[forward] = lax.ppermute(value, "seq", list(pairs))
        return self.last[forward]

    def advance(self, times=1):
        for _ in range(times):
            self.before = []
            self.wanted += self.last.values()
            steps = [(way, *queue.pop(0)) for way, queue in self.queue.items() if queue]
            while steps:
                same = [s for s in steps if s[1] is steps[0][1]]
                moved = same[0][1]
                ways = [(w, j) for w, _, j in same]
                for (way, _, j), value in zip(same, moved.blocks(ways, self.wanted)):
                    moved.landed[way, j] = self.hop(value, way)
                steps = [s for s in steps if s not in same]
            self.wanted = []

    def now(self, *values):
        values = tie(values if len(values) > 1 else values[0], *self.before)
        return values

    def due(self, *values):
        self.wanted += values

    def add(self, moved, more_ahead):
        ahead = self.count // 2 if more_ahead else self.count - 1 - self.count // 2
        for forward, steps in ((True, ahead), (False, self.count - 1 - ahead)):
            self.queue[forward] += [(moved, j) for j in moved.slots(forward, steps)]
        return moved


class Gather:
    def __init__(self, value, axis):
        self.value, self.axis = value, axis
        self.landed, self.count = {}, lax.axis_size("seq")
        self.base = None

    def slots(self, forward, steps):
        return [self.count - 1 - t if forward else 1 + t for t in range(steps)]

    def blocks(self, steps, after):
        return [self.landed.get((w, j + (1 if w else -1)), self.value) for w, j in steps]

    def pieces(self):
        landed = self.landed
        return [self.value] + [
            landed.get((False, j), landed.get((True, j))) for j in range(1, self.count)
        ]

    def early(self, ring):
        pieces = self.pieces()
        pieces[self.count // 2] = self.value
        self.base = jnp.concatenate(pieces, axis=self.axis)
        ring.due(self.base)

    def all(self):
        if self.base is None:
            return jnp.concatenate(self.pieces(), axis=self.axis)
        j = self.count // 2
        last = self.landed[True, j]
        return lax.dynamic_update_slice_in_dim(
            self.base, last, j * last.shape[self.axis], self.axis
        )


class Scatter:
    def __init__(self, find):
        self.find, self.landed, self.count = find, {}, lax.axis_size("seq")

    def slots(self, forward, steps):
        return [steps - t if forward else self.count - steps + t for t in range(steps)]

    def blocks(self, steps, after):
        received = [self.landed.get((w, j + (1 if w else -1))) for w, j in steps]
        received = [v if v is None else tie(v, *after) for v in received]
        return join([self.find(j) for _, j in steps], received)

    def ends(self, ring):
        value, at, rows = self.find(0)
        return ring.now(value), at, rows, self.landed[True, 1], self.landed[False, self.count - 1]

    def total(self, ring):
        value, at, rows = self.find(0)
        own = ring.now(value)[at * rows : (at + 1) * rows].astype(F32)
        return own + self.landed[True, 1].astype(F32) + (
            self.landed[False, self.count - 1].astype(F32)
        )


QUICK = pl.CostEstimate(flops=10**8, bytes_accessed=0, transcendentals=0)


def flipped_total(value, at, rows, *received):
    def kernel(own, ahead, behind, out):
        total = own[...].astype(F32) + ahead[...].astype(F32) + behind[...].astype(F32)
        out[...] = total.T

    block = pl.BlockSpec((rows, TILE), lambda t: (0, t))
    return pl.pallas_call(
        kernel,
        grid=(value.shape[1] // TILE,),
        in_specs=[pl.BlockSpec((rows, TILE), lambda t: (at, t)), block, block],
        out_specs=pl.BlockSpec((TILE, rows), lambda t: (t, 0)),
        out_shape=jax.ShapeDtypeStruct((value.shape[1], rows), F32),
        cost_estimate=QUICK,
    )(value, *received)


def mixed_total(value, at, rows, *received):
    def kernel(own, ahead, behind, straight, flipped):
        total = own[...].astype(F32) + ahead[...].astype(F32) + behind[...].astype(F32)

        @pl.when(pl.program_id(0) < 3)
        def _():
            straight[0] = total

        @pl.when(pl.program_id(0) == 3)
        def _():
            flipped[...] = total.T

    block = pl.BlockSpec((rows, TILE), lambda t: (0, t))
    return pl.pallas_call(
        kernel,
        grid=(4,),
        in_specs=[pl.BlockSpec((rows, TILE), lambda t: (at, t)), block, block],
        out_specs=[
            pl.BlockSpec((1, rows, TILE), lambda t: (jnp.minimum(t, 2), 0, 0)),
            pl.BlockSpec((TILE, rows), lambda t: (0, 0)),
        ],
        out_shape=[
            jax.ShapeDtypeStruct((3, rows, TILE), F32),
            jax.ShapeDtypeStruct((TILE, rows), F32),
        ],
        cost_estimate=QUICK,
    )(value, *received)


def join(found, received):
    ways, width = len(found), found[0][0].shape[1]
    rows = found[0][2]
    steps = 2 if rows % 32 == 0 else 1
    step, got = rows // steps, [v for v in received if v is not None]

    def kernel(*refs):
        got_refs = list(refs[ways : ways + len(got)])
        for way in range(ways):
            value = refs[way][...]
            if received[way] is not None:
                value = (value.astype(F32) + got_refs.pop(0)[...].astype(F32)).astype(BF16)
            refs[len(refs) - ways + way][...] = value

    block = pl.BlockSpec((step, width), lambda i: (i, 0))
    return pl.pallas_call(
        kernel,
        grid=(steps,),
        in_specs=[
            pl.BlockSpec((step, width), lambda i, j=j: (j * steps + i, 0)) for _, j, _ in found
        ]
        + [block] * len(got),
        out_specs=[block] * ways,
        out_shape=[jax.ShapeDtypeStruct((rows, width), BF16)] * ways,
        cost_estimate=QUICK,
    )(*(v for v, _, _ in found), *got)


def matmul(lefts, right, finish, outs, nt=False, first=0, tiles=None, extra=(), keep=False):
    depth = lefts[0].shape[1]
    columns = right.shape[0 if nt else 1]
    tiles = tiles or columns // TILE
    blocks = sum(v.shape[0] for v in lefts) // WINDOW
    rows = blocks * WINDOW
    specs, shapes = [], []
    for kind in outs:
        high = {"rows": rows, "parts": WINDOW, "sums": 1}[kind]
        for _ in range(blocks if kind == "parts" else 1):
            specs.append(pl.BlockSpec((high, TILE), lambda t: (0, t)))
            kept = F32 if kind == "sums" else BF16
            shapes.append(jax.ShapeDtypeStruct((high, tiles * TILE), kept))
    if keep:
        specs.append(pl.BlockSpec((rows, depth), lambda t: (0, 0)))
        shapes.append(jax.ShapeDtypeStruct((rows, depth), BF16))

    def kernel(*refs):
        left_refs, right_ref = refs[: len(lefts)], refs[len(lefts)]
        extra_refs = refs[len(lefts) + 1 : -len(specs)]
        out_refs = refs[-len(specs) :]
        weights = right_ref[:, first : first + depth] if nt else right_ref[...]
        at = 0
        for ref in left_refs:
            for row in range(0, ref.shape[0], WINDOW):
                value = dot_t(ref[row : row + WINDOW, :], weights, 1, 1 if nt else 0)
                finish(value, at, extra_refs, out_refs)
                at += WINDOW
        if keep:

            @pl.when(pl.program_id(0) == 0)
            def _():
                at = 0
                for ref in left_refs:
                    out_refs[-1][at : at + ref.shape[0], :] = ref[...]
                    at += ref.shape[0]

    if nt:
        right_spec = pl.BlockSpec((TILE, right.shape[1]), lambda t: (t, 0))
    else:
        right_spec = pl.BlockSpec((depth, TILE), lambda t: (0, t + first))
    return pl.pallas_call(
        kernel,
        grid=(tiles,),
        in_specs=[pl.BlockSpec(v.shape, lambda t: (0, 0)) for v in lefts]
        + [right_spec]
        + [pl.BlockSpec((v.shape[0], TILE), lambda t: (0, t)) for v in extra],
        out_specs=specs,
        out_shape=shapes,
        cost_estimate=QUICK,
    )(*lefts, right, *extra)


def finish_parts(value, at, extra, outs):
    outs[at // WINDOW][...] = value.astype(BF16)


def finish_rows(value, at, extra, outs):
    outs[0][at : at + WINDOW, :] = value.astype(BF16)


def finish_bias(value, at, extra, outs):
    outs[0][at : at + WINDOW, :] = (value + extra[0][...]).astype(BF16)


def finish_gelu(value, at, extra, outs):
    active, slope = gelu_and_slope(value + extra[0][...])
    outs[0][at : at + WINDOW, :] = active.astype(BF16)
    outs[1][at : at + WINDOW, :] = slope.astype(BF16)


def finish_slope(value, at, extra, outs):
    value = (value * extra[0][at : at + WINDOW, :].astype(F32)).astype(BF16)
    outs[0][at : at + WINDOW, :] = value
    total = jnp.sum(value.astype(F32), axis=0, keepdims=True)
    outs[1][...] = total if at == 0 else outs[1][...] + total


def token_products(pairs, plan, first=0, width=None):
    width = width or pairs[0][0].shape[1]

    def kernel(*refs):
        at = 0
        while at < len(plan):
            parts, end = plan[at], at + 1
            while end < len(plan) and plan[end] == parts:
                end += 1

            def run(parts=parts):
                value = None
                for k in parts:
                    term = dot_t(refs[2 * k][...], refs[2 * k + 1][...], 0, 0)
                    value = term if value is None else value + term
                refs[-1][...] = value.astype(BF16)

            if end - at == len(plan):
                run()
            else:
                tile = pl.program_id(0)
                pl.when((tile >= at) & (tile < end))(run)
            at = end

    specs, arrays = [], []
    for left, right, tile, start, tiles in pairs:
        specs.append(pl.BlockSpec((left.shape[0], width), lambda t: (0, first)))
        specs.append(
            pl.BlockSpec(
                (right.shape[0], TILE),
                lambda t, tile=tile, start=start, tiles=tiles: (
                    0,
                    tile + jnp.clip(t - start, 0, tiles - 1),
                ),
            )
        )
        arrays += [left, right]
    return pl.pallas_call(
        kernel,
        grid=(len(plan),),
        in_specs=specs,
        out_specs=pl.BlockSpec((width, TILE), lambda t: (0, t)),
        out_shape=jax.ShapeDtypeStruct((width, len(plan) * TILE), BF16),
        cost_estimate=QUICK,
    )(*arrays)


def norm_back_parts(parts, unit, factor, gain, straight):
    rows, width = unit.shape
    step = 128

    def kernel(*refs):
        grad = sum(ref[...].astype(F32) for ref in refs[: len(parts)])
        unit, factor, gain, straight, total, rounded = refs[len(parts) :]
        value = straight[...] + norm_back(grad, unit[...], factor[...], gain[...])
        total[...] = value
        rounded[...] = value.astype(BF16)

    block = lambda w: pl.BlockSpec((step, w), lambda i: (i, 0))
    return pl.pallas_call(
        kernel,
        grid=(rows // step,),
        in_specs=[block(width)] * (len(parts) + 1)
        + [block(1), pl.BlockSpec((1, width), lambda i: (0, 0)), block(width)],
        out_specs=[block(width)] * 2,
        out_shape=[jax.ShapeDtypeStruct((rows, width), kind) for kind in (F32, BF16)],
        cost_estimate=QUICK,
    )(*parts, unit, factor, gain[None], straight)


def norm_parts(parts, gain, shift):
    rows, width = parts[0].shape
    step = 128

    def kernel(*refs):
        for i in range(len(parts)):
            unit, _ = norm_stats(refs[i][...].astype(F32))
            refs[-1][i] = (unit * refs[-3][...] + refs[-2][...]).astype(BF16)

    vector = pl.BlockSpec((1, width), lambda i: (0, 0))
    return pl.pallas_call(
        kernel,
        grid=(rows // step,),
        in_specs=[pl.BlockSpec((step, width), lambda i: (i, 0))] * len(parts) + [vector] * 2,
        out_specs=pl.BlockSpec((len(parts), step, width), lambda i: (0, i, 0)),
        out_shape=jax.ShapeDtypeStruct((len(parts), rows, width), BF16),
        cost_estimate=QUICK,
    )(*parts, gain[None], shift[None]).reshape(len(parts) * rows, width)


def swap(value, axis, bit):
    return lax.ppermute(value, axis, [(i, i ^ bit) for i in range(lax.axis_size(axis))])


def bits_of(count):
    return [1 << k for k in range(count.bit_length() - 1)]


def doubled(parts, axis):
    for bit in bits_of(lax.axis_size(axis)):
        parts = jnp.concatenate([parts, swap(parts, axis, bit)], axis=0)
    return parts


def in_slot_order(parts):
    count, groups = lax.axis_size("seq"), lax.axis_size("batch")
    own_s, own_b = lax.axis_index("seq"), lax.axis_index("batch")
    order = (slot_owners() ^ own_s)[:, None] + count * (
        jnp.arange(groups, dtype=jnp.int32) ^ own_b
    )
    parts = jnp.take(parts, order.reshape(-1), axis=0)
    return jnp.moveaxis(parts, 0, -2).reshape(*parts.shape[1:-1], -1)


def small_totals(value, flat, after, beside):
    count, groups = lax.axis_size("seq"), lax.axis_size("batch")
    own_s, own_b = lax.axis_index("seq"), lax.axis_index("batch")
    parts = jnp.moveaxis(value.reshape(*value.shape[:-1], count * groups, -1), -2, 0)
    order = owner_slots()[jnp.arange(count, dtype=jnp.int32) ^ own_s] * groups + (
        jnp.arange(groups, dtype=jnp.int32) ^ own_b
    )[:, None]
    parts = jnp.take(parts, order.reshape(-1), axis=0)
    for bit in reversed(bits_of(groups)):
        half = parts.shape[0] // 2
        parts = parts[:half] + swap(parts[half:], "batch", bit)
    piece = parts.shape[1:]
    parts = tie(parts.reshape(count, -1), *after)
    for bit in reversed(bits_of(count)):
        half = parts.shape[0] // 2
        sent = jnp.concatenate([parts[half:].reshape(-1), flat])
        if bit == 1:
            sent = tie(sent, *beside)
        got = swap(sent, "seq", bit)
        at = half * parts.shape[1]
        parts = parts[:half] + got[:at].reshape(half, -1)
        flat = flat + got[at:]
    return parts.reshape(piece), flat


def batch_gather(value, later=None):
    parts = {0: value}
    for bit in reversed(bits_of(lax.axis_size("batch"))):
        passed = {r: later(v) if later and r else v for r, v in parts.items()}
        parts.update({r | bit: swap(v, "batch", bit) for r, v in passed.items()})
    return [parts[r] for r in range(len(parts))]


def batch_scatter(parts, seen=None, apart=False):
    parts = {r: [v] for r, v in enumerate(parts)}
    added = lambda values: sum(v.astype(F32) for v in values)
    bits = bits_of(len(parts))
    for bit in bits:
        for r in sorted((r for r in parts if r & bit), reverse=True):
            values = parts.pop(r)
            sent = values[0] if len(values) == 1 else total_of(values)
            if seen and bit == bits[-1]:
                seen(sent)
            parts[r ^ bit].append(swap(sent, "batch", bit))
    return parts[0] if apart else added(parts[0])


def total_of(values):
    rows, width = values[0].shape

    def kernel(*refs):
        total = refs[0][...].astype(F32)
        for ref in refs[1:-1]:
            total = total + ref[...].astype(F32)
        refs[-1][...] = total.astype(BF16)

    block = pl.BlockSpec((rows // 2, width), lambda i: (i, 0))
    return pl.pallas_call(
        kernel,
        grid=(2,),
        in_specs=[block] * len(values),
        out_specs=block,
        out_shape=jax.ShapeDtypeStruct((rows, width), BF16),
        cost_estimate=QUICK,
    )(*values)


def move_kernel(order, *refs):
    *values, moved = refs
    width = moved.shape[1] // order.shape[0]
    for i in range(order.shape[0]):
        source = pl.ds(pl.multiple_of(order[i] * width, width), width)
        block = values[0][:, source]
        if len(values) > 1:
            block = sum(v[:, source].astype(F32) for v in values).astype(moved.dtype)
        moved[:, i * width : (i + 1) * width] = block


def reorder(value, order):
    values = value if isinstance(value, (list, tuple)) else [value]
    value = values[0]
    rows, columns = value.shape
    width = columns // order.shape[0]
    if width % 128:
        value = value if len(values) == 1 else total_of(values)
        return jnp.take(value.reshape(rows, -1, width), order, axis=1).reshape(value.shape)
    block = pl.BlockSpec((rows // 2, columns), lambda i, *_: (i, 0))
    return pl.pallas_call(
        move_kernel,
        grid_spec=pltpu.PrefetchScalarGridSpec(
            num_scalar_prefetch=1, grid=(2,), in_specs=[block] * len(values), out_specs=block
        ),
        out_shape=jax.ShapeDtypeStruct(value.shape, value.dtype),
        cost_estimate=QUICK,
    )(order, *values)


def norm_stats(values):
    mean = jnp.mean(values, axis=-1, keepdims=True)
    centered = values - mean
    factor = lax.rsqrt(jnp.mean(centered * centered, axis=-1, keepdims=True) + 1e-05)
    return centered * factor, factor


def norm_back(grad, unit, factor, gain):
    scaled = grad * gain
    inner = jnp.mean(scaled * unit, axis=-1, keepdims=True)
    return factor * (scaled - jnp.mean(scaled, axis=-1, keepdims=True) - unit * inner)


def gelu_and_slope(values):
    root, cubic = (2 / jnp.pi) ** 0.5, 0.044715
    square = values * values
    bend = jnp.tanh(values * (root + root * cubic * square))
    half = 0.5 + 0.5 * bend
    slope = half + values * (0.5 - 0.5 * bend * bend) * (root + 3 * root * cubic * square)
    return values * half, slope


def dot_t(left, right, left_dim, right_dim):
    return lax.dot_general(
        left, right, (((left_dim,), (right_dim,)), ((), ())), preferred_element_type=F32
    )


def masks(start, limit):
    row = lax.broadcasted_iota(jnp.int32, (WINDOW, WINDOW), 0)
    col = lax.broadcasted_iota(jnp.int32, (WINDOW, WINDOW), 1)
    own = col <= row
    spot = jnp.where(own, start + col, start - WINDOW + col)
    return own, (spot >= 0) & ((spot < limit) | (row == col))


def weights_of(query, key, early_key, own, live):
    scores = jnp.where(own, dot_t(query, key, 1, 1), dot_t(query, early_key, 1, 1))
    scores = jnp.where(live, scores * (HEAD_DIM**-0.5), -1e30)
    expo = jnp.exp(scores - jnp.max(scores, axis=-1, keepdims=True))
    return expo / jnp.sum(expo, axis=-1, keepdims=True)


def attend_kernel(limits, start, packed, early, mix, mixed, weights, *branch):
    width = mixed.shape[1]
    own, live = masks(start[0], limits[pl.program_id(0)])
    for head, at in enumerate(range(0, width, HEAD_DIM)):
        cols = lambda k: slice(k * width + at, k * width + at + HEAD_DIM)
        probs = weights_of(packed[:, cols(0)], packed[:, cols(1)], early[:, cols(0)], own, live)
        weights[:, head * WINDOW : (head + 1) * WINDOW] = probs.astype(BF16)
        near = jnp.where(own, probs, 0.0).astype(BF16)
        far = jnp.where(own, 0.0, probs).astype(BF16)
        mixed[:, cols(0)] = (
            dot_t(near, packed[:, cols(2)], 1, 0) + dot_t(far, early[:, cols(1)], 1, 0)
        ).astype(BF16)
    out = dot_t(mixed[...], mix[...], 1, 1).astype(BF16)
    for i, part in enumerate(branch):
        @pl.when(pl.program_id(0) == i)
        def _(part=part):
            part[...] = out


def attend_back_kernel(limits, start, packed, early, weights, grad, g_packed, g_early):
    width = grad.shape[1]
    scale = HEAD_DIM**-0.5
    row = lax.broadcasted_iota(jnp.int32, (WINDOW, WINDOW), 0)
    own = lax.broadcasted_iota(jnp.int32, (WINDOW, WINDOW), 1) <= row
    for head, at in enumerate(range(0, width, HEAD_DIM)):
        cols = lambda k: slice(k * width + at, k * width + at + HEAD_DIM)
        query, key, value = (packed[:, cols(k)] for k in range(3))
        early_key, early_value = (early[:, cols(k)] for k in range(2))
        out = grad[:, cols(0)]
        probs = weights[:, head * WINDOW : (head + 1) * WINDOW].astype(F32)
        g_probs = jnp.where(own, dot_t(out, value, 1, 1), dot_t(out, early_value, 1, 1))
        delta = jnp.sum(probs * g_probs, axis=-1, keepdims=True)
        g_scores = probs * (g_probs - delta)
        near = jnp.where(own, probs, 0.0).astype(BF16)
        far = jnp.where(own, 0.0, probs).astype(BF16)
        g_near = jnp.where(own, g_scores, 0.0).astype(BF16)
        g_far = jnp.where(own, 0.0, g_scores).astype(BF16)
        g_packed[:, cols(0)] = (
            (dot_t(g_near, key, 1, 0) + dot_t(g_far, early_key, 1, 0)) * scale
        ).astype(BF16)
        g_packed[:, cols(1)] = (dot_t(g_near, query, 0, 0) * scale).astype(BF16)
        g_packed[:, cols(2)] = dot_t(near, out, 0, 0).astype(BF16)
        g_early[:, cols(0)] = (dot_t(g_far, query, 0, 0) * scale).astype(BF16)
        g_early[:, cols(1)] = dot_t(far, out, 0, 0).astype(BF16)


def per_chain(kernel, limits, start, arrays, widths, shared=(), parts=0):
    rows = arrays[0].shape[0]
    whole = lambda shape: pl.BlockSpec(shape, lambda i, *_: (0, 0))
    block = lambda w: pl.BlockSpec((WINDOW, w), lambda i, *_: (i, 0))
    part = (WINDOW, shared[0].shape[0] if shared else 0)
    return pl.pallas_call(
        kernel,
        grid_spec=pltpu.PrefetchScalarGridSpec(
            num_scalar_prefetch=2,
            grid=(rows // WINDOW,),
            in_specs=[block(a.shape[1]) for a in arrays]
            + [pl.BlockSpec((v.shape[0], TILE), lambda i, *_: (0, 3)) for v in shared],
            out_specs=[block(w) for w in widths] + [whole(part)] * parts,
        ),
        out_shape=[jax.ShapeDtypeStruct((rows, w), BF16) for w in widths]
        + [jax.ShapeDtypeStruct(part, BF16)] * parts,
        cost_estimate=QUICK,
    )(limits, start, *arrays, *shared)


def shards(
    tokens,
    lengths,
    cotangent,
    ln1_gain,
    ln1_bias,
    w_qkv,
    qv_bias,
    w_out,
    out_bias,
    ln2_gain,
    ln2_bias,
    w_fc,
    fc_bias,
    w_proj,
    proj_bias,
):
    groups = lax.axis_size("batch")
    chain = lax.axis_index("batch")
    place = lax.axis_index("seq")
    rows, width = tokens.shape[1:]
    count = lax.axis_size("seq")
    slice_width = width // count
    heads_width = w_out.shape[0]
    assert rows == WINDOW and lengths.shape[1] == 1 and tokens.shape[0] == 1
    start = (place * rows).astype(jnp.int32)
    limits = lengths[:, 0][chain ^ jnp.arange(groups, dtype=jnp.int32)]
    valid = (start + jnp.arange(rows, dtype=jnp.int32) < limits[0]).astype(F32)
    to_slots, from_slots = slot_owners(), owner_slots()
    back_order = from_slots[slot_owners(-1)]

    tokens, cotangent = tokens[0], cotangent[0]
    vectors = jnp.stack([ln1_gain, ln1_bias, out_bias, ln2_gain, ln2_bias, proj_bias])
    vectors = doubled(vectors[None], "seq")
    ring = Ring(vectors)
    vectors = in_slot_order(doubled(vectors, "batch"))
    gain_one, shift_one, mix_shift, gain_two, shift_two, down_shift = (
        vectors[i].astype(F32) for i in range(6)
    )

    qkv_width = 3 * heads_width
    assert heads_width == TILE
    mix_in = jnp.concatenate([w_qkv.reshape(slice_width, qkv_width), w_out.T], axis=1)
    mix_in, up_in, down_in = Gather(mix_in, 0), Gather(w_fc, 0), Gather(w_proj, 1)
    late = {}
    g_down, g_up = (Scatter(lambda j, n=n: (late[n], j, slice_width)) for n in ("down", "up"))

    def find_mix(j):
        for value, lo, wide in late["mix"]:
            if lo <= j * slice_width < lo + wide:
                return value, j - lo // slice_width, slice_width

    g_mix = Scatter(find_mix)
    for moved, more_ahead in (
        (mix_in, True), (up_in, False), (down_in, True), (g_down, False), (g_up, True), (g_mix, False)
    ):
        ring.add(moved, more_ahead)
    more = max(0, count // 2 - 4)

    ring.advance()
    own_tokens = reorder(ring.now(tokens), to_slots)
    next_tokens = reorder(ring.now(tokens), slot_owners(1))
    early_tokens = lax.ppermute(next_tokens, "seq", [(i, i + 1) for i in range(count - 1)])
    parts = batch_gather(tie(own_tokens, vectors))
    ring.advance()
    early_parts = batch_gather(early_tokens)
    grad_out = reorder(ring.now(cotangent), to_slots).astype(F32) * valid[:, None]
    grad_y_own = grad_out.astype(BF16)
    ring.due(grad_y_own)
    ring.advance(1 + more)
    normed = norm_parts(ring.now(*parts), gain_one, shift_one)
    ring.due(normed)
    grad_y = batch_gather(tie(grad_y_own, early_parts[0]))
    ring.advance()
    normed_early = norm_parts(ring.now(*early_parts), gain_one, shift_one)
    ring.due(normed_early)
    mix_in.early(ring)
    ring.advance()
    ring.due(*grad_y)

    mix_in = mix_in.all()
    zeros = jnp.zeros((heads_width,), F32)
    shift = jnp.concatenate([qv_bias[0].astype(F32), zeros, qv_bias[1].astype(F32)])[None]
    (packed,) = matmul(
        [ring.now(normed)], mix_in, finish_bias, ["rows"], tiles=3, extra=[shift]
    )
    (early,) = matmul(
        [ring.now(normed_early)],
        mix_in,
        finish_bias,
        ["rows"],
        first=1,
        tiles=2,
        extra=[shift[:, heads_width:]],
    )
    starts = start.reshape(1)
    ring.due(packed, early)
    ring.advance()
    mixed, weights, *branch = per_chain(
        attend_kernel,
        limits,
        starts,
        (ring.now(packed), early),
        (heads_width, heads_width // HEAD_DIM * WINDOW),
        (mix_in,),
        groups,
    )
    ring.due(*branch)
    ring.advance()
    branch = batch_scatter(ring.now(*branch), ring.due)
    grad_y = jnp.concatenate(grad_y, axis=0)
    ring.due(grad_y)
    ring.advance(1 + more)
    inputs = own_tokens.astype(F32)
    resid = inputs + branch + mix_shift
    unit_two, factor_two = norm_stats(resid)
    second_own = (unit_two * gain_two + shift_two).astype(BF16)
    up_in = up_in.all()
    ring.due(second_own, up_in)
    ring.advance()
    second = batch_gather(second_own, ring.now)

    active, slope, second = matmul(
        ring.now(*second),
        up_in,
        finish_gelu,
        ["rows", "rows"],
        extra=[fc_bias.astype(F32)[None]],
        keep=True,
    )
    ring.due(active)
    ring.advance(1 + more)
    straight = lambda left, right: token_products(
        [(left, right, 0, 0, right.shape[1] // TILE)], [[0]] * (right.shape[1] // TILE)
    )
    late["down"] = straight(grad_y, ring.now(active))
    ring.due(late["down"])
    ring.advance()
    down_in.early(ring)
    ring.advance()
    down_in = down_in.all()
    grad_pre, grad_fc_bias = matmul(
        [ring.now(grad_y)], down_in, finish_slope, ["rows", "sums"], nt=True, extra=[slope]
    )
    ring.due(grad_pre)
    ring.advance()
    parts = matmul([ring.now(grad_pre)], up_in, finish_parts, ["parts"], nt=True)
    ring.due(*parts)
    ring.advance()
    sent = []
    grad_second = batch_scatter(ring.now(*parts), sent.append, True)
    late["up"] = straight(tie(second, *sent), grad_pre)
    ring.due(late["up"])
    ring.advance()
    grad_resid, grad_branch_own = norm_back_parts(
        ring.now(*grad_second), unit_two, factor_two, gain_two, grad_out
    )
    grad_second = sum(v.astype(F32) for v in grad_second)
    result = matmul([tie(active, grad_branch_own)], down_in, finish_parts, ["parts"])
    ring.due(*result)
    ring.advance(1 + more)
    grad_branch = batch_gather(grad_branch_own, ring.now)
    grad_w_proj = flipped_total(*g_down.ends(ring))
    ring.due(grad_w_proj)

    grad_mixed, grad_branch = matmul(
        tie(grad_branch, grad_w_proj), mix_in, finish_rows, ["rows"], first=3, tiles=1, keep=True
    )
    ring.due(grad_mixed)
    ring.advance()
    g_packed, g_early = per_chain(
        attend_back_kernel,
        limits,
        starts,
        (packed, early, weights, ring.now(grad_mixed)),
        (qkv_width, 2 * heads_width),
    )
    pairs = [
        (normed, g_packed, 0, 0, 3), (normed_early, g_early, 0, 1, 2), (grad_branch, mixed, 0, 3, 1)
    ]

    def mix_piece(first, wide):
        return token_products(pairs, [[0], [0, 1], [0, 1], [2]], first, wide), first * wide, wide

    late["mix"] = [mix_piece(2, TILE)]
    ring.due(late["mix"][0][0])
    result = batch_scatter(ring.now(*result), ring.due)
    ring.advance()
    back = matmul(
        [ring.now(g_early)], mix_in, finish_parts, ["parts"], nt=True, first=heads_width
    )
    pairs[0] = (tie(normed, back[0]), *pairs[0][1:])
    late["mix"].append(mix_piece(1, TILE))
    result = resid + result + down_shift
    ring.due(late["mix"][1][0], result)
    ring.advance()
    sent = []
    back = batch_scatter(ring.now(*back), sent.append, True)
    grad_own = matmul([tie(g_packed, *sent)], mix_in, finish_parts, ["parts"], nt=True)
    pairs[0] = (tie(normed, grad_own[0]), *pairs[0][1:])
    late["mix"].append(mix_piece(3, TILE))
    ring.due(late["mix"][2][0])
    ring.advance()
    moved = reorder(ring.now(*back), back_order)
    grad_own = batch_scatter(ring.now(*grad_own), ring.due)
    moved = lax.ppermute(moved, "seq", [(i + 1, i) for i in range(count - 1)])
    back = sum(v.astype(F32) for v in back)
    pairs[0] = (ring.now(normed), *pairs[0][1:])
    late["mix"].append(mix_piece(0, TILE))
    ring.due(late["mix"][3][0])
    ring.advance()
    block_out = reorder(ring.now(result).astype(BF16), from_slots)
    while any(ring.queue.values()):
        ring.advance()
    unit_one, factor_one = norm_stats(inputs)
    unit_early, _ = norm_stats(early_tokens.astype(F32))
    grad_normed = grad_own + moved.astype(F32)
    grad_tokens = grad_resid + norm_back(grad_normed, unit_one, factor_one, gain_one)

    column = lambda value: jnp.sum(value.astype(F32), axis=0)
    flat = jnp.concatenate(
        [
            grad_fc_bias[0],
            column(g_packed[:, :heads_width]),
            column(g_packed[:, 2 * heads_width :]) + column(g_early[:, heads_width:]),
        ]
    )
    ff = grad_fc_bias.shape[1]
    sums = jnp.stack(
        [
            jnp.sum(grad_own * unit_one + back * unit_early, axis=0),
            jnp.sum(grad_own + back, axis=0),
            column(grad_branch_own),
            jnp.sum(grad_second * unit_two, axis=0),
            jnp.sum(grad_second, axis=0),
            column(grad_y_own),
        ]
    )
    grad_tokens = reorder(grad_tokens.astype(BF16), from_slots)
    grad_w_fc = g_up.total(ring)
    after = [*ring.last.values(), grad_tokens, block_out, grad_w_fc]
    grad_w_qkv, grad_w_out = mixed_total(*g_mix.ends(ring))
    sums, flat = small_totals(sums, flat, after, [grad_w_qkv, grad_w_out])
    return (
        block_out[None],
        grad_tokens[None],
        sums[0],
        sums[1],
        grad_w_qkv.transpose(1, 0, 2),
        flat[ff:].reshape(2, heads_width),
        grad_w_out,
        sums[2],
        sums[3],
        sums[4],
        grad_w_fc,
        flat[:ff],
        grad_w_proj,
        sums[5],
    )


def solution(mesh):
    everywhere = P(("seq", "batch"))
    rows = P("batch", "seq", None)
    return jax.shard_map(
        shards,
        mesh=mesh,
        in_specs=(
            rows,
            P(),
            rows,
            everywhere,
            everywhere,
            P("seq", None, "batch"),
            P(None, "batch"),
            P("batch", "seq"),
            everywhere,
            everywhere,
            everywhere,
            P("seq", "batch"),
            P("batch"),
            P("batch", "seq"),
            everywhere,
        ),
        out_specs=(
            rows,
            rows,
            everywhere,
            everywhere,
            P("seq", None, "batch"),
            P(None, "batch"),
            P("batch", "seq"),
            everywhere,
            everywhere,
            everywhere,
            P("seq", "batch"),
            P("batch"),
            P("batch", "seq"),
            everywhere,
        ),
        check_vma=False,
    )
```
